128 devices in a mesh: pipe: 2 (over x_hi), seq: 16 (over x_lo, y, core), chan: 4 (over z).
Axes of the slice: x: 4 (x_hi: 2, x_lo: 2; x = x_hi * 2 + x_lo), y: 4, z: 4, core: 2. Of those that a mesh axis runs over, the one named last changes fastest.
Arguments:
- fwd_in: bfloat16 [2, 2048, 8192], P('pipe', 'seq', 'chan'), may hold values from -14 to 14
- saved_in: bfloat16 [2, 2048, 8192], P('pipe', 'seq', 'chan'), may hold values from -14 to 14
- saved_conv: bfloat16 [2, 2048, 8192], P('pipe', 'seq', 'chan'), may hold values from -5 to 5
- grad_out: bfloat16 [2, 2048, 8192], P('pipe', 'seq', 'chan'), may hold values from -14 to 14
- filters: bfloat16 [2, 2048, 8192], P('pipe', None, 'chan'), may hold values from -1.2 to 1.2
- mix_params: float32 [2, 7, 8192], P('pipe', None, 'chan'), may hold values from -1.5 to 1.5
- span_order: int32 [16], replicated, may hold values from 0 to 15, each once
Outputs:
- layer_out: bfloat16 [2, 2048, 8192], P('pipe', 'seq', 'chan')
- input_grad: bfloat16 [2, 2048, 8192], P('pipe', 'seq', 'chan')
- param_grad: float32 [2, 7, 8192], P('pipe', None, 'chan')
- received: bfloat16 [2, 2048, 8192], P('pipe', 'seq', 'chan')
The draws below stay inside these ranges and needn't reach their ends.
Inputs may be any that keep to these rules, and one draw needn't show every extreme that they name: span_order holds each block position once.
All inputs are finite; a program needn't handle non-finite values.
Results may differ from the reference program's by a relative error of at most 0.015.
Values may be sent and summed in bfloat16 or wider, within the bound.
No kernel may reach another device: no remote copies, remote signals or barrier semaphores. Data moves between devices by JAX's collectives and lax.ppermute only.
A program may use at most 192 MiB of HBM per device.

```python
import math
import jax
import jax.numpy as jnp
from jax import lax

D = 8192
TOK_DEV = 128
SEQ_LEN = 2048
SPANS = 16
SEGMENTS = 2
N_SEQ = 16


def activation_law(key, rows_rise):
    key_base, key_cols = jax.random.split(key, 2)
    shape = (SEGMENTS, SEQ_LEN, D)
    base = jnp.clip(jax.random.normal(key_base, shape, jnp.float32), -4.0, 4.0)
    spread = jax.random.uniform(key_cols, (SEGMENTS, 1, D), jnp.float32, math.log(0.5), math.log(1.5))
    column_pos = jnp.arange(D, dtype=jnp.float32) / max(D - 1, 1)
    column_scale = jnp.exp(spread) * jnp.power(3.0, column_pos)[None, None, :] / 2.0
    row_pos = jnp.arange(SEQ_LEN, dtype=jnp.float32) / max(SEQ_LEN - 1, 1)
    row_scale = jnp.power(3.0, rows_rise * row_pos)[None, :, None] / (1.0 + rows_rise)
    return base * column_scale * row_scale


def draw_fwd_in(key, part):
    return activation_law(jax.random.fold_in(key, 11), 0.0).astype(jnp.bfloat16)


def draw_saved_in(key, part):
    return activation_law(jax.random.fold_in(key, 12), 0.0).astype(jnp.bfloat16)


def draw_grad_out(key, part):
    return activation_law(jax.random.fold_in(key, 13), 1.0).astype(jnp.bfloat16)


def draw_filters(key, part):
    key_rate, key_noise = jax.random.split(jax.random.fold_in(key, 21), 2)
    decay_rate = jnp.exp(jax.random.uniform(key_rate, (SEGMENTS, 1, D), jnp.float32, math.log(0.05 / SEQ_LEN), math.log(1.0 / 30.0)))
    lag_pos = jnp.arange(SEQ_LEN, dtype=jnp.float32)[None, :, None]
    amplitude = jnp.sqrt(2.0 * jnp.maximum(decay_rate, 1.0 / SEQ_LEN))
    noise = jnp.clip(jax.random.normal(key_noise, (SEGMENTS, SEQ_LEN, D), jnp.float32), -4.0, 4.0)
    taps = noise * jnp.exp(-decay_rate * lag_pos) * amplitude
    return jnp.clip(taps, -1.2, 1.2).astype(jnp.bfloat16)


def draw_mix_params(key, part):
    key_gain, key_mag, key_sign, key_bias = jax.random.split(jax.random.fold_in(key, 31), 4)
    gains = jax.random.uniform(key_gain, (SEGMENTS, 1, D), jnp.float32, 0.5, 1.5)
    magnitude = jax.random.uniform(key_mag, (SEGMENTS, 3, D), jnp.float32, 0.5, 1.5)
    biases = jnp.clip(0.5 * jax.random.normal(key_bias, (SEGMENTS, 3, D), jnp.float32), -1.5, 1.5)
    scales = magnitude * jnp.sign(jax.random.normal(key_sign, (SEGMENTS, 3, D), jnp.float32))
    rows = [gains[:, 0], scales[:, 0], biases[:, 0], scales[:, 1], biases[:, 1], scales[:, 2], biases[:, 2]]
    return jnp.stack(rows, axis=1)


def levels(stream_key, shape, cuts, smallest, largest):
    loudness, own = 1.0, jax.random.fold_in(stream_key, 6)
    for axis_at, blocks in cuts:
        steps = jnp.exp(jax.random.uniform(jax.random.fold_in(own, axis_at), (blocks,), jnp.float32, smallest / len(cuts), largest / len(cuts)))
        loudness = loudness * jnp.repeat(steps, shape[axis_at] // blocks).reshape([-1 if axis == axis_at else 1 for axis in range(len(shape))])
    return loudness


def bell_draw(stream_key, shape, deviation, most, cuts=(), kind=jnp.bfloat16):
    gain = levels(stream_key, shape, cuts, -0.22, 0.18) if cuts else 1.0
    drawn = jax.random.normal(stream_key, shape, jnp.float32) * deviation * gain
    return jnp.minimum(jnp.maximum(drawn, -most), most).astype(kind)


def setup_inputs(seed: int = 0) -> dict:
    key_of = jax.random.split(jax.random.key(seed), 8)
    fwd_in = draw_fwd_in(jax.random.fold_in(key_of[7], 71), 0)
    saved_in = draw_saved_in(jax.random.fold_in(key_of[7], 71), 0)
    saved_conv = bell_draw(key_of[2], (SEGMENTS, SEQ_LEN, D), 1.0, 5.0, ((0, 2), (1, 16), (2, 4)))
    grad_out = draw_grad_out(jax.random.fold_in(key_of[7], 71), 0)
    filters = draw_filters(jax.random.fold_in(key_of[7], 71), 0)
    mix_params = draw_mix_params(jax.random.fold_in(key_of[7], 71), 0)
    span_order = jax.random.permutation(key_of[6], N_SEQ).astype(jnp.int32)
    return {"fwd_in": fwd_in, "saved_in": saved_in, "saved_conv": saved_conv, "grad_out": grad_out, "filters": filters, "mix_params": mix_params, "span_order": span_order}


EPSILON = 1e-05

def mixer_fields(inputs, params):
    squares = lax.optimization_barrier(jnp.mean(inputs * inputs, axis=1, keepdims=True))
    inv_rms = lax.rsqrt(squares + EPSILON)
    normed = inputs * inv_rms
    scaled = normed * params[0]
    query_feat = scaled * params[1] + params[2]
    key_feat = scaled * params[3] + params[4]
    value_feat = scaled * params[5] + params[6]
    return (inv_rms, normed, scaled, query_feat, key_feat, value_feat)

def causal_filter(signal, taps):
    length, channels = signal.shape
    group_width = math.gcd(channels, 512)

    def per_group(both_parts):
        signal_part, taps_part = both_parts
        spectrum = jnp.fft.rfft(signal_part, 2 * length, axis=0) * jnp.fft.rfft(taps_part, 2 * length, axis=0)
        return jnp.fft.irfft(spectrum, 2 * length, axis=0)[:length]
    grouped_signal = signal.reshape(length, channels // group_width, group_width).transpose(1, 0, 2)
    grouped_taps = taps.reshape(length, channels // group_width, group_width).transpose(1, 0, 2)
    blocked = lax.map(per_group, (grouped_signal, grouped_taps))
    return blocked.transpose(1, 0, 2).reshape(length, channels).astype(jnp.float32)

def to_sequence(stored, span_order):
    blocks = stored.reshape(SPANS, TOK_DEV, stored.shape[-1])
    return jnp.zeros_like(blocks).at[span_order].set(blocks).reshape(SEQ_LEN, stored.shape[-1])

def to_storage(ordered, span_order):
    blocks = ordered.reshape(SPANS, TOK_DEV, ordered.shape[-1])
    return blocks[span_order].reshape(SEQ_LEN, ordered.shape[-1])

def reference(fwd_in, saved_in, saved_conv, grad_out, filters, mix_params, span_order):
    layer_outs = []
    input_grads = []
    param_grads = []
    for segment_index in range(SEGMENTS):
        params = mix_params[segment_index].astype(jnp.float32)
        taps = filters[segment_index].astype(jnp.float32)
        inputs = fwd_in[segment_index].astype(jnp.float32)
        inv_rms, normed, scaled, query_feat, key_feat, value_feat = mixer_fields(inputs, params)
        mixed = (key_feat * value_feat).astype(jnp.bfloat16)
        conv_seq = causal_filter(to_sequence(mixed, span_order).astype(jnp.float32), taps)
        conv = lax.optimization_barrier(to_storage(conv_seq, span_order).astype(jnp.bfloat16))
        layer_outs.append((inputs + query_feat * conv.astype(jnp.float32)).astype(jnp.bfloat16))
        saved = saved_in[segment_index].astype(jnp.float32)
        cotangent = grad_out[segment_index].astype(jnp.float32)
        inv_rms, normed, scaled, query_feat, key_feat, value_feat = mixer_fields(saved, params)
        grad_conv = (cotangent * query_feat).astype(jnp.bfloat16)
        grad_seq = to_sequence(grad_conv, span_order).astype(jnp.float32)
        grad_mixed_seq = causal_filter(grad_seq[::-1], taps)[::-1]
        grad_mixed = lax.optimization_barrier(to_storage(grad_mixed_seq, span_order).astype(jnp.bfloat16))
        grad_mixed = grad_mixed.astype(jnp.float32)
        grad_query = cotangent * saved_conv[segment_index].astype(jnp.float32)
        grad_key = grad_mixed * value_feat
        grad_value = grad_mixed * key_feat
        grad_scaled = grad_query * params[1] + grad_key * params[3] + grad_value * params[5]
        rows = jnp.stack([lax.optimization_barrier(jnp.sum(grad_scaled * normed, axis=0)), lax.optimization_barrier(jnp.sum(grad_query * scaled, axis=0)), lax.optimization_barrier(jnp.sum(grad_query, axis=0)), lax.optimization_barrier(jnp.sum(grad_key * scaled, axis=0)), lax.optimization_barrier(jnp.sum(grad_key, axis=0)), lax.optimization_barrier(jnp.sum(grad_value * scaled, axis=0)), lax.optimization_barrier(jnp.sum(grad_value, axis=0))])
        param_grads.append(rows)
        grad_normed = grad_scaled * params[0]
        cross = lax.optimization_barrier(jnp.mean(grad_normed * normed, axis=1, keepdims=True))
        input_grads.append((cotangent + inv_rms * (grad_normed - normed * cross)).astype(jnp.bfloat16))
    layer_out = jnp.stack(layer_outs)
    input_grad = jnp.stack(input_grads)
    param_grad = jnp.stack(param_grads)
    received = jnp.stack([input_grad[1], layer_out[0]])
    return (layer_out, input_grad, param_grad, received)
```

```python
import functools

import jax
import jax.numpy as jnp
import ml_dtypes
import numpy as np
from jax import lax
from jax.experimental import pallas as pl
from jax.experimental.pallas import tpu as pltpu
from jax.sharding import PartitionSpec as P

D = 8192
EPSILON = 1e-05
BLOCK = 256
LANES = 128


def split_bf16(table):
    high = table.astype(np.float32).astype(ml_dtypes.bfloat16)
    low = (table - high.astype(np.float64)).astype(np.float32).astype(ml_dtypes.bfloat16)
    return high, low


def transform_tables():
    period = 2 * BLOCK
    freq = np.arange(BLOCK)[:, None]
    time = np.arange(BLOCK)[None, :]
    angle = 2.0 * np.pi / period * (freq * time % period)
    real, imag = np.cos(angle), -np.sin(angle)
    imag[0] = np.where(np.arange(BLOCK) % 2 == 0, 1.0, -1.0)
    enter = np.concatenate([real, imag], axis=0)
    angle = 2.0 * np.pi / period * (freq * (time + BLOCK) % period)
    real, imag = 2.0 * np.cos(angle), -2.0 * np.sin(angle)
    real[0] = 1.0
    imag[0] = np.where(np.arange(BLOCK) % 2 == 0, 1.0, -1.0)
    leave = np.concatenate([real, imag], axis=0).T / period
    return split_bf16(enter) + split_bf16(leave)


def rows_to_columns(rows):
    return jnp.concatenate([rows] * 16, axis=0).T


def columns_to_rows(columns):
    lane = lax.broadcasted_iota(jnp.int32, (128, 128), 1)
    square = jnp.zeros((128, 128), jnp.float32)
    for index, column in enumerate(columns):
        square = jnp.where(lane == index, column, square)
    return square.T[:8]


def lane_groups_sum(block):
    total = block[:, :128]
    for at in range(128, block.shape[1], 128):
        total = total + block[:, at : at + 128]
    return total


def squares_kernel(fwd_ref, saved_ref, out_ref, acc):
    step = pl.program_id(0)

    @pl.when(step == 0)
    def _():
        acc[...] = jnp.zeros_like(acc)

    fwd = fwd_ref[0].astype(jnp.float32)
    saved = saved_ref[0].astype(jnp.float32)
    acc[0] += lane_groups_sum(fwd * fwd)
    acc[1] += lane_groups_sum(saved * saved)

    @pl.when(step == pl.num_programs(0) - 1)
    def _():
        out_ref[...] = columns_to_rows(
            [jnp.sum(acc[index], axis=1, keepdims=True) for index in range(2)]
        )


def squares(fwd_in, saved_in):
    rows, width = fwd_in.shape[1:]
    wide = 512
    spec = pl.BlockSpec((1, rows, wide), lambda step: (0, 0, step))
    return pl.pallas_call(
        squares_kernel,
        out_shape=jax.ShapeDtypeStruct((8, 128), jnp.float32),
        grid=(width // wide,),
        in_specs=[spec, spec],
        out_specs=pl.BlockSpec((8, 128), lambda step: (0, 0)),
        scratch_shapes=[pltpu.VMEM((2, rows, 128), jnp.float32)],
        name="squares",
    )(fwd_in, saved_in)


def over_chan(rows):
    count = lax.axis_size("chan")
    got = [rows]
    for apart in range(1, count):
        got.append(
            lax.ppermute(rows, "chan", [(low, (low + apart) % count) for low in range(count)])
        )
    return got


def inv_rms_columns(stat_refs):
    total = sum(ref[...] for ref in stat_refs)
    return rows_to_columns(lax.rsqrt(total / D + EPSILON))


def enter_kernel(s0, s1, s2, s3, fwd_ref, saved_ref, cot_ref, params_ref, out_ref, inv):
    @pl.when(pl.program_id(0) == 0)
    def _():
        inv[...] = inv_rms_columns((s0, s1, s2, s3))

    inv_fwd = inv[:, 0:1]
    inv_saved = inv[:, 1:2]
    for group in range(fwd_ref.shape[2] // LANES):
        at = pl.ds(group * LANES, LANES)
        p = [params_ref[0, row : row + 1, at] for row in range(7)]
        scaled = fwd_ref[0, :, at].astype(jnp.float32) * inv_fwd * p[0]
        mixed = (scaled * p[3] + p[4]) * (scaled * p[5] + p[6])
        scaled = saved_ref[0, :, at].astype(jnp.float32) * inv_saved * p[0]
        grad_conv = cot_ref[0, :, at].astype(jnp.float32) * (scaled * p[1] + p[2])
        out_ref[group, :, :LANES] = mixed.astype(jnp.bfloat16)
        out_ref[group, :, LANES:] = grad_conv.astype(jnp.bfloat16)


def enter(stats, fwd_in, saved_in, grad_out, mix_params):
    rows, width = fwd_in.shape[1:]
    wide = 512
    spec = pl.BlockSpec((1, rows, wide), lambda step: (0, 0, step))
    stat_spec = pl.BlockSpec((8, 128), lambda step: (0, 0))
    return pl.pallas_call(
        enter_kernel,
        out_shape=jax.ShapeDtypeStruct((width // LANES, rows, 2 * LANES), jnp.bfloat16),
        grid=(width // wide,),
        in_specs=[stat_spec] * 4
        + [spec, spec, spec, pl.BlockSpec((1, 7, wide), lambda step: (0, 0, step))],
        out_specs=pl.BlockSpec((wide // LANES, rows, 2 * LANES), lambda step: (step, 0, 0)),
        scratch_shapes=[pltpu.VMEM((rows, 128), jnp.float32)],
        name="enter",
    )(*stats, fwd_in, saved_in, grad_out, mix_params)


def conv_kernel(
    where_ref, order_ref, signal_ref, taps_ref, enter_hi, enter_lo, leave_hi, leave_lo, out_ref,
    ordered, spectra, filt, filt_nyq, product,
):
    del where_ref
    stored, rows, _ = signal_ref.shape
    blocks = stored * rows // BLOCK

    def transform(data):
        return jnp.dot(enter_hi[...], data, preferred_element_type=jnp.float32) + jnp.dot(
            enter_lo[...], data, preferred_element_type=jnp.float32
        )

    for index in range(stored):
        at = pl.multiple_of(order_ref[index] * rows, rows)
        ordered[pl.ds(at, rows), :] = signal_ref[index]

    freq = lax.broadcasted_iota(jnp.int32, (2 * BLOCK, LANES), 0)
    parity = jnp.where(freq % 2 == 0, 1.0, -1.0)
    first = lax.broadcasted_iota(jnp.int32, (BLOCK, LANES), 0) == 0
    earlier = None
    for index in range(blocks):
        current = transform(taps_ref[0, index * BLOCK : (index + 1) * BLOCK, :])
        both = parity * current
        if earlier is not None:
            both = both + earlier
        earlier = current
        real, imag = both[:BLOCK], both[BLOCK:]
        filt[index, 0] = real
        filt[index, 1] = jnp.where(first, 0.0, imag)
        filt_nyq[index] = jnp.where(first, imag, real)
        spectra[index] = transform(ordered[index * BLOCK : (index + 1) * BLOCK, :])

    def products(tile, carry):
        at = pl.multiple_of(tile * 8, 8)
        low = pl.ds(at, 8)
        high = pl.ds(pl.multiple_of(BLOCK + tile * 8, 8), 8)
        f_re = [filt[d, 0, low, :] for d in range(blocks)]
        f_im = [filt[d, 1, low, :] for d in range(blocks)]
        f_nq = [filt_nyq[d, low, :] for d in range(blocks)]
        for adjoint in (False, True):
            lanes = slice(LANES, 2 * LANES) if adjoint else slice(0, LANES)
            x_re = [spectra[j, low, lanes] for j in range(blocks)]
            x_im = [spectra[j, high, lanes] for j in range(blocks)]
            for i in range(blocks):
                re = im = None
                for j in range(i, blocks) if adjoint else range(i + 1):
                    d = abs(i - j)
                    a, b = f_re[d] * x_re[j], f_im[d] * x_im[j]
                    c, e = f_nq[d] * x_im[j], f_im[d] * x_re[j]
                    one = a + b if adjoint else a - b
                    two = c - e if adjoint else c + e
                    re = one if re is None else re + one
                    im = two if im is None else im + two
                product[i, low, lanes] = re
                product[i, high, lanes] = im
        return carry

    lax.fori_loop(0, BLOCK // 8, products, 0)

    for index in range(blocks):
        value = product[index]
        top = value.astype(jnp.bfloat16)
        rest = (value - top.astype(jnp.float32)).astype(jnp.bfloat16)
        left = (
            jnp.dot(leave_hi[...], top, preferred_element_type=jnp.float32)
            + jnp.dot(leave_lo[...], top, preferred_element_type=jnp.float32)
            + jnp.dot(leave_hi[...], rest, preferred_element_type=jnp.float32)
        )
        ordered[index * BLOCK : (index + 1) * BLOCK, :] = left.astype(jnp.bfloat16)

    for index in range(stored):
        at = pl.multiple_of(order_ref[index] * rows, rows)
        out_ref[index] = ordered[pl.ds(at, rows), :]


def convolve(signal, filters, span_order, tables):
    stored, rows, wide = signal.shape
    length = stored * rows
    blocks = length // BLOCK
    where = lax.axis_index("seq").astype(jnp.int32).reshape(1)
    whole = lambda shape: pl.BlockSpec(shape, lambda step, *_: (0,) * len(shape))
    return pl.pallas_call(
        conv_kernel,
        out_shape=jax.ShapeDtypeStruct(signal.shape, jnp.bfloat16),
        grid_spec=pltpu.PrefetchScalarGridSpec(
            num_scalar_prefetch=2,
            grid=(1,),
            in_specs=[
                whole(signal.shape),
                pl.BlockSpec((1, length, LANES), lambda step, at, order: (0, 0, at[0])),
            ]
            + [whole(table.shape) for table in tables],
            out_specs=whole(signal.shape),
            scratch_shapes=[
                pltpu.VMEM((length, wide), jnp.bfloat16),
                pltpu.VMEM((blocks, 2 * BLOCK, wide), jnp.float32),
                pltpu.VMEM((blocks, 2, BLOCK, LANES), jnp.float32),
                pltpu.VMEM((blocks, BLOCK, LANES), jnp.float32),
                pltpu.VMEM((blocks, 2 * BLOCK, wide), jnp.float32),
            ],
        ),
        name="convolve",
    )(where, span_order, signal, filters, *tables)


def leave_kernel(
    s0, s1, s2, s3, back_ref, fwd_ref, saved_ref, sconv_ref, cot_ref, params_ref,
    layer_ref, partial_ref, sums_ref, cross_ref, inv, acc,
):
    step = pl.program_id(0)

    @pl.when(step == 0)
    def _():
        inv[...] = inv_rms_columns((s0, s1, s2, s3))
        acc[...] = jnp.zeros_like(acc)

    inv_fwd = inv[:, 0:1]
    inv_saved = inv[:, 1:2]
    cross = acc[...]
    for group in range(fwd_ref.shape[2] // LANES):
        at = pl.ds(group * LANES, LANES)
        p = [params_ref[0, row : row + 1, at] for row in range(7)]
        inputs = fwd_ref[0, :, at].astype(jnp.float32)
        query = inputs * inv_fwd * p[0] * p[1] + p[2]
        conv = back_ref[group, :, :LANES].astype(jnp.float32)
        layer_ref[0, :, at] = (inputs + query * conv).astype(jnp.bfloat16)

        grad_mixed = back_ref[group, :, LANES:].astype(jnp.float32)
        cot = cot_ref[0, :, at].astype(jnp.float32)
        normed = saved_ref[0, :, at].astype(jnp.float32) * inv_saved
        scaled = normed * p[0]
        grad_query = cot * sconv_ref[0, :, at].astype(jnp.float32)
        grad_key = grad_mixed * (scaled * p[5] + p[6])
        grad_value = grad_mixed * (scaled * p[3] + p[4])
        grad_scaled = grad_query * p[1] + grad_key * p[3] + grad_value * p[5]
        rows = [
            grad_scaled * normed,
            grad_query * scaled,
            grad_query,
            grad_key * scaled,
            grad_key,
            grad_value * scaled,
            grad_value,
        ]
        rows = [jnp.sum(row, axis=0, keepdims=True) for row in rows]
        sums_ref[group] = jnp.concatenate(rows + [jnp.zeros_like(rows[0])], axis=0)
        grad_normed = grad_scaled * p[0]
        cross = cross + grad_normed * normed
        partial_ref[:, at] = cot + inv_saved * grad_normed
    acc[...] = cross

    @pl.when(step == pl.num_programs(0) - 1)
    def _():
        cross_ref[...] = columns_to_rows([jnp.sum(acc[...], axis=1, keepdims=True)])


def leave(stats, back, fwd_in, saved_in, saved_conv, grad_out, mix_params):
    rows, width = fwd_in.shape[1:]
    wide = 512
    spec = pl.BlockSpec((1, rows, wide), lambda step: (0, 0, step))
    small = pl.BlockSpec((8, 128), lambda step: (0, 0))
    return pl.pallas_call(
        leave_kernel,
        out_shape=(
            jax.ShapeDtypeStruct(fwd_in.shape, jnp.bfloat16),
            jax.ShapeDtypeStruct((rows, width), jnp.float32),
            jax.ShapeDtypeStruct((width // LANES, 8, LANES), jnp.float32),
            jax.ShapeDtypeStruct((8, 128), jnp.float32),
        ),
        grid=(width // wide,),
        in_specs=[small] * 4
        + [pl.BlockSpec((wide // LANES, rows, 2 * LANES), lambda step: (step, 0, 0))]
        + [spec] * 4
        + [pl.BlockSpec((1, 7, wide), lambda step: (0, 0, step))],
        out_specs=(
            spec,
            pl.BlockSpec((rows, wide), lambda step: (0, step)),
            pl.BlockSpec((wide // LANES, 8, LANES), lambda step: (step, 0, 0)),
            small,
        ),
        scratch_shapes=[pltpu.VMEM((rows, 128), jnp.float32)] * 2,
        name="leave",
    )(*stats, back, fwd_in, saved_in, saved_conv, grad_out, mix_params)


def input_grad_kernel(s0, s1, s2, s3, c0, c1, c2, c3, partial_ref, saved_ref, out_ref, factor):
    @pl.when(pl.program_id(0) == 0)
    def _():
        inv = inv_rms_columns((s0, s1, s2, s3))[:, 1:2]
        cross = rows_to_columns(c0[...] + c1[...] + c2[...] + c3[...])[:, 0:1] / D
        factor[...] = jnp.broadcast_to(inv * inv * cross, factor.shape)

    scale = factor[:, 0:1]
    for at in range(0, partial_ref.shape[1], LANES):
        at = pl.ds(at, LANES)
        out_ref[0, :, at] = (
            partial_ref[:, at] - saved_ref[0, :, at].astype(jnp.float32) * scale
        ).astype(jnp.bfloat16)


def finish_input_grad(stats, crosses, partial, saved_in):
    rows, width = partial.shape
    wide = 512
    spec = pl.BlockSpec((1, rows, wide), lambda step: (0, 0, step))
    small = pl.BlockSpec((8, 128), lambda step: (0, 0))
    return pl.pallas_call(
        input_grad_kernel,
        out_shape=jax.ShapeDtypeStruct(saved_in.shape, jnp.bfloat16),
        grid=(width // wide,),
        in_specs=[small] * 8 + [pl.BlockSpec((rows, wide), lambda step: (0, step)), spec],
        out_specs=spec,
        scratch_shapes=[pltpu.VMEM((rows, 128), jnp.float32)],
        name="input_grad",
    )(*stats, *crosses, partial, saved_in)


def per_device(tables, fwd_in, saved_in, saved_conv, grad_out, filters, mix_params, span_order):
    stats = over_chan(squares(fwd_in, saved_in))
    payload = enter(stats, fwd_in, saved_in, grad_out, mix_params)
    payload = lax.all_to_all(payload, "seq", 0, 0)
    back = convolve(payload, filters, span_order, tables)
    back = lax.all_to_all(back, "seq", 0, 0)
    layer_out, partial, sums, cross = leave(
        stats, back, fwd_in, saved_in, saved_conv, grad_out, mix_params
    )
    crosses = over_chan(cross)
    input_grad = finish_input_grad(stats, crosses, partial, saved_in)
    outgoing = jnp.where(lax.axis_index("pipe") == 0, layer_out, input_grad)
    received = lax.ppermute(outgoing, "pipe", [(0, 1), (1, 0)])
    sums = jnp.sum(lax.all_to_all(sums, "seq", 0, 0), axis=0)
    sums = lax.all_gather(sums, "seq", axis=1, tiled=True)
    param_grad = sums[:7]
    return (layer_out, input_grad, param_grad[None], received)


def solution(mesh):
    tables = transform_tables()
    in_specs = (
        P("pipe", "seq", "chan"),
        P("pipe", "seq", "chan"),
        P("pipe", "seq", "chan"),
        P("pipe", "seq", "chan"),
        P("pipe", None, "chan"),
        P("pipe", None, "chan"),
        P(),
    )
    out_specs = (
        P("pipe", "seq", "chan"),
        P("pipe", "seq", "chan"),
        P("pipe", None, "chan"),
        P("pipe", "seq", "chan"),
    )
    return jax.shard_map(
        functools.partial(per_device, tuple(jnp.asarray(table) for table in tables)),
        mesh=mesh,
        in_specs=in_specs,
        out_specs=out_specs,
        check_vma=False,
    )
```

```python
import functools

import jax
import jax.numpy as jnp
import ml_dtypes
import numpy as np
from jax import lax
from jax.experimental import pallas as pl
from jax.experimental.pallas import tpu as pltpu
from jax.sharding import PartitionSpec as P

D = 8192
EPSILON = 1e-05
BLOCK = 256
LANES = 128


def split_bf16(table):
    high = table.astype(np.float32).astype(ml_dtypes.bfloat16)
    low = (table - high.astype(np.float64)).astype(np.float32).astype(ml_dtypes.bfloat16)
    return high, low


def transform_tables():
    period = 2 * BLOCK
    freq = np.arange(BLOCK)[:, None]
    time = np.arange(BLOCK)[None, :]
    angle = 2.0 * np.pi / period * (freq * time % period)
    real, imag = np.cos(angle), -np.sin(angle)
    imag[0] = np.where(np.arange(BLOCK) % 2 == 0, 1.0, -1.0)
    enter = np.concatenate([real, imag], axis=0)
    angle = 2.0 * np.pi / period * (freq * (time + BLOCK) % period)
    real, imag = 2.0 * np.cos(angle), -2.0 * np.sin(angle)
    real[0] = 1.0
    imag[0] = np.where(np.arange(BLOCK) % 2 == 0, 1.0, -1.0)
    leave = np.concatenate([real, imag], axis=0).T / period
    return split_bf16(enter) + split_bf16(leave)


def rows_to_columns(rows):
    return jnp.concatenate([rows] * 16, axis=0).T


def columns_to_rows(columns):
    lane = lax.broadcasted_iota(jnp.int32, (128, 128), 1)
    square = jnp.zeros((128, 128), jnp.float32)
    for index, column in enumerate(columns):
        square = jnp.where(lane == index, column, square)
    return square.T[:8]


def lane_groups_sum(block):
    total = block[:, :128]
    for at in range(128, block.shape[1], 128):
        total = total + block[:, at : at + 128]
    return total


def pack_kernel(fwd_ref, saved_ref, cot_ref, out_ref, squares_ref, acc):
    step = pl.program_id(0)
    rows = fwd_ref.shape[1]

    @pl.when(step == 0)
    def _():
        acc[...] = jnp.zeros_like(acc)

    for group in range(fwd_ref.shape[2] // LANES):
        at = pl.ds(group * LANES, LANES)
        for index, ref in enumerate((fwd_ref, saved_ref, cot_ref)):
            value = ref[0, :, at]
            out_ref[group, index * rows : (index + 1) * rows, :] = value
            if index < 2:
                wide = value.astype(jnp.float32)
                acc[index] += wide * wide

    @pl.when(step == pl.num_programs(0) - 1)
    def _():
        squares_ref[...] = columns_to_rows(
            [jnp.sum(acc[index], axis=1, keepdims=True) for index in range(2)]
        )


def pack(fwd_in, saved_in, grad_out):
    rows, width = fwd_in.shape[1:]
    wide = 512
    spec = pl.BlockSpec((1, rows, wide), lambda step: (0, 0, step))
    return pl.pallas_call(
        pack_kernel,
        out_shape=(
            jax.ShapeDtypeStruct((width // LANES, 3 * rows, LANES), jnp.bfloat16),
            jax.ShapeDtypeStruct((8, 128), jnp.float32),
        ),
        grid=(width // wide,),
        in_specs=[spec] * 3,
        out_specs=(
            pl.BlockSpec((wide // LANES, 3 * rows, LANES), lambda step: (step, 0, 0)),
            pl.BlockSpec((8, 128), lambda step: (0, 0)),
        ),
        scratch_shapes=[pltpu.VMEM((2, rows, 128), jnp.float32)],
        name="pack",
    )(fwd_in, saved_in, grad_out)


def over_chan(rows):
    count = lax.axis_size("chan")
    got = [rows]
    for apart in range(1, count):
        got.append(
            lax.ppermute(rows, "chan", [(low, (low + apart) % count) for low in range(count)])
        )
    return got


def early_kernel(s0, s1, s2, s3, saved_ref, sconv_ref, cot_ref, out_ref, inv_rows, inv):
    @pl.when(pl.program_id(0) == 0)
    def _():
        rows = lax.rsqrt((s0[...] + s1[...] + s2[...] + s3[...]) / D + EPSILON)
        inv_rows[...] = rows
        inv[...] = rows_to_columns(rows)

    inv_saved = inv[:, 1:2]
    for group in range(saved_ref.shape[2] // LANES):
        at = pl.ds(group * LANES, LANES)
        normed = saved_ref[0, :, at].astype(jnp.float32) * inv_saved
        grad_query = cot_ref[0, :, at].astype(jnp.float32) * sconv_ref[0, :, at].astype(jnp.float32)
        out_ref[group, 0:2, :] = inv_rows[0:2, :]
        out_ref[group, 2:3, :] = jnp.sum(grad_query, axis=0, keepdims=True)
        out_ref[group, 3:4, :] = jnp.sum(grad_query * normed, axis=0, keepdims=True)
        out_ref[group, 4:8, :] = jnp.zeros((4, LANES), jnp.float32)


def early(stats, saved_in, saved_conv, grad_out):
    rows, width = saved_in.shape[1:]
    wide = 512
    spec = pl.BlockSpec((1, rows, wide), lambda step: (0, 0, step))
    small = pl.BlockSpec((8, 128), lambda step: (0, 0))
    return pl.pallas_call(
        early_kernel,
        out_shape=(
            jax.ShapeDtypeStruct((width // LANES, 8, LANES), jnp.float32),
            jax.ShapeDtypeStruct((8, 128), jnp.float32),
        ),
        grid=(width // wide,),
        in_specs=[small] * 4 + [spec] * 3,
        out_specs=(
            pl.BlockSpec((wide // LANES, 8, LANES), lambda step: (step, 0, 0)),
            small,
        ),
        scratch_shapes=[pltpu.VMEM((rows, 128), jnp.float32)],
        name="early",
    )(*stats, saved_in, saved_conv, grad_out)


def filter_kernel(where_ref, taps_ref, enter_hi, enter_lo, filt):
    del where_ref
    freq = lax.broadcasted_iota(jnp.int32, (2 * BLOCK, LANES), 0)
    parity = jnp.where(freq % 2 == 0, 1.0, -1.0)
    first = lax.broadcasted_iota(jnp.int32, (BLOCK, LANES), 0) == 0
    earlier = None
    for index in range(filt.shape[0]):
        taps = taps_ref[0, index * BLOCK : (index + 1) * BLOCK, :]
        current = jnp.dot(enter_hi[...], taps, preferred_element_type=jnp.float32) + jnp.dot(
            enter_lo[...], taps, preferred_element_type=jnp.float32
        )
        both = parity * current
        if earlier is not None:
            both = both + earlier
        earlier = current
        real, imag = both[:BLOCK], both[BLOCK:]
        filt[index, 0] = real
        filt[index, 1] = jnp.where(first, 0.0, imag)
        filt[index, 2] = jnp.where(first, imag, real)


def whole(shape):
    return pl.BlockSpec(shape, lambda step, *_: (0,) * len(shape))


def filter_spectra(where, filters, tables):
    length = filters.shape[1]
    shape = (length // BLOCK, 3, BLOCK, LANES)
    return pl.pallas_call(
        filter_kernel,
        out_shape=jax.ShapeDtypeStruct(shape, jnp.float32),
        grid_spec=pltpu.PrefetchScalarGridSpec(
            num_scalar_prefetch=1,
            grid=(1,),
            in_specs=[pl.BlockSpec((1, length, LANES), lambda step, at: (0, 0, at[0]))]
            + [whole(table.shape) for table in tables[:2]],
            out_specs=whole(shape),
        ),
        name="filter_spectra",
    )(where, filters, *tables[:2])


def conv_kernel(
    where_ref, order_ref, raw_ref, early_ref, params_ref, filt, enter_hi, enter_lo, leave_hi,
    leave_lo, out_ref, ordered, spectra, product, inv,
):
    del where_ref
    stored = raw_ref.shape[0]
    rows = raw_ref.shape[1] // 3
    blocks = stored * rows // BLOCK
    p = [params_ref[0, row : row + 1, :] for row in range(7)]

    inv_rows = jnp.concatenate([early_ref[index] for index in range(stored)], axis=0)
    inv[...] = inv_rows.T
    for index in range(stored):
        at = pl.multiple_of(order_ref[index] * rows, rows)
        inv_fwd = inv[:, 8 * index : 8 * index + 1]
        inv_saved = inv[:, 8 * index + 1 : 8 * index + 2]
        scaled = raw_ref[index, :rows, :].astype(jnp.float32) * inv_fwd * p[0]
        mixed = (scaled * p[3] + p[4]) * (scaled * p[5] + p[6])
        scaled = raw_ref[index, rows : 2 * rows, :].astype(jnp.float32) * inv_saved * p[0]
        cot = raw_ref[index, 2 * rows :, :].astype(jnp.float32)
        ordered[pl.ds(at, rows), :LANES] = mixed.astype(jnp.bfloat16)
        ordered[pl.ds(at, rows), LANES:] = (cot * (scaled * p[1] + p[2])).astype(jnp.bfloat16)

    for index in range(blocks):
        data = ordered[index * BLOCK : (index + 1) * BLOCK, :]
        spectra[index] = jnp.dot(
            enter_hi[...], data, preferred_element_type=jnp.float32
        ) + jnp.dot(enter_lo[...], data, preferred_element_type=jnp.float32)

    def products(tile, carry):
        low = pl.ds(pl.multiple_of(tile * 8, 8), 8)
        high = pl.ds(pl.multiple_of(BLOCK + tile * 8, 8), 8)
        f_re = [filt[d, 0, low, :] for d in range(blocks)]
        f_im = [filt[d, 1, low, :] for d in range(blocks)]
        f_nq = [filt[d, 2, low, :] for d in range(blocks)]
        for adjoint in (False, True):
            lanes = slice(LANES, 2 * LANES) if adjoint else slice(0, LANES)
            x_re = [spectra[j, low, lanes] for j in range(blocks)]
            x_im = [spectra[j, high, lanes] for j in range(blocks)]
            for i in range(blocks):
                re = im = None
                for j in range(i, blocks) if adjoint else range(i + 1):
                    d = abs(i - j)
                    a, b = f_re[d] * x_re[j], f_im[d] * x_im[j]
                    c, e = f_nq[d] * x_im[j], f_im[d] * x_re[j]
                    one = a + b if adjoint else a - b
                    two = c - e if adjoint else c + e
                    re = one if re is None else re + one
                    im = two if im is None else im + two
                product[i, low, lanes] = re
                product[i, high, lanes] = im
        return carry

    lax.fori_loop(0, BLOCK // 8, products, 0)

    for index in range(blocks):
        value = product[index]
        top = value.astype(jnp.bfloat16)
        rest = (value - top.astype(jnp.float32)).astype(jnp.bfloat16)
        left = (
            jnp.dot(leave_hi[...], top, preferred_element_type=jnp.float32)
            + jnp.dot(leave_lo[...], top, preferred_element_type=jnp.float32)
            + jnp.dot(leave_hi[...], rest, preferred_element_type=jnp.float32)
        )
        ordered[index * BLOCK : (index + 1) * BLOCK, :] = left.astype(jnp.bfloat16)

    fold = lambda block: jnp.sum(block.reshape(rows // 8, 8, LANES), axis=0)
    sums = [jnp.zeros((8, LANES), jnp.float32)] * 3
    for index in range(stored):
        at = pl.multiple_of(order_ref[index] * rows, rows)
        block = ordered[pl.ds(at, rows), :]
        out_ref[index, :rows, :] = block
        grad_mixed = block[:, LANES:].astype(jnp.float32)
        inv_saved = inv[:, 8 * index + 1 : 8 * index + 2]
        normed = raw_ref[index, rows : 2 * rows, :].astype(jnp.float32) * inv_saved
        once = grad_mixed * normed
        for power, term in enumerate((grad_mixed, once, once * normed)):
            sums[power] = sums[power] + fold(term)

    m0, m1, m2 = [jnp.sum(total, axis=0, keepdims=True) for total in sums]
    known = early_ref[0]
    for index in range(1, stored):
        known = known + early_ref[index]
    q0, q1 = known[2:3], known[3:4]
    key_normed = p[0] * p[5] * m2 + p[6] * m1
    value_normed = p[0] * p[3] * m2 + p[4] * m1
    grads = jnp.concatenate(
        [
            p[1] * q1 + p[3] * key_normed + p[5] * value_normed,
            p[0] * q1,
            q0,
            p[0] * key_normed,
            p[0] * p[5] * m1 + p[6] * m0,
            p[0] * value_normed,
            p[0] * p[3] * m1 + p[4] * m0,
            jnp.zeros_like(q0),
        ],
        axis=0,
    )
    top = grads.astype(jnp.bfloat16)
    rest = (grads - top.astype(jnp.float32)).astype(jnp.bfloat16)
    for index in range(stored):
        out_ref[index, rows : rows + 8, :LANES] = top
        out_ref[index, rows : rows + 8, LANES:] = rest


def convolve(where, raw, known, mix_params, spectra, span_order, tables):
    stored = raw.shape[0]
    rows = raw.shape[1] // 3
    length = stored * rows
    blocks = length // BLOCK
    out_shape = (stored, rows + 8, 2 * LANES)
    return pl.pallas_call(
        conv_kernel,
        out_shape=jax.ShapeDtypeStruct(out_shape, jnp.bfloat16),
        grid_spec=pltpu.PrefetchScalarGridSpec(
            num_scalar_prefetch=2,
            grid=(1,),
            in_specs=[
                whole(raw.shape),
                whole(known.shape),
                pl.BlockSpec((1, 7, LANES), lambda step, at, order: (0, 0, at[0])),
                whole(spectra.shape),
            ]
            + [whole(table.shape) for table in tables],
            out_specs=whole(out_shape),
            scratch_shapes=[
                pltpu.VMEM((length, 2 * LANES), jnp.bfloat16),
                pltpu.VMEM((blocks, 2 * BLOCK, 2 * LANES), jnp.float32),
                pltpu.VMEM((blocks, 2 * BLOCK, 2 * LANES), jnp.float32),
                pltpu.VMEM((128, 8 * stored), jnp.float32),
            ],
        ),
        name="convolve",
    )(where, span_order, raw, known, mix_params, spectra, *tables)


def leave_kernel(
    pipe_ref, inv_rows, back_ref, fwd_ref, saved_ref, sconv_ref, cot_ref, params_ref,
    layer_ref, send_ref, partial_ref, sums_ref, cross_ref, inv, acc,
):
    step = pl.program_id(0)
    rows = fwd_ref.shape[1]

    @pl.when(step == 0)
    def _():
        inv[...] = rows_to_columns(inv_rows[...])
        acc[...] = jnp.zeros_like(acc)

    inv_fwd = inv[:, 0:1]
    inv_saved = inv[:, 1:2]
    first = pipe_ref[0] == 0
    cross = acc[...]
    for group in range(fwd_ref.shape[2] // LANES):
        at = pl.ds(group * LANES, LANES)
        p = [params_ref[0, row : row + 1, at] for row in range(7)]
        inputs = fwd_ref[0, :, at].astype(jnp.float32)
        query = inputs * inv_fwd * (p[0] * p[1]) + p[2]
        conv = back_ref[group, :rows, :LANES].astype(jnp.float32)
        layer = inputs + query * conv
        layer_ref[0, :, at] = layer.astype(jnp.bfloat16)

        grad_mixed = back_ref[group, :rows, LANES:].astype(jnp.float32)
        cot = cot_ref[0, :, at].astype(jnp.float32)
        normed = saved_ref[0, :, at].astype(jnp.float32) * inv_saved
        scaled = normed * p[0]
        grad_query = cot * sconv_ref[0, :, at].astype(jnp.float32)
        mixed_grad = (scaled * p[5] + p[6]) * p[3] + (scaled * p[3] + p[4]) * p[5]
        grad_normed = (grad_query * p[1] + grad_mixed * mixed_grad) * p[0]
        cross = cross + grad_normed * normed
        partial = cot + inv_saved * grad_normed
        partial_ref[:, at] = partial
        send_ref[0, :, at] = jnp.where(first, layer, partial).astype(jnp.bfloat16)
        sums_ref[0, :, at] = (
            back_ref[group, rows : rows + 8, :LANES].astype(jnp.float32)
            + back_ref[group, rows : rows + 8, LANES:].astype(jnp.float32)
        )[:7]
    acc[...] = cross

    @pl.when(step == pl.num_programs(0) - 1)
    def _():
        cross_ref[...] = columns_to_rows([jnp.sum(acc[...], axis=1, keepdims=True)])


def leave(pipe, inv_rows, back, fwd_in, saved_in, saved_conv, grad_out, mix_params):
    rows, width = fwd_in.shape[1:]
    wide = 512
    spec = pl.BlockSpec((1, rows, wide), lambda step, *_: (0, 0, step))
    small = pl.BlockSpec((8, 128), lambda step, *_: (0, 0))
    params = pl.BlockSpec((1, 7, wide), lambda step, *_: (0, 0, step))
    return pl.pallas_call(
        leave_kernel,
        out_shape=(
            jax.ShapeDtypeStruct(fwd_in.shape, jnp.bfloat16),
            jax.ShapeDtypeStruct(fwd_in.shape, jnp.bfloat16),
            jax.ShapeDtypeStruct((rows, width), jnp.float32),
            jax.ShapeDtypeStruct(mix_params.shape, jnp.float32),
            jax.ShapeDtypeStruct((8, 128), jnp.float32),
        ),
        grid_spec=pltpu.PrefetchScalarGridSpec(
            num_scalar_prefetch=1,
            grid=(width // wide,),
            in_specs=[small]
            + [
                pl.BlockSpec(
                    (wide // LANES, rows + 8, 2 * LANES), lambda step, *_: (step, 0, 0)
                )
            ]
            + [spec] * 4
            + [params],
            out_specs=(
                spec,
                spec,
                pl.BlockSpec((rows, wide), lambda step, *_: (0, step)),
                params,
                small,
            ),
            scratch_shapes=[pltpu.VMEM((rows, 128), jnp.float32)] * 2,
        ),
        name="leave",
    )(pipe, inv_rows, back, fwd_in, saved_in, saved_conv, grad_out, mix_params)


def subtract_kernel(scale_ref, value_ref, saved_ref, out_ref, scale):
    @pl.when(pl.program_id(0) == 0)
    def _():
        scale[...] = rows_to_columns(scale_ref[...])

    factor = scale[:, 0:1]
    for at in range(0, out_ref.shape[2], LANES):
        at = pl.ds(at, LANES)
        value = value_ref[0, :, at].astype(jnp.float32)
        saved = saved_ref[0, :, at].astype(jnp.float32)
        out_ref[0, :, at] = (value - saved * factor).astype(jnp.bfloat16)


def subtract(scale_rows, value, saved, name):
    rows, width = saved.shape[1:]
    wide = 1024
    spec = pl.BlockSpec((1, rows, wide), lambda step: (0, 0, step))
    return pl.pallas_call(
        subtract_kernel,
        out_shape=jax.ShapeDtypeStruct(saved.shape, jnp.bfloat16),
        grid=(width // wide,),
        in_specs=[pl.BlockSpec((8, 128), lambda step: (0, 0)), spec, spec],
        out_specs=spec,
        scratch_shapes=[pltpu.VMEM((rows, 128), jnp.float32)],
        name=name,
    )(scale_rows, value, saved)


def per_device(tables, fwd_in, saved_in, saved_conv, grad_out, filters, mix_params, span_order):
    where = lax.axis_index("seq").astype(jnp.int32).reshape(1)
    pipe = lax.axis_index("pipe").astype(jnp.int32)
    raw, sums = pack(fwd_in, saved_in, grad_out)
    raw = lax.all_to_all(raw, "seq", 0, 0)
    peer_saved = lax.ppermute(saved_in, "pipe", [(1, 0)])
    known, inv_rows = early(over_chan(sums), saved_in, saved_conv, grad_out)
    known = lax.all_to_all(known, "seq", 0, 0)
    spectra = filter_spectra(where, filters, tables)
    back = convolve(where, raw, known, mix_params, spectra, span_order, tables)
    back = lax.all_to_all(back, "seq", 0, 0)
    layer_out, outgoing, partial, param_grad, cross = leave(
        pipe.reshape(1), inv_rows, back, fwd_in, saved_in, saved_conv, grad_out, mix_params
    )
    incoming = lax.ppermute(outgoing, "pipe", [(0, 1), (1, 0)])
    cross = sum(over_chan(cross))[:1]
    scale = cross * (inv_rows[1:2] * inv_rows[1:2] / D)
    scale = jnp.broadcast_to(scale, (8, 128))
    peer_scale = lax.ppermute(scale, "pipe", [(1, 0)])
    input_grad = subtract(scale, partial[None], saved_in, "input_grad")
    received = subtract(peer_scale, incoming, peer_saved, "received")
    return (layer_out, input_grad, param_grad, received)


def solution(mesh):
    tables = transform_tables()
    in_specs = (
        P("pipe", "seq", "chan"),
        P("pipe", "seq", "chan"),
        P("pipe", "seq", "chan"),
        P("pipe", "seq", "chan"),
        P("pipe", None, "chan"),
        P("pipe", None, "chan"),
        P(),
    )
    out_specs = (
        P("pipe", "seq", "chan"),
        P("pipe", "seq", "chan"),
        P("pipe", None, "chan"),
        P("pipe", "seq", "chan"),
    )
    return jax.shard_map(
        functools.partial(per_device, tuple(jnp.asarray(table) for table in tables)),
        mesh=mesh,
        in_specs=in_specs,
        out_specs=out_specs,
        check_vma=False,
    )
```

```python
import functools

import jax
import jax.numpy as jnp
import ml_dtypes
import numpy as np
from jax import lax
from jax.experimental import pallas as pl
from jax.experimental.pallas import tpu as pltpu
from jax.sharding import PartitionSpec as P


D = 8192
EPSILON = 1e-05
BLOCK = 256
LANES = 128


def split_bf16(table):
    high = table.astype(np.float32).astype(ml_dtypes.bfloat16)
    low = (table - high.astype(np.float64)).astype(np.float32).astype(ml_dtypes.bfloat16)
    return high, low


def transform_tables():
    period = 2 * BLOCK
    freq = np.arange(BLOCK)[:, None]
    time = np.arange(BLOCK)[None, :]
    angle = 2.0 * np.pi / period * (freq * time % period)
    real, imag = np.cos(angle), -np.sin(angle)
    imag[0] = np.where(np.arange(BLOCK) % 2 == 0, 1.0, -1.0)
    enter = np.concatenate([real, imag], axis=0)
    angle = 2.0 * np.pi / period * (freq * (time + BLOCK) % period)
    real, imag = 2.0 * np.cos(angle), -2.0 * np.sin(angle)
    real[0] = 1.0
    imag[0] = np.where(np.arange(BLOCK) % 2 == 0, 1.0, -1.0)
    leave = np.concatenate([real, imag], axis=0).T / period
    return split_bf16(enter) + split_bf16(leave)


def rows_to_columns(rows):
    return jnp.concatenate([rows] * 16, axis=0).T


def columns_to_rows(columns):
    lane = lax.broadcasted_iota(jnp.int32, (128, 128), 1)
    square = jnp.zeros((128, 128), jnp.float32)
    for index, column in enumerate(columns):
        square = jnp.where(lane == index, column, square)
    return square.T[:8]


VMEM = pl.BlockSpec(memory_space=pltpu.VMEM)
SMEM = pl.BlockSpec(memory_space=pltpu.SMEM)


def in_vmem(array):
    return pltpu.with_memory_space_constraint(array, pltpu.VMEM)


HBM = pl.BlockSpec(memory_space=pl.ANY)


def in_hbm(array):
    return pltpu.with_memory_space_constraint(array, pltpu.HBM)


def lane_spec(rows, wide):
    return pl.BlockSpec((1, rows, wide), lambda step, *_: (0, 0, step))


def whole(shape):
    return pl.BlockSpec(shape, lambda step, *_: (0,) * len(shape))


def pack_kernel(fwd_ref, saved_ref, cot_ref, out_ref, squares_ref, acc):
    step = pl.program_id(0)
    rows = fwd_ref.shape[1]

    @pl.when(step == 0)
    def _():
        acc[...] = jnp.zeros_like(acc)

    totals = [acc[0], acc[1]]
    for group in range(fwd_ref.shape[2] // LANES):
        at = pl.ds(group * LANES, LANES)
        for index, ref in enumerate((fwd_ref, saved_ref, cot_ref)):
            value = ref[0, :, at]
            out_ref[group, index * rows : (index + 1) * rows, :] = value
            if index < 2:
                wide = value.astype(jnp.float32)
                totals[index] = totals[index] + wide * wide
    acc[0] = totals[0]
    acc[1] = totals[1]

    @pl.when(step == pl.num_programs(0) - 1)
    def _():
        squares_ref[...] = columns_to_rows(
            [jnp.sum(acc[index], axis=1, keepdims=True) for index in range(2)]
        )


def pack(fwd_in, saved_in, grad_out):
    rows, width = fwd_in.shape[1:]
    wide = 512
    return pl.pallas_call(
        pack_kernel,
        out_shape=(
            jax.ShapeDtypeStruct((width // LANES, 3 * rows, LANES), jnp.bfloat16),
            jax.ShapeDtypeStruct((8, 128), jnp.float32),
        ),
        grid=(width // wide,),
        in_specs=[lane_spec(rows, wide)] * 3,
        out_specs=(
            pl.BlockSpec((wide // LANES, 3 * rows, LANES), lambda step: (step, 0, 0)),
            whole((8, 128)),
        ),
        scratch_shapes=[pltpu.VMEM((2, rows, 128), jnp.float32)],
        name="pack",
        compiler_params=pltpu.CompilerParams(vmem_limit_bytes=16 << 20),
    )(in_hbm(fwd_in), in_hbm(saved_in), in_hbm(grad_out))


def over_chan(rows):
    count = lax.axis_size("chan")
    got = [rows]
    for apart in range(1, count):
        got.append(
            lax.ppermute(rows, "chan", [(low, (low + apart) % count) for low in range(count)])
        )
    return got


def across(rows, flip):
    count = lax.axis_size("seq")
    return lax.ppermute(rows, "seq", [(low, low ^ flip) for low in range(count)])


def round_ring(rows, apart):
    count = lax.axis_size("seq")
    place = lambda low: low // 8 * 8 + (low + 2 * apart) % 8
    return lax.ppermute(rows, "seq", [(low, place(low)) for low in range(count)])


def gather_order():
    own = lax.axis_index("seq").astype(jnp.int32)
    block = jnp.arange(16, dtype=jnp.int32)
    core = (block ^ own) & 1
    back = (own // 2 - block // 2) % 4
    side = (block // 8) ^ (own // 8)
    return side * 8 + back * 2 + core


def early_kernel(where_ref, inv_ref, saved_ref, sconv_ref, cot_ref, out_ref, inv):
    @pl.when(pl.program_id(0) == 0)
    def _():
        inv[...] = rows_to_columns(inv_ref[0:8, :])

    inv_saved = inv[:, 1:2]
    for group in range(saved_ref.shape[2] // LANES):
        at = pl.ds(group * LANES, LANES)
        normed = saved_ref[0, :, at].astype(jnp.float32) * inv_saved
        grad_query = cot_ref[0, :, at].astype(jnp.float32) * sconv_ref[0, :, at].astype(jnp.float32)
        out_ref[0:1, at] = jnp.sum(grad_query, axis=0, keepdims=True)
        out_ref[1:2, at] = jnp.sum(grad_query * normed, axis=0, keepdims=True)


def early(where, inv, saved_in, saved_conv, grad_out):
    rows, width = saved_in.shape[1:]
    wide = 512
    return pl.pallas_call(
        early_kernel,
        out_shape=jax.ShapeDtypeStruct((2, width), jnp.float32),
        grid_spec=pltpu.PrefetchScalarGridSpec(
            num_scalar_prefetch=1,
            grid=(width // wide,),
            in_specs=[VMEM] + [lane_spec(rows, wide)] * 3,
            out_specs=pl.BlockSpec((2, wide), lambda step, *_: (0, step)),
            scratch_shapes=[pltpu.VMEM((rows, 128), jnp.float32)],
        ),
        name="early",
        compiler_params=pltpu.CompilerParams(vmem_limit_bytes=12 << 20),
    )(where, inv, saved_in, saved_conv, grad_out)


def side_by_side(ref, index):
    at = 2 * index * BLOCK
    return jnp.concatenate([ref[at : at + BLOCK, :], ref[at + BLOCK : at + 2 * BLOCK, :]], axis=1)


def enter_transform(enter_hi, enter_lo, data):
    return jnp.dot(enter_hi[...], data, preferred_element_type=jnp.float32) + jnp.dot(
        enter_lo[...], data, preferred_element_type=jnp.float32
    )


def filter_kernel(where_ref, taps_ref, enter_hi, enter_lo, filt):
    del where_ref
    freq = lax.broadcasted_iota(jnp.int32, (2 * BLOCK, LANES), 0)
    parity = jnp.where(freq % 2 == 0, 1.0, -1.0)
    first = lax.broadcasted_iota(jnp.int32, (BLOCK, LANES), 0) == 0
    earlier = None
    for pair in range(filt.shape[0] // 2):
        pair_spectra = enter_transform(enter_hi, enter_lo, side_by_side(taps_ref.at[0], pair))
        for side in range(2):
            current = pair_spectra[:, side * LANES : (side + 1) * LANES]
            both = parity * current
            if earlier is not None:
                both = both + earlier
            earlier = current
            real, imag = both[:BLOCK], both[BLOCK:]
            index = 2 * pair + side
            filt[index, 0] = real
            filt[index, 1] = jnp.where(first, 0.0, imag)
            filt[index, 2] = jnp.where(first, imag, real)


def filter_spectra(where, filters, tables):
    length = filters.shape[1]
    shape = (length // BLOCK, 3, BLOCK, LANES)
    return pl.pallas_call(
        filter_kernel,
        out_shape=pltpu.VMEM(shape, jnp.float32),
        grid_spec=pltpu.PrefetchScalarGridSpec(
            num_scalar_prefetch=1,
            grid=(1,),
            in_specs=[pl.BlockSpec((1, length, LANES), lambda step, at: (0, 0, at[0]))]
            + [whole(table.shape) for table in tables[:2]],
            out_specs=VMEM,
        ),
        name="filter_spectra",
        compiler_params=pltpu.CompilerParams(vmem_limit_bytes=16 << 20),
    )(where, in_hbm(filters), *[in_hbm(table) for table in tables[:2]])


def fold(block):
    return jnp.sum(block.reshape(block.shape[0] // 8, 8, LANES), axis=0)


def conv_kernel(
    where_ref, order_ref, gathered_ref, inv_ref, params_ref, filt, raw_hbm, enter_hi_hbm,
    enter_lo_hbm, leave_hi_hbm, leave_lo_hbm, out_hbm, raw_ref, enter_hi, enter_lo, leave_hi,
    leave_lo, out_ref, ordered, spectra, product, inv_rows, inv, raw_sem, table_sem, out_sem,
):
    stored = raw_ref.shape[0]
    raw_copies = [
        pltpu.make_async_copy(raw_hbm.at[index], raw_ref.at[index], raw_sem.at[index])
        for index in range(stored)
    ]
    table_copies = [
        pltpu.make_async_copy(source, target, table_sem.at[index])
        for index, (source, target) in enumerate(
            (
                (enter_hi_hbm, enter_hi),
                (enter_lo_hbm, enter_lo),
                (leave_hi_hbm, leave_hi),
                (leave_lo_hbm, leave_lo),
            )
        )
    ]
    out_copies = [
        pltpu.make_async_copy(out_ref.at[index], out_hbm.at[index], out_sem.at[index])
        for index in range(stored)
    ]
    for copy in raw_copies + table_copies:
        copy.start()
    rows = raw_ref.shape[1] // 3
    blocks = stored * rows // BLOCK
    lanes = pl.ds(pl.multiple_of(where_ref[0] * LANES, LANES), LANES)
    p = [params_ref[0, row : row + 1, lanes] for row in range(7)]

    for index in range(stored):
        inv_rows[2 * index : 2 * index + 2, :] = inv_ref[pl.ds(2 * gathered_ref[index], 2), :]
    inv[...] = jnp.concatenate([inv_rows[...]] * (128 // (2 * stored)), axis=0).T
    for index in range(stored):
        raw_copies[index].wait()
        at = pl.multiple_of(order_ref[index] * rows, rows)
        inv_fwd = inv[:, 2 * index : 2 * index + 1]
        inv_saved = inv[:, 2 * index + 1 : 2 * index + 2]
        scaled = raw_ref[index, :rows, :].astype(jnp.float32) * inv_fwd * p[0]
        mixed = (scaled * p[3] + p[4]) * (scaled * p[5] + p[6])
        scaled = raw_ref[index, rows : 2 * rows, :].astype(jnp.float32) * inv_saved * p[0]
        cot = raw_ref[index, 2 * rows :, :].astype(jnp.float32)
        ordered[pl.ds(at, rows), :LANES] = mixed.astype(jnp.bfloat16)
        ordered[pl.ds(at, rows), LANES:] = (cot * (scaled * p[1] + p[2])).astype(jnp.bfloat16)

    table_copies[0].wait()
    table_copies[1].wait()
    for index in range(blocks):
        data = ordered[index * BLOCK : (index + 1) * BLOCK, :]
        spectra[index] = enter_transform(enter_hi, enter_lo, data)

    def products(tile, carry):
        low = pl.ds(pl.multiple_of(tile * 8, 8), 8)
        high = pl.ds(pl.multiple_of(BLOCK + tile * 8, 8), 8)
        f_re = [filt[d, 0, low, :] for d in range(blocks)]
        f_im = [filt[d, 1, low, :] for d in range(blocks)]
        f_nq = [filt[d, 2, low, :] for d in range(blocks)]
        for adjoint in (False, True):
            lanes = slice(LANES, 2 * LANES) if adjoint else slice(0, LANES)
            x_re = [spectra[j, low, lanes] for j in range(blocks)]
            x_im = [spectra[j, high, lanes] for j in range(blocks)]
            for i in range(blocks):
                re = im = None
                for j in range(i, blocks) if adjoint else range(i + 1):
                    d = abs(i - j)
                    a, b = f_re[d] * x_re[j], f_im[d] * x_im[j]
                    c, e = f_nq[d] * x_im[j], f_im[d] * x_re[j]
                    one = a + b if adjoint else a - b
                    two = c - e if adjoint else c + e
                    re = one if re is None else re + one
                    im = two if im is None else im + two
                product[i, low, lanes] = re
                product[i, high, lanes] = im
        return carry

    lax.fori_loop(0, BLOCK // 8, products, 0)

    table_copies[2].wait()
    table_copies[3].wait()
    for index in range(blocks):
        value = product[index]
        top = value.astype(jnp.bfloat16)
        rest = (value - top.astype(jnp.float32)).astype(jnp.bfloat16)
        left = (
            jnp.dot(leave_hi[...], top, preferred_element_type=jnp.float32)
            + jnp.dot(leave_lo[...], top, preferred_element_type=jnp.float32)
            + jnp.dot(leave_hi[...], rest, preferred_element_type=jnp.float32)
        )
        ordered[index * BLOCK : (index + 1) * BLOCK, :] = left.astype(jnp.bfloat16)

    sums = [jnp.zeros((8, LANES), jnp.float32)] * 3
    for index in range(stored):
        at = pl.multiple_of(order_ref[index] * rows, rows)
        block = ordered[pl.ds(at, rows), :]
        out_ref[index, :rows, :] = block
        grad_mixed = block[:, LANES:].astype(jnp.float32)
        inv_saved = inv[:, 2 * index + 1 : 2 * index + 2]
        normed = raw_ref[index, rows : 2 * rows, :].astype(jnp.float32) * inv_saved
        once = grad_mixed * normed
        for power, term in enumerate((grad_mixed, once, once * normed)):
            sums[power] = sums[power] + fold(term)

    sums = jnp.concatenate(
        [jnp.sum(total, axis=0, keepdims=True) for total in sums]
        + [jnp.zeros((5, LANES), jnp.float32)],
        axis=0,
    )
    top = sums.astype(jnp.bfloat16)
    rest = (sums - top.astype(jnp.float32)).astype(jnp.bfloat16)
    for index in range(stored):
        out_ref[index, rows : rows + 8, :LANES] = top
        out_ref[index, rows : rows + 8, LANES:] = rest
        out_copies[index].start()
    for copy in out_copies:
        copy.wait()


def convolve(where, order, gathered, raw, inv, params, spectra, tables):
    stored = raw.shape[0]
    rows = raw.shape[1] // 3
    length = stored * rows
    blocks = length // BLOCK
    return pl.pallas_call(
        conv_kernel,
        out_shape=pltpu.HBM((stored, rows + 8, 2 * LANES), jnp.bfloat16),
        in_specs=[SMEM] * 3 + [VMEM] * 3 + [HBM] * 5,
        out_specs=HBM,
        scratch_shapes=[
            pltpu.VMEM(raw.shape, jnp.bfloat16),
            *[pltpu.VMEM(table.shape, jnp.bfloat16) for table in tables],
            pltpu.VMEM((stored, rows + 8, 2 * LANES), jnp.bfloat16),
            pltpu.VMEM((length, 2 * LANES), jnp.bfloat16),
            pltpu.VMEM((blocks, 2 * BLOCK, 2 * LANES), jnp.float32),
            pltpu.VMEM((blocks, 2 * BLOCK, 2 * LANES), jnp.float32),
            pltpu.VMEM((2 * stored, 128), jnp.float32),
            pltpu.VMEM((128, 128), jnp.float32),
            pltpu.SemaphoreType.DMA((stored,)),
            pltpu.SemaphoreType.DMA((4,)),
            pltpu.SemaphoreType.DMA((stored,)),
        ],
        name="convolve",
        compiler_params=pltpu.CompilerParams(vmem_limit_bytes=28 << 20),
    )(
        where, order, gathered, inv, params, in_vmem(spectra), in_hbm(raw),
        *[in_hbm(table) for table in tables],
    )


def leave_kernel(
    pipe_ref, inv_ref, back_ref, known_ref, fwd_ref, saved_ref, sconv_ref, cot_ref, params_ref,
    layer_ref, send_ref, partial_ref, grads_ref, cross_ref, inv, acc,
):
    step = pl.program_id(0)
    rows = fwd_ref.shape[1]

    @pl.when(step == 0)
    def _():
        inv[...] = rows_to_columns(inv_ref[0:8, :])
        acc[...] = jnp.zeros_like(acc)

    inv_fwd = inv[:, 0:1]
    inv_saved = inv[:, 1:2]
    first = pipe_ref[0] == 0
    cross = acc[...]
    groups = fwd_ref.shape[2] // LANES
    for group in range(groups):
        at = pl.ds(group * LANES, LANES)
        p = [params_ref[0, row : row + 1, at] for row in range(7)]
        inputs = fwd_ref[0, :, at].astype(jnp.float32)
        query = inputs * inv_fwd * p[0] * p[1] + p[2]
        conv = back_ref[step * groups + group, :rows, :LANES].astype(jnp.float32)
        layer = inputs + query * conv
        layer_ref[0, :, at] = layer.astype(jnp.bfloat16)

        grad_mixed = back_ref[step * groups + group, :rows, LANES:].astype(jnp.float32)
        cot = cot_ref[0, :, at].astype(jnp.float32)
        normed = saved_ref[0, :, at].astype(jnp.float32) * inv_saved
        scaled = normed * p[0]
        grad_query = cot * sconv_ref[0, :, at].astype(jnp.float32)
        mixed_grad = (scaled * p[5] + p[6]) * p[3] + (scaled * p[3] + p[4]) * p[5]
        grad_normed = (grad_query * p[1] + grad_mixed * mixed_grad) * p[0]
        cross = cross + grad_normed * normed
        partial = cot + inv_saved * grad_normed
        partial_ref[0, :, at] = partial
        send_ref[0, :, at] = jnp.where(first, layer, partial).astype(jnp.bfloat16)

        extra = back_ref[step * groups + group, rows : rows + 8, :].astype(jnp.float32)
        extra = extra[:, :LANES] + extra[:, LANES:]
        m0, m1, m2 = extra[0:1], extra[1:2], extra[2:3]
        q0, q1 = known_ref[0:1, at], known_ref[1:2, at]
        key_normed = p[0] * p[5] * m2 + p[6] * m1
        value_normed = p[0] * p[3] * m2 + p[4] * m1
        grads = [
            p[1] * q1 + p[3] * key_normed + p[5] * value_normed,
            p[0] * q1,
            q0,
            p[0] * key_normed,
            p[0] * p[5] * m1 + p[6] * m0,
            p[0] * value_normed,
            p[0] * p[3] * m1 + p[4] * m0,
        ]
        grads_ref[0, :, at] = jnp.concatenate(grads, axis=0)
    acc[...] = cross

    @pl.when(step == pl.num_programs(0) - 1)
    def _():
        cross = columns_to_rows([jnp.sum(acc[...], axis=1, keepdims=True)])[0:1]
        cross_ref[...] = jnp.broadcast_to(cross, (8, 128))


def leave(pipe, inv, back, known, fwd_in, saved_in, saved_conv, grad_out, mix_params):
    rows, width = fwd_in.shape[1:]
    wide = 512
    spec, params = lane_spec(rows, wide), lane_spec(7, wide)
    return pl.pallas_call(
        leave_kernel,
        out_shape=(
            jax.ShapeDtypeStruct(fwd_in.shape, jnp.bfloat16),
            jax.ShapeDtypeStruct(fwd_in.shape, jnp.bfloat16),
            jax.ShapeDtypeStruct(fwd_in.shape, jnp.float32),
            jax.ShapeDtypeStruct(mix_params.shape, jnp.float32),
            jax.ShapeDtypeStruct((8, 128), jnp.float32),
        ),
        grid_spec=pltpu.PrefetchScalarGridSpec(
            num_scalar_prefetch=1,
            grid=(width // wide,),
            in_specs=[VMEM, VMEM, pl.BlockSpec((2, wide), lambda step, *_: (0, step))]
            + [spec] * 4
            + [params],
            out_specs=(spec, spec, spec, params, whole((8, 128))),
            scratch_shapes=[pltpu.VMEM((rows, 128), jnp.float32)] * 2,
        ),
        name="leave",
        compiler_params=pltpu.CompilerParams(vmem_limit_bytes=24 << 20),
    )(pipe, inv, in_vmem(back), known, fwd_in, saved_in, saved_conv, grad_out, mix_params)


def subtract_kernel(scale_ref, value_ref, saved_ref, out_ref, scale):
    @pl.when(pl.program_id(0) == 0)
    def _():
        scale[...] = rows_to_columns(scale_ref[...])

    factor = scale[:, 0:1]
    for at in range(0, out_ref.shape[2], LANES):
        at = pl.ds(at, LANES)
        value = value_ref[0, :, at].astype(jnp.float32)
        saved = saved_ref[0, :, at].astype(jnp.float32)
        out_ref[0, :, at] = (value - saved * factor).astype(jnp.bfloat16)


def subtract(scale_rows, value, saved, resident):
    rows, width = saved.shape[1:]
    wide = width if resident else 1024
    spec = lane_spec(rows, wide)
    if resident:
        value, saved = in_vmem(value), in_vmem(saved)
    return pl.pallas_call(
        subtract_kernel,
        out_shape=jax.ShapeDtypeStruct(saved.shape, jnp.bfloat16),
        grid=(width // wide,),
        in_specs=[VMEM] + [VMEM if resident else spec] * 2,
        out_specs=spec,
        scratch_shapes=[pltpu.VMEM((rows, 128), jnp.float32)],
        compiler_params=pltpu.CompilerParams(vmem_limit_bytes=16 << 20),
    )(scale_rows, value, saved)


def per_device(tables, fwd_in, saved_in, saved_conv, grad_out, filters, mix_params, span_order):
    where = lax.axis_index("seq").astype(jnp.int32).reshape(1)
    pipe = lax.axis_index("pipe").astype(jnp.int32).reshape(1)
    raw, sums = pack(fwd_in, saved_in, grad_out)
    raw = lax.all_to_all(raw, "seq", 0, 0)
    sums = sum(over_chan(sums))[:2]
    sums = jnp.concatenate([sums, across(sums, 1)], axis=0)
    sums = jnp.concatenate([sums] + [round_ring(sums, apart) for apart in (1, 2, 3)], axis=0)
    inv = lax.rsqrt(jnp.concatenate([sums, across(sums, 8)], axis=0) / D + EPSILON)
    spectra = filter_spectra(where, filters, tables)
    peer_saved = lax.ppermute(saved_in, "pipe", [(1, 0)])
    back = convolve(where, span_order, gather_order(), raw, inv, mix_params, spectra, tables)
    back = lax.all_to_all(back, "seq", 0, 0)
    known = early(where, inv, saved_in, saved_conv, grad_out)
    for flip in (1, 2, 4, 8):
        known = known + across(known, flip)
    layer_out, outgoing, partial, param_grad, cross = leave(
        pipe, inv, back, known, fwd_in, saved_in, saved_conv, grad_out, mix_params
    )
    incoming = lax.ppermute(outgoing, "pipe", [(0, 1), (1, 0)])
    crosses = over_chan(cross)
    scale = sum(crosses) * (inv[1:2] * inv[1:2] / D)
    peer_scale = lax.ppermute(scale, "pipe", [(1, 0)])
    input_grad = subtract(scale, partial, saved_in, False)
    received = subtract(peer_scale, incoming, peer_saved, True)
    return (layer_out, input_grad, param_grad, received)


def solution(mesh):
    tables = transform_tables()
    in_specs = (
        P("pipe", "seq", "chan"),
        P("pipe", "seq", "chan"),
        P("pipe", "seq", "chan"),
        P("pipe", "seq", "chan"),
        P("pipe", None, "chan"),
        P("pipe", None, "chan"),
        P(),
    )
    out_specs = (
        P("pipe", "seq", "chan"),
        P("pipe", "seq", "chan"),
        P("pipe", None, "chan"),
        P("pipe", "seq", "chan"),
    )
    return jax.shard_map(
        functools.partial(per_device, tuple(jnp.asarray(table) for table in tables)),
        mesh=mesh,
        in_specs=in_specs,
        out_specs=out_specs,
        check_vma=False,
    )
```

```python
import functools

import jax
import jax.numpy as jnp
import ml_dtypes
import numpy as np
from jax import lax
from jax.experimental import pallas as pl
from jax.experimental.pallas import tpu as pltpu
from jax.sharding import PartitionSpec as P


D = 8192
EPSILON = 1e-05
BLOCK = 256
LANES = 128


def split_bf16(table):
    high = table.astype(np.float32).astype(ml_dtypes.bfloat16)
    low = (table - high.astype(np.float64)).astype(np.float32).astype(ml_dtypes.bfloat16)
    return high, low


def transform_tables():
    period = 2 * BLOCK
    freq = np.arange(BLOCK)[:, None]
    time = np.arange(BLOCK)[None, :]
    angle = 2.0 * np.pi / period * (freq * time % period)
    real, imag = np.cos(angle), -np.sin(angle)
    imag[0] = np.where(np.arange(BLOCK) % 2 == 0, 1.0, -1.0)
    enter = np.concatenate([real, imag], axis=0)
    angle = 2.0 * np.pi / period * (freq * (time + BLOCK) % period)
    real, imag = 2.0 * np.cos(angle), -2.0 * np.sin(angle)
    real[0] = 1.0
    imag[0] = np.where(np.arange(BLOCK) % 2 == 0, 1.0, -1.0)
    leave = np.concatenate([real, imag], axis=0).T / period
    return split_bf16(enter) + split_bf16(leave)


def rows_to_columns(rows):
    return jnp.concatenate([rows] * 16, axis=0).T


def columns_to_rows(columns):
    lane = lax.broadcasted_iota(jnp.int32, (128, 128), 1)
    square = jnp.zeros((128, 128), jnp.float32)
    for index, column in enumerate(columns):
        square = jnp.where(lane == index, column, square)
    return square.T[:8]


VMEM = pl.BlockSpec(memory_space=pltpu.VMEM)
SMEM = pl.BlockSpec(memory_space=pltpu.SMEM)


def in_vmem(array):
    return pltpu.with_memory_space_constraint(array, pltpu.VMEM)


HBM = pl.BlockSpec(memory_space=pl.ANY)


def in_hbm(array):
    return pltpu.with_memory_space_constraint(array, pltpu.HBM)


def lane_spec(rows, wide):
    return pl.BlockSpec((1, rows, wide), lambda step, *_: (0, 0, step))


def whole(shape):
    return pl.BlockSpec(shape, lambda step, *_: (0,) * len(shape))


def pack_kernel(fwd_hbm, saved_hbm, cot_hbm, out_hbm, squares_ref, held, in_sem, out_sem):
    rows, width = held.shape[1:]
    steps = in_sem.shape[1]
    wide = width // steps
    sources = (fwd_hbm, saved_hbm, cot_hbm)
    arriving = [
        [
            pltpu.make_async_copy(
                source.at[0, :, pl.ds(step * wide, wide)],
                held.at[index, :, pl.ds(step * wide, wide)],
                in_sem.at[index, step],
            )
            for index, source in enumerate(sources)
        ]
        for step in range(steps)
    ]
    for copies in arriving:
        for copy in copies:
            copy.start()
    leaving = []
    totals = [jnp.zeros((rows, LANES), jnp.float32)] * 2
    for step, copies in enumerate(arriving):
        for index, copy in enumerate(copies):
            copy.wait()
            for group in range(step * wide // LANES, (step + 1) * wide // LANES):
                out = pltpu.make_async_copy(
                    held.at[index, :, pl.ds(group * LANES, LANES)],
                    out_hbm.at[group, pl.ds(index * rows, rows), :],
                    out_sem.at[index, group],
                )
                out.start()
                leaving.append(out)
        for index in range(2):
            for group in range(step * wide // LANES, (step + 1) * wide // LANES):
                value = held[index, :, group * LANES : (group + 1) * LANES].astype(jnp.float32)
                totals[index] = totals[index] + value * value
    squares_ref[...] = columns_to_rows([jnp.sum(total, axis=1, keepdims=True) for total in totals])
    for copy in leaving:
        copy.wait()


def pack(fwd_in, saved_in, grad_out):
    rows, width = fwd_in.shape[1:]
    return pl.pallas_call(
        pack_kernel,
        out_shape=(
            pltpu.HBM((width // LANES, 3 * rows, LANES), jnp.bfloat16),
            jax.ShapeDtypeStruct((8, 128), jnp.float32),
        ),
        in_specs=[HBM] * 3,
        out_specs=(HBM, VMEM),
        scratch_shapes=[
            pltpu.VMEM((3, rows, width), jnp.bfloat16),
            pltpu.SemaphoreType.DMA((3, 4)),
            pltpu.SemaphoreType.DMA((3, width // LANES)),
        ],
        name="pack",
        compiler_params=pltpu.CompilerParams(vmem_limit_bytes=16 << 20),
    )(in_hbm(fwd_in), in_hbm(saved_in), in_hbm(grad_out))


def over_chan(rows):
    count = lax.axis_size("chan")
    got = [rows]
    for apart in range(1, count):
        got.append(
            lax.ppermute(rows, "chan", [(low, (low + apart) % count) for low in range(count)])
        )
    return got


def across(rows, flip):
    count = lax.axis_size("seq")
    return lax.ppermute(rows, "seq", [(low, low ^ flip) for low in range(count)])


def round_ring(rows, apart):
    count = lax.axis_size("seq")
    place = lambda low: low // 8 * 8 + (low + 2 * apart) % 8
    return lax.ppermute(rows, "seq", [(low, place(low)) for low in range(count)])


def gather_order():
    own = lax.axis_index("seq").astype(jnp.int32)
    block = jnp.arange(16, dtype=jnp.int32)
    core = (block ^ own) & 1
    back = (own // 2 - block // 2) % 4
    side = (block // 8) ^ (own // 8)
    return side * 8 + back * 2 + core


def early_kernel(sums_ref, saved_ref, sconv_ref, cot_ref, out_ref, inv):
    step = pl.program_id(0)

    @pl.when(step == 0)
    def _():
        inv[...] = rows_to_columns(lax.rsqrt(sums_ref[...] / D + EPSILON))

    inv_saved = inv[:, 1:2]
    pairs = saved_ref.shape[2] // (2 * LANES)
    half = out_ref.shape[0] // 2
    for pair in range(pairs):
        at = pl.ds(pair * 2 * LANES, 2 * LANES)
        normed = saved_ref[0, :, at].astype(jnp.float32) * inv_saved
        grad_query = cot_ref[0, :, at].astype(jnp.float32) * sconv_ref[0, :, at].astype(jnp.float32)
        row = step * pairs + pair
        out_ref[pl.ds(row, 1), :] = jnp.sum(grad_query, axis=0, keepdims=True)
        out_ref[pl.ds(row + half, 1), :] = jnp.sum(grad_query * normed, axis=0, keepdims=True)


def early(sums, saved_in, saved_conv, grad_out):
    rows, width = saved_in.shape[1:]
    wide = 512
    return pl.pallas_call(
        early_kernel,
        out_shape=jax.ShapeDtypeStruct((width // LANES, 2 * LANES), jnp.float32),
        grid=(width // wide,),
        in_specs=[VMEM] + [lane_spec(rows, wide)] * 3,
        out_specs=whole((width // LANES, 2 * LANES)),
        scratch_shapes=[pltpu.VMEM((rows, 128), jnp.float32)],
        name="early",
        compiler_params=pltpu.CompilerParams(vmem_limit_bytes=12 << 20),
    )(sums, in_hbm(saved_in), in_hbm(saved_conv), in_hbm(grad_out))


def side_by_side(ref, index):
    at = 2 * index * BLOCK
    return jnp.concatenate([ref[at : at + BLOCK, :], ref[at + BLOCK : at + 2 * BLOCK, :]], axis=1)


def enter_transform(enter_hi, enter_lo, data):
    return jnp.dot(enter_hi[...], data, preferred_element_type=jnp.float32) + jnp.dot(
        enter_lo[...], data, preferred_element_type=jnp.float32
    )


def filter_kernel(where_ref, taps_ref, enter_hi, enter_lo, filt):
    del where_ref
    freq = lax.broadcasted_iota(jnp.int32, (2 * BLOCK, LANES), 0)
    parity = jnp.where(freq % 2 == 0, 1.0, -1.0)
    first = lax.broadcasted_iota(jnp.int32, (BLOCK, LANES), 0) == 0
    earlier = None
    for pair in range(filt.shape[0] // 2):
        pair_spectra = enter_transform(enter_hi, enter_lo, side_by_side(taps_ref.at[0], pair))
        for side in range(2):
            current = pair_spectra[:, side * LANES : (side + 1) * LANES]
            both = parity * current
            if earlier is not None:
                both = both + earlier
            earlier = current
            real, imag = both[:BLOCK], both[BLOCK:]
            index = 2 * pair + side
            filt[index, 0] = real
            filt[index, 1] = jnp.where(first, 0.0, imag)
            filt[index, 2] = jnp.where(first, imag, real)


def filter_spectra(where, filters, tables):
    length = filters.shape[1]
    shape = (length // BLOCK, 3, BLOCK, LANES)
    return pl.pallas_call(
        filter_kernel,
        out_shape=pltpu.VMEM(shape, jnp.float32),
        grid_spec=pltpu.PrefetchScalarGridSpec(
            num_scalar_prefetch=1,
            grid=(1,),
            in_specs=[pl.BlockSpec((1, length, LANES), lambda step, at: (0, 0, at[0]))]
            + [whole(table.shape) for table in tables[:2]],
            out_specs=VMEM,
        ),
        name="filter_spectra",
        compiler_params=pltpu.CompilerParams(vmem_limit_bytes=16 << 20),
    )(where, in_hbm(filters), *[in_hbm(table) for table in tables[:2]])


def fold(block):
    return jnp.sum(block.reshape(block.shape[0] // 8, 8, LANES), axis=0)


def conv_kernel(
    where_ref, order_ref, gathered_ref, inv_ref, known_ref, params_ref, filt, raw_hbm, enter_hi_hbm,
    enter_lo_hbm, leave_hi_hbm, leave_lo_hbm, out_hbm, raw_ref, enter_hi, enter_lo, leave_hi,
    leave_lo, out_ref, ordered, spectra, product, inv_rows, inv, raw_sem, table_sem, out_sem,
):
    stored = raw_ref.shape[0]
    raw_copies = [
        pltpu.make_async_copy(raw_hbm.at[index], raw_ref.at[index], raw_sem.at[index])
        for index in range(stored)
    ]
    table_copies = [
        pltpu.make_async_copy(source, target, table_sem.at[index])
        for index, (source, target) in enumerate(
            (
                (enter_hi_hbm, enter_hi),
                (enter_lo_hbm, enter_lo),
                (leave_hi_hbm, leave_hi),
                (leave_lo_hbm, leave_lo),
            )
        )
    ]
    out_copies = [
        pltpu.make_async_copy(out_ref.at[index], out_hbm.at[index], out_sem.at[index])
        for index in range(stored)
    ]
    for copy in raw_copies + table_copies:
        copy.start()
    rows = raw_ref.shape[1] // 3
    blocks = stored * rows // BLOCK
    lanes = pl.ds(pl.multiple_of(where_ref[0] * LANES, LANES), LANES)
    p = [params_ref[0, row : row + 1, lanes] for row in range(7)]

    for index in range(stored):
        inv_rows[2 * index : 2 * index + 2, :] = inv_ref[pl.ds(2 * gathered_ref[index], 2), :]
    inv[...] = jnp.concatenate([inv_rows[...]] * (128 // (2 * stored)), axis=0).T
    for index in range(stored):
        raw_copies[index].wait()
        at = pl.multiple_of(order_ref[index] * rows, rows)
        inv_fwd = inv[:, 2 * index : 2 * index + 1]
        inv_saved = inv[:, 2 * index + 1 : 2 * index + 2]
        scaled = raw_ref[index, :rows, :].astype(jnp.float32) * inv_fwd * p[0]
        mixed = (scaled * p[3] + p[4]) * (scaled * p[5] + p[6])
        scaled = raw_ref[index, rows : 2 * rows, :].astype(jnp.float32) * inv_saved * p[0]
        cot = raw_ref[index, 2 * rows :, :].astype(jnp.float32)
        ordered[pl.ds(at, rows), :LANES] = mixed.astype(jnp.bfloat16)
        ordered[pl.ds(at, rows), LANES:] = (cot * (scaled * p[1] + p[2])).astype(jnp.bfloat16)

    table_copies[0].wait()
    table_copies[1].wait()
    for index in range(blocks):
        data = ordered[index * BLOCK : (index + 1) * BLOCK, :]
        spectra[index] = enter_transform(enter_hi, enter_lo, data)

    def products(tile, carry):
        low = pl.ds(pl.multiple_of(tile * 8, 8), 8)
        high = pl.ds(pl.multiple_of(BLOCK + tile * 8, 8), 8)
        f_re = [filt[d, 0, low, :] for d in range(blocks)]
        f_im = [filt[d, 1, low, :] for d in range(blocks)]
        f_nq = [filt[d, 2, low, :] for d in range(blocks)]
        for adjoint in (False, True):
            lanes = slice(LANES, 2 * LANES) if adjoint else slice(0, LANES)
            x_re = [spectra[j, low, lanes] for j in range(blocks)]
            x_im = [spectra[j, high, lanes] for j in range(blocks)]
            for i in range(blocks):
                re = im = None
                for j in range(i, blocks) if adjoint else range(i + 1):
                    d = abs(i - j)
                    a, b = f_re[d] * x_re[j], f_im[d] * x_im[j]
                    c, e = f_nq[d] * x_im[j], f_im[d] * x_re[j]
                    one = a + b if adjoint else a - b
                    two = c - e if adjoint else c + e
                    re = one if re is None else re + one
                    im = two if im is None else im + two
                product[i, low, lanes] = re
                product[i, high, lanes] = im
        return carry

    lax.fori_loop(0, BLOCK // 8, products, 0)

    table_copies[2].wait()
    table_copies[3].wait()
    for index in range(blocks):
        value = product[index]
        top = value.astype(jnp.bfloat16)
        rest = (value - top.astype(jnp.float32)).astype(jnp.bfloat16)
        left = (
            jnp.dot(leave_hi[...], top, preferred_element_type=jnp.float32)
            + jnp.dot(leave_lo[...], top, preferred_element_type=jnp.float32)
            + jnp.dot(leave_hi[...], rest, preferred_element_type=jnp.float32)
        )
        ordered[index * BLOCK : (index + 1) * BLOCK, :] = left.astype(jnp.bfloat16)

    sums = [jnp.zeros((8, LANES), jnp.float32)] * 3
    for index in range(stored):
        at = pl.multiple_of(order_ref[index] * rows, rows)
        block = ordered[pl.ds(at, rows), :]
        out_ref[index, :rows, :] = block
        grad_mixed = block[:, LANES:].astype(jnp.float32)
        inv_saved = inv[:, 2 * index + 1 : 2 * index + 2]
        normed = raw_ref[index, rows : 2 * rows, :].astype(jnp.float32) * inv_saved
        once = grad_mixed * normed
        for power, term in enumerate((grad_mixed, once, once * normed)):
            sums[power] = sums[power] + fold(term)

    sums = jnp.concatenate(
        [jnp.sum(total, axis=0, keepdims=True) for total in sums]
        + [jnp.zeros((5, LANES), jnp.float32)],
        axis=0,
    )
    known = known_ref[...].astype(jnp.bfloat16)
    top = sums.astype(jnp.bfloat16)
    rest = (sums - top.astype(jnp.float32)).astype(jnp.bfloat16)
    for index in range(stored):
        out_ref[index, rows : rows + 16, :] = known
        out_ref[index, rows + 16 :, :LANES] = top
        out_ref[index, rows + 16 :, LANES:] = rest
        out_copies[index].start()
    for copy in out_copies:
        copy.wait()


def convolve(where, order, gathered, raw, inv, known, params, spectra, tables):
    stored = raw.shape[0]
    rows = raw.shape[1] // 3
    length = stored * rows
    blocks = length // BLOCK
    return pl.pallas_call(
        conv_kernel,
        out_shape=pltpu.HBM((stored, rows + 24, 2 * LANES), jnp.bfloat16),
        in_specs=[SMEM] * 3 + [VMEM] * 4 + [HBM] * 5,
        out_specs=HBM,
        scratch_shapes=[
            pltpu.VMEM(raw.shape, jnp.bfloat16),
            *[pltpu.VMEM(table.shape, jnp.bfloat16) for table in tables],
            pltpu.VMEM((stored, rows + 24, 2 * LANES), jnp.bfloat16),
            pltpu.VMEM((length, 2 * LANES), jnp.bfloat16),
            pltpu.VMEM((blocks, 2 * BLOCK, 2 * LANES), jnp.float32),
            pltpu.VMEM((blocks, 2 * BLOCK, 2 * LANES), jnp.float32),
            pltpu.VMEM((2 * stored, 128), jnp.float32),
            pltpu.VMEM((128, 128), jnp.float32),
            pltpu.SemaphoreType.DMA((stored,)),
            pltpu.SemaphoreType.DMA((4,)),
            pltpu.SemaphoreType.DMA((stored,)),
        ],
        name="convolve",
        compiler_params=pltpu.CompilerParams(vmem_limit_bytes=28 << 20),
    )(
        where, order, gathered, inv, known, params, in_vmem(spectra), in_hbm(raw),
        *[in_hbm(table) for table in tables],
    )


def leave_kernel(
    pipe_ref, inv_ref, back_ref, fwd_ref, saved_ref, sconv_ref, cot_ref, params_ref,
    layer_ref, send_ref, partial_ref, grads_ref, cross_ref, inv, acc, known,
):
    step = pl.program_id(0)
    rows = fwd_ref.shape[1]

    @pl.when(step == 0)
    def _():
        inv[...] = rows_to_columns(inv_ref[0:8, :])
        acc[...] = jnp.zeros_like(acc)
        total = back_ref[0, rows : rows + 16, :].astype(jnp.float32)
        for index in range(1, back_ref.shape[0]):
            total = total + back_ref[index, rows : rows + 16, :].astype(jnp.float32)
        for row in range(16):
            known[row] = total[row : row + 1, :]

    inv_fwd = inv[:, 0:1]
    inv_saved = inv[:, 1:2]
    first = pipe_ref[0] == 0
    cross = acc[...]
    groups = fwd_ref.shape[2] // LANES
    for group in range(groups):
        at = pl.ds(group * LANES, LANES)
        p = [params_ref[0, row : row + 1, at] for row in range(7)]
        inputs = fwd_ref[0, :, at].astype(jnp.float32)
        query = inputs * inv_fwd * p[0] * p[1] + p[2]
        conv = back_ref[step * groups + group, :rows, :LANES].astype(jnp.float32)
        layer = inputs + query * conv
        layer_ref[0, :, at] = layer.astype(jnp.bfloat16)

        grad_mixed = back_ref[step * groups + group, :rows, LANES:].astype(jnp.float32)
        cot = cot_ref[0, :, at].astype(jnp.float32)
        normed = saved_ref[0, :, at].astype(jnp.float32) * inv_saved
        scaled = normed * p[0]
        grad_query = cot * sconv_ref[0, :, at].astype(jnp.float32)
        mixed_grad = (scaled * p[5] + p[6]) * p[3] + (scaled * p[3] + p[4]) * p[5]
        grad_normed = (grad_query * p[1] + grad_mixed * mixed_grad) * p[0]
        cross = cross + grad_normed * normed
        partial = cot + inv_saved * grad_normed
        partial_ref[0, :, at] = partial
        send_ref[0, :, at] = jnp.where(first, layer, partial).astype(jnp.bfloat16)

        extra = back_ref[step * groups + group, rows + 16 :, :].astype(jnp.float32)
        extra = extra[:, :LANES] + extra[:, LANES:]
        m0, m1, m2 = extra[0:1], extra[1:2], extra[2:3]
        row = step * (groups // 2) + group // 2
        side = slice(group % 2 * LANES, (group % 2 + 1) * LANES)
        q0, q1 = known[row, :, side], known[row + 8, :, side]
        key_normed = p[0] * p[5] * m2 + p[6] * m1
        value_normed = p[0] * p[3] * m2 + p[4] * m1
        grads = [
            p[1] * q1 + p[3] * key_normed + p[5] * value_normed,
            p[0] * q1,
            q0,
            p[0] * key_normed,
            p[0] * p[5] * m1 + p[6] * m0,
            p[0] * value_normed,
            p[0] * p[3] * m1 + p[4] * m0,
        ]
        grads_ref[0, :, at] = jnp.concatenate(grads, axis=0)
    acc[...] = cross

    @pl.when(step == pl.num_programs(0) - 1)
    def _():
        cross = columns_to_rows([jnp.sum(acc[...], axis=1, keepdims=True)])
        cross_ref[...] = cross * (inv_ref[1:2, :] * inv_ref[1:2, :] / D)


def leave(pipe, inv, back, fwd_in, saved_in, saved_conv, grad_out, mix_params):
    rows, width = fwd_in.shape[1:]
    wide = 512
    spec, params = lane_spec(rows, wide), lane_spec(7, wide)
    return pl.pallas_call(
        leave_kernel,
        out_shape=(
            jax.ShapeDtypeStruct(fwd_in.shape, jnp.bfloat16),
            jax.ShapeDtypeStruct(fwd_in.shape, jnp.bfloat16),
            jax.ShapeDtypeStruct(fwd_in.shape, jnp.float32),
            jax.ShapeDtypeStruct(mix_params.shape, jnp.float32),
            jax.ShapeDtypeStruct((8, 128), jnp.float32),
        ),
        grid_spec=pltpu.PrefetchScalarGridSpec(
            num_scalar_prefetch=1,
            grid=(width // wide,),
            in_specs=[VMEM, VMEM]
            + [spec] * 4
            + [params],
            out_specs=(spec, spec, spec, params, whole((8, 128))),
            scratch_shapes=[pltpu.VMEM((rows, 128), jnp.float32)] * 2
            + [pltpu.VMEM((16, 1, 2 * LANES), jnp.float32)],
        ),
        name="leave",
        compiler_params=pltpu.CompilerParams(vmem_limit_bytes=24 << 20),
    )(pipe, inv, in_vmem(back), fwd_in, saved_in, saved_conv, grad_out, mix_params)


def subtract_kernel(row, s0, s1, s2, s3, value_ref, saved_ref, out_ref, scale):
    step = pl.program_id(0)

    @pl.when(step == 0)
    def _():
        scale[...] = rows_to_columns(s0[...] + s1[...] + s2[...] + s3[...])

    factor = scale[:, row : row + 1]
    wide = out_ref.shape[2]
    for at in range(0, wide, LANES):
        source = pl.ds(at, LANES)
        if value_ref.shape[2] != wide:
            source = pl.ds(pl.multiple_of(step * wide + at, LANES), LANES)
        value = value_ref[0, :, source].astype(jnp.float32)
        saved = saved_ref[0, :, source].astype(jnp.float32)
        out_ref[0, :, pl.ds(at, LANES)] = (value - saved * factor).astype(jnp.bfloat16)


def subtract(row, scales, value, saved, resident):
    rows, width = saved.shape[1:]
    wide = 512
    spec = lane_spec(rows, wide)
    if resident:
        value, saved = in_vmem(value), in_vmem(saved)
    return pl.pallas_call(
        functools.partial(subtract_kernel, row),
        out_shape=jax.ShapeDtypeStruct(saved.shape, jnp.bfloat16),
        grid=(width // wide,),
        in_specs=[VMEM] * 4 + [VMEM if resident else spec] * 2,
        out_specs=spec,
        scratch_shapes=[pltpu.VMEM((rows, 128), jnp.float32)],
        compiler_params=pltpu.CompilerParams(vmem_limit_bytes=16 << 20),
    )(*scales, value, saved)


def per_device(tables, fwd_in, saved_in, saved_conv, grad_out, filters, mix_params, span_order):
    where = lax.axis_index("seq").astype(jnp.int32).reshape(1)
    pipe = lax.axis_index("pipe").astype(jnp.int32).reshape(1)
    peer_saved = lax.ppermute(saved_in, "pipe", [(1, 0)])
    raw, sums = pack(fwd_in, saved_in, grad_out)
    raw = lax.all_to_all(raw, "seq", 0, 0)
    own_sums = sum(over_chan(sums))
    sums = own_sums[:2]
    sums = jnp.concatenate([sums, across(sums, 1)], axis=0)
    sums = jnp.concatenate([sums] + [round_ring(sums, apart) for apart in (1, 2, 3)], axis=0)
    inv = lax.rsqrt(jnp.concatenate([sums, across(sums, 8)], axis=0) / D + EPSILON)
    spectra = filter_spectra(where, filters, tables)
    known = early(own_sums, saved_in, saved_conv, grad_out)
    back = convolve(where, span_order, gather_order(), raw, inv, known, mix_params, spectra, tables)
    back = lax.all_to_all(back, "seq", 0, 0)
    layer_out, outgoing, partial, param_grad, cross = leave(
        pipe, inv, back, fwd_in, saved_in, saved_conv, grad_out, mix_params
    )
    peer_cross = lax.ppermute(cross, "pipe", [(1, 0)])
    incoming = lax.ppermute(outgoing, "pipe", [(0, 1), (1, 0)])
    scales = over_chan(jnp.concatenate([cross[:1], peer_cross[:1], cross[:6]], axis=0))
    input_grad = subtract(0, scales, partial, saved_in, False)
    received = subtract(1, scales, incoming, peer_saved, True)
    return (layer_out, input_grad, param_grad, received)


def solution(mesh):
    tables = transform_tables()
    in_specs = (
        P("pipe", "seq", "chan"),
        P("pipe", "seq", "chan"),
        P("pipe", "seq", "chan"),
        P("pipe", "seq", "chan"),
        P("pipe", None, "chan"),
        P("pipe", None, "chan"),
        P(),
    )
    out_specs = (
        P("pipe", "seq", "chan"),
        P("pipe", "seq", "chan"),
        P("pipe", None, "chan"),
        P("pipe", "seq", "chan"),
    )
    return jax.shard_map(
        functools.partial(per_device, tuple(jnp.asarray(table) for table in tables)),
        mesh=mesh,
        in_specs=in_specs,
        out_specs=out_specs,
        check_vma=False,
    )
```

```python
import functools

import jax
import jax.numpy as jnp
import ml_dtypes
import numpy as np
from jax import lax
from jax.experimental import pallas as pl
from jax.experimental.pallas import tpu as pltpu
from jax.sharding import PartitionSpec as P


D = 8192
EPSILON = 1e-05
BLOCK = 256
LANES = 128


def split_bf16(table):
    high = table.astype(np.float32).astype(ml_dtypes.bfloat16)
    low = (table - high.astype(np.float64)).astype(np.float32).astype(ml_dtypes.bfloat16)
    return high, low


def transform_tables():
    period = 2 * BLOCK
    freq = np.arange(BLOCK)[:, None]
    time = np.arange(BLOCK)[None, :]
    angle = 2.0 * np.pi / period * (freq * time % period)
    real, imag = np.cos(angle), -np.sin(angle)
    imag[0] = np.where(np.arange(BLOCK) % 2 == 0, 1.0, -1.0)
    enter = np.concatenate([real, imag], axis=0)
    angle = 2.0 * np.pi / period * (freq * (time + BLOCK) % period)
    real, imag = 2.0 * np.cos(angle), -2.0 * np.sin(angle)
    real[0] = 1.0
    imag[0] = np.where(np.arange(BLOCK) % 2 == 0, 1.0, -1.0)
    leave = np.concatenate([real, imag], axis=0).T / period
    return tuple(np.concatenate(split_bf16(table), axis=1) for table in (enter, leave))


def rows_to_columns(rows):
    return jnp.concatenate([rows] * 16, axis=0).T


def columns_to_rows(columns):
    lane = lax.broadcasted_iota(jnp.int32, (128, 128), 1)
    square = jnp.zeros((128, 128), jnp.float32)
    for index, column in enumerate(columns):
        square = jnp.where(lane == index, column, square)
    return square.T[:8]


VMEM = pl.BlockSpec(memory_space=pltpu.VMEM)
SMEM = pl.BlockSpec(memory_space=pltpu.SMEM)


def in_vmem(array):
    return pltpu.with_memory_space_constraint(array, pltpu.VMEM)


HBM = pl.BlockSpec(memory_space=pl.ANY)


def in_hbm(array):
    return pltpu.with_memory_space_constraint(array, pltpu.HBM)


def lane_spec(rows, wide):
    return pl.BlockSpec((1, rows, wide), lambda step, *_: (0, 0, step))


def whole(shape):
    return pl.BlockSpec(shape, lambda step, *_: (0,) * len(shape))


def pack_kernel(fwd_hbm, saved_hbm, cot_hbm, out_hbm, squares_ref, held, in_sem, out_sem):
    rows, width = held.shape[1:]
    steps = in_sem.shape[1]
    wide = width // steps
    sources = (fwd_hbm, saved_hbm, cot_hbm)
    arriving = [
        [
            pltpu.make_async_copy(
                source.at[0, :, pl.ds(step * wide, wide)],
                held.at[index, :, pl.ds(step * wide, wide)],
                in_sem.at[index, step],
            )
            for index, source in enumerate(sources)
        ]
        for step in range(steps)
    ]
    for copies in arriving:
        for copy in copies:
            copy.start()
    leaving = []
    totals = [jnp.zeros((rows, LANES), jnp.float32)] * 2
    for step, copies in enumerate(arriving):
        for index, copy in enumerate(copies):
            copy.wait()
            for group in range(step * wide // LANES, (step + 1) * wide // LANES):
                out = pltpu.make_async_copy(
                    held.at[index, :, pl.ds(group * LANES, LANES)],
                    out_hbm.at[group, pl.ds(index * rows, rows), :],
                    out_sem.at[index, group],
                )
                out.start()
                leaving.append(out)
        for index in range(2):
            for group in range(step * wide // LANES, (step + 1) * wide // LANES):
                value = held[index, :, group * LANES : (group + 1) * LANES].astype(jnp.float32)
                totals[index] = totals[index] + value * value
    squares_ref[...] = columns_to_rows([jnp.sum(total, axis=1, keepdims=True) for total in totals])
    for copy in leaving:
        copy.wait()


def pack(fwd_in, saved_in, grad_out):
    rows, width = fwd_in.shape[1:]
    return pl.pallas_call(
        pack_kernel,
        out_shape=(
            pltpu.HBM((width // LANES, 3 * rows, LANES), jnp.bfloat16),
            jax.ShapeDtypeStruct((8, 128), jnp.float32),
        ),
        in_specs=[HBM] * 3,
        out_specs=(HBM, VMEM),
        scratch_shapes=[
            pltpu.VMEM((3, rows, width), jnp.bfloat16),
            pltpu.SemaphoreType.DMA((3, 4)),
            pltpu.SemaphoreType.DMA((3, width // LANES)),
        ],
        name="pack",
        compiler_params=pltpu.CompilerParams(vmem_limit_bytes=16 << 20),
    )(in_hbm(fwd_in), in_hbm(saved_in), in_hbm(grad_out))


def across(rows, axis, flip):
    count = lax.axis_size(axis)
    return lax.ppermute(rows, axis, [(low, low ^ flip) for low in range(count)])


def early_kernel(sums_ref, saved_ref, sconv_ref, cot_ref, out_ref, inv):
    step = pl.program_id(0)

    @pl.when(step == 0)
    def _():
        inv[...] = rows_to_columns(lax.rsqrt(sums_ref[...] / D + EPSILON))

    inv_saved = inv[:, 1:2]
    pairs = saved_ref.shape[2] // (2 * LANES)
    half = out_ref.shape[0] // 2
    for pair in range(pairs):
        at = pl.ds(pair * 2 * LANES, 2 * LANES)
        normed = saved_ref[0, :, at].astype(jnp.float32) * inv_saved
        grad_query = cot_ref[0, :, at].astype(jnp.float32) * sconv_ref[0, :, at].astype(jnp.float32)
        row = step * pairs + pair
        out_ref[pl.ds(row, 1), :] = jnp.sum(grad_query, axis=0, keepdims=True)
        out_ref[pl.ds(row + half, 1), :] = jnp.sum(grad_query * normed, axis=0, keepdims=True)


def early(sums, saved_in, saved_conv, grad_out):
    rows, width = saved_in.shape[1:]
    wide = 512
    return pl.pallas_call(
        early_kernel,
        out_shape=jax.ShapeDtypeStruct((width // LANES, 2 * LANES), jnp.float32),
        grid=(width // wide,),
        in_specs=[VMEM] + [lane_spec(rows, wide)] * 3,
        out_specs=whole((width // LANES, 2 * LANES)),
        scratch_shapes=[pltpu.VMEM((rows, 128), jnp.float32)],
        name="early",
        compiler_params=pltpu.CompilerParams(vmem_limit_bytes=12 << 20),
    )(sums, in_hbm(saved_in), in_hbm(saved_conv), in_hbm(grad_out))


def side_by_side(ref, index):
    at = 2 * index * BLOCK
    return jnp.concatenate([ref[at : at + BLOCK, :], ref[at + BLOCK : at + 2 * BLOCK, :]], axis=1)


def table_dot(table, data):
    return jnp.dot(
        table[...], jnp.concatenate([data, data], axis=0), preferred_element_type=jnp.float32
    )


def filter_kernel(where_ref, taps_ref, enter, filt):
    del where_ref
    freq = lax.broadcasted_iota(jnp.int32, (2 * BLOCK, LANES), 0)
    parity = jnp.where(freq % 2 == 0, 1.0, -1.0)
    first = lax.broadcasted_iota(jnp.int32, (BLOCK, LANES), 0) == 0
    earlier = None
    for pair in range(filt.shape[0] // 2):
        pair_spectra = table_dot(enter, side_by_side(taps_ref.at[0], pair))
        for side in range(2):
            current = pair_spectra[:, side * LANES : (side + 1) * LANES]
            both = parity * current
            if earlier is not None:
                both = both + earlier
            earlier = current
            real, imag = both[:BLOCK], both[BLOCK:]
            index = 2 * pair + side
            filt[index, 0] = real
            filt[index, 1] = jnp.where(first, 0.0, imag)
            filt[index, 2] = jnp.where(first, imag, real)


def filter_spectra(where, filters, tables):
    length = filters.shape[1]
    shape = (length // BLOCK, 3, BLOCK, LANES)
    return pl.pallas_call(
        filter_kernel,
        out_shape=pltpu.VMEM(shape, jnp.float32),
        grid_spec=pltpu.PrefetchScalarGridSpec(
            num_scalar_prefetch=1,
            grid=(1,),
            in_specs=[pl.BlockSpec((1, length, LANES), lambda step, at: (0, 0, at[0]))]
            + [whole(tables[0].shape)],
            out_specs=VMEM,
        ),
        name="filter_spectra",
        compiler_params=pltpu.CompilerParams(vmem_limit_bytes=16 << 20),
    )(where, in_hbm(filters), in_hbm(tables[0]))


def fold(block):
    return jnp.sum(block.reshape(block.shape[0] // 8, 8, LANES), axis=0)


def conv_kernel(
    where_ref, order_ref, gathered_ref, inv_ref, known_ref, params_ref, filt, raw_hbm, enter_hbm,
    leave_hbm, out_hbm, raw_ref, enter, leave, out_ref, ordered, spectra, product, inv_rows, inv, raw_sem, table_sem, out_sem,
):
    stored = raw_ref.shape[0]
    raw_copies = [
        pltpu.make_async_copy(raw_hbm.at[index], raw_ref.at[index], raw_sem.at[index])
        for index in range(stored)
    ]
    table_copies = [
        pltpu.make_async_copy(source, target, table_sem.at[index])
        for index, (source, target) in enumerate(((enter_hbm, enter), (leave_hbm, leave)))
    ]
    out_copies = [
        pltpu.make_async_copy(out_ref.at[index], out_hbm.at[index], out_sem.at[index])
        for index in range(stored)
    ]
    for copy in raw_copies + table_copies:
        copy.start()
    rows = raw_ref.shape[1] // 3
    blocks = stored * rows // BLOCK
    lanes = pl.ds(pl.multiple_of(where_ref[0] * LANES, LANES), LANES)
    p = [params_ref[0, row : row + 1, lanes] for row in range(7)]

    gains = [p[0] * p[1], p[0] * p[3], p[0] * p[5]]
    for index in range(stored):
        inv_rows[2 * index : 2 * index + 2, :] = inv_ref[pl.ds(2 * gathered_ref[index], 2), :]
    inv[...] = jnp.concatenate([inv_rows[...]] * (128 // (2 * stored)), axis=0).T
    for index in range(stored):
        raw_copies[index].wait()
        at = pl.multiple_of(order_ref[index] * rows, rows)
        inv_fwd = inv[:, 2 * index : 2 * index + 1]
        inv_saved = inv[:, 2 * index + 1 : 2 * index + 2]
        normed = raw_ref[index, :rows, :].astype(jnp.float32) * inv_fwd
        mixed = (normed * gains[1] + p[4]) * (normed * gains[2] + p[6])
        normed = raw_ref[index, rows : 2 * rows, :].astype(jnp.float32) * inv_saved
        cot = raw_ref[index, 2 * rows :, :].astype(jnp.float32)
        ordered[pl.ds(at, rows), :LANES] = mixed.astype(jnp.bfloat16)
        ordered[pl.ds(at, rows), LANES:] = (cot * (normed * gains[0] + p[2])).astype(jnp.bfloat16)

    table_copies[0].wait()
    for index in range(blocks):
        data = ordered[index * BLOCK : (index + 1) * BLOCK, :]
        spectra[index] = table_dot(enter, data)

    def products(tile, carry):
        low = pl.ds(pl.multiple_of(tile * 8, 8), 8)
        high = pl.ds(pl.multiple_of(BLOCK + tile * 8, 8), 8)
        f_re = [filt[d, 0, low, :] for d in range(blocks)]
        f_im = [filt[d, 1, low, :] for d in range(blocks)]
        f_nq = [filt[d, 2, low, :] for d in range(blocks)]
        for adjoint in (False, True):
            lanes = slice(LANES, 2 * LANES) if adjoint else slice(0, LANES)
            x_re = [spectra[j, low, lanes] for j in range(blocks)]
            x_im = [spectra[j, high, lanes] for j in range(blocks)]
            for i in range(blocks):
                re = im = None
                for j in range(i, blocks) if adjoint else range(i + 1):
                    d = abs(i - j)
                    a, b = f_re[d] * x_re[j], f_im[d] * x_im[j]
                    c, e = f_nq[d] * x_im[j], f_im[d] * x_re[j]
                    one = a + b if adjoint else a - b
                    two = c - e if adjoint else c + e
                    re = one if re is None else re + one
                    im = two if im is None else im + two
                product[i, low, lanes] = re
                product[i, high, lanes] = im
        return carry

    lax.fori_loop(0, BLOCK // 8, products, 0)

    table_copies[1].wait()
    for index in range(blocks):
        left = table_dot(leave, product[index].astype(jnp.bfloat16))
        ordered[index * BLOCK : (index + 1) * BLOCK, :] = left.astype(jnp.bfloat16)

    sums = [jnp.zeros((8, LANES), jnp.float32)] * 3
    for index in range(stored):
        at = pl.multiple_of(order_ref[index] * rows, rows)
        block = ordered[pl.ds(at, rows), :]
        out_ref[index, :rows, :] = block
        grad_mixed = block[:, LANES:].astype(jnp.float32)
        inv_saved = inv[:, 2 * index + 1 : 2 * index + 2]
        normed = raw_ref[index, rows : 2 * rows, :].astype(jnp.float32) * inv_saved
        once = grad_mixed * normed
        for power, term in enumerate((grad_mixed, once, once * normed)):
            sums[power] = sums[power] + fold(term)

    sums = jnp.concatenate(
        [jnp.sum(total, axis=0, keepdims=True) for total in sums]
        + [jnp.zeros((5, LANES), jnp.float32)],
        axis=0,
    )
    known = known_ref[...].astype(jnp.bfloat16)
    top = sums.astype(jnp.bfloat16)
    rest = (sums - top.astype(jnp.float32)).astype(jnp.bfloat16)
    for index in range(stored):
        out_ref[index, rows : rows + 16, :] = known
        out_ref[index, rows + 16 :, :LANES] = top
        out_ref[index, rows + 16 :, LANES:] = rest
        out_copies[index].start()
    for copy in out_copies:
        copy.wait()


def convolve(where, order, gathered, raw, inv, known, params, spectra, tables):
    stored = raw.shape[0]
    rows = raw.shape[1] // 3
    length = stored * rows
    blocks = length // BLOCK
    return pl.pallas_call(
        conv_kernel,
        out_shape=pltpu.HBM((stored, rows + 24, 2 * LANES), jnp.bfloat16),
        in_specs=[SMEM] * 3 + [VMEM] * 4 + [HBM] * 3,
        out_specs=HBM,
        scratch_shapes=[
            pltpu.VMEM(raw.shape, jnp.bfloat16),
            *[pltpu.VMEM(table.shape, jnp.bfloat16) for table in tables],
            pltpu.VMEM((stored, rows + 24, 2 * LANES), jnp.bfloat16),
            pltpu.VMEM((length, 2 * LANES), jnp.bfloat16),
            pltpu.VMEM((blocks, 2 * BLOCK, 2 * LANES), jnp.float32),
            pltpu.VMEM((blocks, 2 * BLOCK, 2 * LANES), jnp.float32),
            pltpu.VMEM((2 * stored, 128), jnp.float32),
            pltpu.VMEM((128, 128), jnp.float32),
            pltpu.SemaphoreType.DMA((stored,)),
            pltpu.SemaphoreType.DMA((2,)),
            pltpu.SemaphoreType.DMA((stored,)),
        ],
        name="convolve",
        compiler_params=pltpu.CompilerParams(vmem_limit_bytes=28 << 20),
    )(
        where, order, gathered, inv, known, params, in_vmem(spectra), in_hbm(raw),
        *[in_hbm(table) for table in tables],
    )


def leave_kernel(
    pipe_ref, inv_ref, back_ref, fwd_ref, saved_ref, sconv_ref, cot_ref, params_ref,
    layer_ref, send_ref, partial_ref, grads_ref, cross_ref, inv, acc, known,
):
    step = pl.program_id(0)
    rows = fwd_ref.shape[1]

    @pl.when(step == 0)
    def _():
        inv[...] = rows_to_columns(inv_ref[0:8, :])
        acc[...] = jnp.zeros_like(acc)
        total = back_ref[0, rows : rows + 16, :].astype(jnp.float32)
        for index in range(1, back_ref.shape[0]):
            total = total + back_ref[index, rows : rows + 16, :].astype(jnp.float32)
        for row in range(16):
            known[row] = total[row : row + 1, :]

    inv_fwd = inv[:, 0:1]
    inv_saved = inv[:, 1:2]
    first = pipe_ref[0] == 0
    cross = acc[...]
    groups = fwd_ref.shape[2] // LANES
    for group in range(groups):
        at = pl.ds(group * LANES, LANES)
        p = [params_ref[0, row : row + 1, at] for row in range(7)]
        inputs = fwd_ref[0, :, at].astype(jnp.float32)
        query = inputs * inv_fwd * p[0] * p[1] + p[2]
        conv = back_ref[step * groups + group, :rows, :LANES].astype(jnp.float32)
        layer = inputs + query * conv
        layer_ref[0, :, at] = layer.astype(jnp.bfloat16)

        grad_mixed = back_ref[step * groups + group, :rows, LANES:].astype(jnp.float32)
        cot = cot_ref[0, :, at].astype(jnp.float32)
        normed = saved_ref[0, :, at].astype(jnp.float32) * inv_saved
        scaled = normed * p[0]
        grad_query = cot * sconv_ref[0, :, at].astype(jnp.float32)
        mixed_grad = (scaled * p[5] + p[6]) * p[3] + (scaled * p[3] + p[4]) * p[5]
        grad_normed = (grad_query * p[1] + grad_mixed * mixed_grad) * p[0]
        cross = cross + grad_normed * normed
        partial = cot + inv_saved * grad_normed
        partial_ref[0, :, at] = partial
        send_ref[0, :, at] = jnp.where(first, layer, partial).astype(jnp.bfloat16)

        extra = back_ref[step * groups + group, rows + 16 :, :].astype(jnp.float32)
        extra = extra[:, :LANES] + extra[:, LANES:]
        m0, m1, m2 = extra[0:1], extra[1:2], extra[2:3]
        row = step * (groups // 2) + group // 2
        side = slice(group % 2 * LANES, (group % 2 + 1) * LANES)
        q0, q1 = known[row, :, side], known[row + 8, :, side]
        key_normed = p[0] * p[5] * m2 + p[6] * m1
        value_normed = p[0] * p[3] * m2 + p[4] * m1
        grads = [
            p[1] * q1 + p[3] * key_normed + p[5] * value_normed,
            p[0] * q1,
            q0,
            p[0] * key_normed,
            p[0] * p[5] * m1 + p[6] * m0,
            p[0] * value_normed,
            p[0] * p[3] * m1 + p[4] * m0,
        ]
        grads_ref[0, :, at] = jnp.concatenate(grads, axis=0)
    acc[...] = cross

    @pl.when(step == pl.num_programs(0) - 1)
    def _():
        cross = columns_to_rows([jnp.sum(acc[...], axis=1, keepdims=True)])
        cross = cross[0:1] * (inv_ref[1:2, :] * inv_ref[1:2, :] / D)
        cross_ref[...] = jnp.broadcast_to(cross, (8, 128))


def leave(pipe, inv, back, fwd_in, saved_in, saved_conv, grad_out, mix_params):
    rows, width = fwd_in.shape[1:]
    wide = 512
    spec, params = lane_spec(rows, wide), lane_spec(7, wide)
    return pl.pallas_call(
        leave_kernel,
        out_shape=(
            jax.ShapeDtypeStruct(fwd_in.shape, jnp.bfloat16),
            jax.ShapeDtypeStruct(fwd_in.shape, jnp.bfloat16),
            jax.ShapeDtypeStruct(fwd_in.shape, jnp.float32),
            jax.ShapeDtypeStruct(mix_params.shape, jnp.float32),
            jax.ShapeDtypeStruct((8, 128), jnp.float32),
        ),
        grid_spec=pltpu.PrefetchScalarGridSpec(
            num_scalar_prefetch=1,
            grid=(width // wide,),
            in_specs=[VMEM, VMEM]
            + [spec] * 4
            + [params],
            out_specs=(spec, spec, spec, params, whole((8, 128))),
            scratch_shapes=[pltpu.VMEM((rows, 128), jnp.float32)] * 2
            + [pltpu.VMEM((16, 1, 2 * LANES), jnp.float32)],
        ),
        name="leave",
        compiler_params=pltpu.CompilerParams(vmem_limit_bytes=24 << 20),
    )(pipe, inv, in_vmem(back), fwd_in, saved_in, saved_conv, grad_out, mix_params)


def subtract_kernel(row, first, second, value_ref, saved_ref, out_ref, scale):
    step = pl.program_id(0)

    @pl.when(step == 0)
    def _():
        scale[...] = rows_to_columns(first[...] + second[...])

    factor = scale[:, row : row + 1]
    wide = out_ref.shape[2]
    for at in range(0, wide, LANES):
        own = source = pl.ds(at, LANES)
        if value_ref.shape[2] != wide:
            source = pl.ds(pl.multiple_of(step * wide + at, LANES), LANES)
        value = value_ref[0, :, source].astype(jnp.float32)
        saved = saved_ref[0, :, own].astype(jnp.float32)
        out_ref[0, :, own] = (value - saved * factor).astype(jnp.bfloat16)


def subtract(row, scales, value, saved, resident):
    rows, width = saved.shape[1:]
    wide = 512
    spec = lane_spec(rows, wide)
    if resident:
        value, saved = in_vmem(value), in_hbm(saved)
    return pl.pallas_call(
        functools.partial(subtract_kernel, row),
        out_shape=jax.ShapeDtypeStruct(saved.shape, jnp.bfloat16),
        grid=(width // wide,),
        in_specs=[VMEM] * 2 + [VMEM if resident else spec, spec],
        out_specs=spec,
        scratch_shapes=[pltpu.VMEM((rows, 128), jnp.float32)],
        compiler_params=pltpu.CompilerParams(vmem_limit_bytes=16 << 20),
    )(*scales, value, saved)


def per_device(tables, fwd_in, saved_in, saved_conv, grad_out, filters, mix_params, span_order):
    where = lax.axis_index("seq").astype(jnp.int32).reshape(1)
    pipe = lax.axis_index("pipe").astype(jnp.int32).reshape(1)
    gathered = jnp.arange(lax.axis_size("seq"), dtype=jnp.int32) ^ where
    raw, sums = pack(fwd_in, saved_in, grad_out)
    raw = lax.all_to_all(raw, "seq", 0, 0)
    for flip in (1, 2):
        sums = sums + across(sums, "chan", flip)
    own_sums, sums = sums, sums[:2]
    for flip in (1, 2, 4):
        sums = jnp.concatenate([sums, across(sums, "seq", flip)], axis=0)
    sums = jnp.concatenate([sums, across(sums, "seq", 8)], axis=0)
    inv = lax.rsqrt(sums / D + EPSILON)
    peer_saved = lax.ppermute(saved_in, "pipe", [(1, 0)])
    known = early(own_sums, saved_in, saved_conv, grad_out)
    spectra = filter_spectra(where, filters, tables)
    back = convolve(where, span_order, gathered, raw, inv, known, mix_params, spectra, tables)
    back = lax.all_to_all(back, "seq", 0, 0)
    layer_out, outgoing, partial, param_grad, cross = leave(
        pipe, inv, back, fwd_in, saved_in, saved_conv, grad_out, mix_params
    )
    peer_cross = lax.ppermute(cross, "pipe", [(1, 0)])
    incoming = lax.ppermute(outgoing, "pipe", [(0, 1), (1, 0)])
    own_row = lax.broadcasted_iota(jnp.int32, cross.shape, 0) == 0
    scale = jnp.where(own_row, cross, peer_cross)
    scale = scale + across(scale, "chan", 1)
    scales = (scale, across(scale, "chan", 2))
    input_grad = subtract(0, scales, partial, saved_in, False)
    received = subtract(1, scales, incoming, peer_saved, True)
    return (layer_out, input_grad, param_grad, received)


def solution(mesh):
    tables = transform_tables()
    in_specs = (
        P("pipe", "seq", "chan"),
        P("pipe", "seq", "chan"),
        P("pipe", "seq", "chan"),
        P("pipe", "seq", "chan"),
        P("pipe", None, "chan"),
        P("pipe", None, "chan"),
        P(),
    )
    out_specs = (
        P("pipe", "seq", "chan"),
        P("pipe", "seq", "chan"),
        P("pipe", None, "chan"),
        P("pipe", "seq", "chan"),
    )
    return jax.shard_map(
        functools.partial(per_device, tuple(jnp.asarray(table) for table in tables)),
        mesh=mesh,
        in_specs=in_specs,
        out_specs=out_specs,
        check_vma=False,
    )
```

```python
import functools

import jax
import jax.numpy as jnp
import ml_dtypes
import numpy as np
from jax import lax
from jax.experimental import pallas as pl
from jax.experimental.pallas import tpu as pltpu
from jax.sharding import PartitionSpec as P


D = 8192
EPSILON = 1e-05
BLOCK = 256
LANES = 128


def split_bf16(table):
    high = table.astype(np.float32).astype(ml_dtypes.bfloat16)
    low = (table - high.astype(np.float64)).astype(np.float32).astype(ml_dtypes.bfloat16)
    return high, low


def transform_tables():
    period = 2 * BLOCK
    freq = np.arange(BLOCK)[:, None]
    time = np.arange(BLOCK)[None, :]
    angle = 2.0 * np.pi / period * (freq * time % period)
    real, imag = np.cos(angle), -np.sin(angle)
    imag[0] = np.where(np.arange(BLOCK) % 2 == 0, 1.0, -1.0)
    enter = np.concatenate([real, imag], axis=0)
    angle = 2.0 * np.pi / period * (freq * (time + BLOCK) % period)
    real, imag = 2.0 * np.cos(angle), -2.0 * np.sin(angle)
    real[0] = 1.0
    imag[0] = np.where(np.arange(BLOCK) % 2 == 0, 1.0, -1.0)
    leave = np.concatenate([real, imag], axis=0).T / period
    return (np.concatenate(split_bf16(enter), axis=1), split_bf16(leave)[0])


def rows_to_columns(rows):
    return jnp.concatenate([rows] * 16, axis=0).T


def columns_to_rows(columns):
    lane = lax.broadcasted_iota(jnp.int32, (128, 128), 1)
    square = jnp.zeros((128, 128), jnp.float32)
    for index, column in enumerate(columns):
        square = jnp.where(lane == index, column, square)
    return square.T[:8]


VMEM = pl.BlockSpec(memory_space=pltpu.VMEM)
SMEM = pl.BlockSpec(memory_space=pltpu.SMEM)


def in_vmem(array):
    return pltpu.with_memory_space_constraint(array, pltpu.VMEM)


HBM = pl.BlockSpec(memory_space=pl.ANY)


def in_hbm(array):
    return pltpu.with_memory_space_constraint(array, pltpu.HBM)


def lane_spec(rows, wide):
    return pl.BlockSpec((1, rows, wide), lambda step, *_: (0, 0, step))


def whole(shape):
    return pl.BlockSpec(shape, lambda step, *_: (0,) * len(shape))


def pack_kernel(fwd_hbm, saved_hbm, cot_hbm, out_hbm, squares_ref, held, in_sem, out_sem):
    rows, width = held.shape[1:]
    steps = in_sem.shape[1]
    wide = width // steps
    sources = (fwd_hbm, saved_hbm, cot_hbm)
    arriving = [
        [
            pltpu.make_async_copy(
                source.at[0, :, pl.ds(step * wide, wide)],
                held.at[index, :, pl.ds(step * wide, wide)],
                in_sem.at[index, step],
            )
            for index, source in enumerate(sources)
        ]
        for step in range(steps)
    ]
    for copies in arriving:
        for copy in copies:
            copy.start()
    leaving = []
    totals = [jnp.zeros((rows, LANES), jnp.float32)] * 2
    for step, copies in enumerate(arriving):
        for index, copy in enumerate(copies):
            copy.wait()
            for group in range(step * wide // LANES, (step + 1) * wide // LANES):
                out = pltpu.make_async_copy(
                    held.at[index, :, pl.ds(group * LANES, LANES)],
                    out_hbm.at[group, pl.ds(index * rows, rows), :],
                    out_sem.at[index, group],
                )
                out.start()
                leaving.append(out)
        for index in range(2):
            for group in range(step * wide // LANES, (step + 1) * wide // LANES):
                value = held[index, :, group * LANES : (group + 1) * LANES].astype(jnp.float32)
                totals[index] = totals[index] + value * value
    squares_ref[...] = columns_to_rows([jnp.sum(total, axis=1, keepdims=True) for total in totals])
    for copy in leaving:
        copy.wait()


def pack(fwd_in, saved_in, grad_out):
    rows, width = fwd_in.shape[1:]
    return pl.pallas_call(
        pack_kernel,
        out_shape=(
            pltpu.HBM((width // LANES, 3 * rows, LANES), jnp.bfloat16),
            jax.ShapeDtypeStruct((8, 128), jnp.float32),
        ),
        in_specs=[HBM] * 3,
        out_specs=(HBM, VMEM),
        scratch_shapes=[
            pltpu.VMEM((3, rows, width), jnp.bfloat16),
            pltpu.SemaphoreType.DMA((3, 4)),
            pltpu.SemaphoreType.DMA((3, width // LANES)),
        ],
        name="pack",
        compiler_params=pltpu.CompilerParams(vmem_limit_bytes=16 << 20),
    )(in_hbm(fwd_in), in_hbm(saved_in), in_hbm(grad_out))


def over_chan(rows):
    count = lax.axis_size("chan")
    got = [rows]
    for apart in range(1, count):
        got.append(
            lax.ppermute(rows, "chan", [(low, (low + apart) % count) for low in range(count)])
        )
    return got


def across(rows, flip):
    count = lax.axis_size("seq")
    return lax.ppermute(rows, "seq", [(low, low ^ flip) for low in range(count)])


def round_ring(rows, apart):
    count = lax.axis_size("seq")
    place = lambda low: low // 8 * 8 + (low + 2 * apart) % 8
    return lax.ppermute(rows, "seq", [(low, place(low)) for low in range(count)])


def gather_order():
    own = lax.axis_index("seq").astype(jnp.int32)
    block = jnp.arange(16, dtype=jnp.int32)
    core = (block ^ own) & 1
    back = (own // 2 - block // 2) % 4
    side = (block // 8) ^ (own // 8)
    return side * 8 + back * 2 + core


def early_kernel(sums_ref, saved_ref, sconv_ref, cot_ref, out_ref, inv):
    step = pl.program_id(0)

    @pl.when(step == 0)
    def _():
        inv[...] = rows_to_columns(lax.rsqrt(sums_ref[...] / D + EPSILON))

    inv_saved = inv[:, 1:2]
    pairs = saved_ref.shape[2] // (2 * LANES)
    half = out_ref.shape[0] // 2
    for pair in range(pairs):
        at = pl.ds(pair * 2 * LANES, 2 * LANES)
        normed = saved_ref[0, :, at].astype(jnp.float32) * inv_saved
        grad_query = cot_ref[0, :, at].astype(jnp.float32) * sconv_ref[0, :, at].astype(jnp.float32)
        row = step * pairs + pair
        out_ref[pl.ds(row, 1), :] = jnp.sum(grad_query, axis=0, keepdims=True)
        out_ref[pl.ds(row + half, 1), :] = jnp.sum(grad_query * normed, axis=0, keepdims=True)


def early(sums, saved_in, saved_conv, grad_out):
    rows, width = saved_in.shape[1:]
    wide = 512
    return pl.pallas_call(
        early_kernel,
        out_shape=jax.ShapeDtypeStruct((width // LANES, 2 * LANES), jnp.float32),
        grid=(width // wide,),
        in_specs=[VMEM] + [lane_spec(rows, wide)] * 3,
        out_specs=whole((width // LANES, 2 * LANES)),
        scratch_shapes=[pltpu.VMEM((rows, 128), jnp.float32)],
        name="early",
        compiler_params=pltpu.CompilerParams(vmem_limit_bytes=12 << 20),
    )(sums, in_hbm(saved_in), in_hbm(saved_conv), in_hbm(grad_out))


def side_by_side(ref, index):
    at = 2 * index * BLOCK
    return jnp.concatenate([ref[at : at + BLOCK, :], ref[at + BLOCK : at + 2 * BLOCK, :]], axis=1)


def table_dot(table, data):
    return jnp.dot(
        table[...], jnp.concatenate([data, data], axis=0), preferred_element_type=jnp.float32
    )


def filter_kernel(where_ref, taps_ref, enter, filt, edge):
    del where_ref
    freq = lax.broadcasted_iota(jnp.int32, (2 * BLOCK, LANES), 0)
    parity = jnp.where(freq % 2 == 0, 1.0, -1.0)
    first = lax.broadcasted_iota(jnp.int32, (8, LANES), 0) == 0
    earlier = None
    for pair in range(filt.shape[0] // 2):
        pair_spectra = table_dot(enter, side_by_side(taps_ref.at[0], pair))
        for side in range(2):
            current = pair_spectra[:, side * LANES : (side + 1) * LANES]
            both = parity * current
            if earlier is not None:
                both = both + earlier
            earlier = current
            real, imag = both[:BLOCK], both[BLOCK:]
            index = 2 * pair + side
            filt[index, 0] = real
            filt[index, 1] = imag - real
            filt[index, 2] = imag + real
            edge[index, 0] = jnp.where(first, 0.0, imag[:8])
            edge[index, 1] = jnp.where(first, imag[:8], real[:8])


def filter_spectra(where, filters, tables):
    length = filters.shape[1]
    shape = (length // BLOCK, 3, BLOCK, LANES)
    edge_shape = (length // BLOCK, 2, 8, LANES)
    return pl.pallas_call(
        filter_kernel,
        out_shape=(pltpu.VMEM(shape, jnp.float32), pltpu.VMEM(edge_shape, jnp.float32)),
        grid_spec=pltpu.PrefetchScalarGridSpec(
            num_scalar_prefetch=1,
            grid=(1,),
            in_specs=[pl.BlockSpec((1, length, LANES), lambda step, at: (0, 0, at[0]))]
            + [whole(tables[0].shape)],
            out_specs=(VMEM, VMEM),
        ),
        name="filter_spectra",
        compiler_params=pltpu.CompilerParams(vmem_limit_bytes=16 << 20),
    )(where, in_hbm(filters), in_hbm(tables[0]))


def fold(block):
    return jnp.sum(block.reshape(block.shape[0] // 8, 8, LANES), axis=0)


def conv_kernel(
    where_ref, order_ref, gathered_ref, inv_ref, known_ref, params_ref, filt, edge, raw_hbm, enter_hbm,
    leave_hbm, out_hbm, raw_ref, enter, leave, out_ref, ordered, spectra, product, inv_rows, inv, raw_sem, table_sem, out_sem,
):
    stored = raw_ref.shape[0]
    raw_copies = [
        pltpu.make_async_copy(raw_hbm.at[index], raw_ref.at[index], raw_sem.at[index])
        for index in range(stored)
    ]
    table_copies = [
        pltpu.make_async_copy(source, target, table_sem.at[index])
        for index, (source, target) in enumerate(((enter_hbm.at[:, pl.ds(0, BLOCK)], enter), (leave_hbm, leave)))
    ]
    out_copies = [
        pltpu.make_async_copy(out_ref.at[index], out_hbm.at[index], out_sem.at[index])
        for index in range(stored)
    ]
    for copy in raw_copies + table_copies:
        copy.start()
    rows = raw_ref.shape[1] // 3
    blocks = stored * rows // BLOCK
    lanes = pl.ds(pl.multiple_of(where_ref[0] * LANES, LANES), LANES)
    p = [params_ref[0, row : row + 1, lanes] for row in range(7)]

    gains = [p[0] * p[1], p[0] * p[3], p[0] * p[5]]
    for index in range(stored):
        inv_rows[2 * index : 2 * index + 2, :] = inv_ref[pl.ds(2 * gathered_ref[index], 2), :]
    inv[...] = jnp.concatenate([inv_rows[...]] * (128 // (2 * stored)), axis=0).T
    for index in range(stored):
        if index % 4 == 0:
            for copy in raw_copies[index : index + 4]:
                copy.wait()
        at = pl.multiple_of(order_ref[index] * rows, rows)
        inv_fwd = inv[:, 2 * index : 2 * index + 1]
        inv_saved = inv[:, 2 * index + 1 : 2 * index + 2]
        normed = raw_ref[index, :rows, :].astype(jnp.float32) * inv_fwd
        mixed = (normed * gains[1] + p[4]) * (normed * gains[2] + p[6])
        normed = raw_ref[index, rows : 2 * rows, :].astype(jnp.float32) * inv_saved
        cot = raw_ref[index, 2 * rows :, :].astype(jnp.float32)
        ordered[pl.ds(at, rows), :LANES] = mixed.astype(jnp.bfloat16)
        ordered[pl.ds(at, rows), LANES:] = (cot * (normed * gains[0] + p[2])).astype(jnp.bfloat16)

    table_copies[0].wait()
    for index in range(blocks):
        data = ordered[index * BLOCK : (index + 1) * BLOCK, :]
        spectra[index] = jnp.dot(enter[...], data, preferred_element_type=jnp.float32)

    def forward_and_adjoint(low, high, one_product):
        for adjoint in (False, True):
            lanes = slice(LANES, 2 * LANES) if adjoint else slice(0, LANES)
            x_re = [spectra[j, low, lanes] for j in range(blocks)]
            x_im = [spectra[j, high, lanes] for j in range(blocks)]
            for i in range(blocks):
                terms = range(i, blocks) if adjoint else range(i + 1)
                re, im = one_product(adjoint, x_re, x_im, [(abs(i - j), j) for j in terms])
                product[i, low, lanes] = re
                product[i, high, lanes] = im

    def total(terms):
        terms = list(terms)
        return functools.reduce(lambda one, two: one + two, terms)

    def first_tile(adjoint, x_re, x_im, terms):
        f_re = [filt[d, 0, 0:8, :] for d in range(blocks)]
        f_im = [edge[d, 0] for d in range(blocks)]
        f_nq = [edge[d, 1] for d in range(blocks)]
        direct = total(f_re[d] * x_re[j] for d, j in terms)
        crossed = total(f_im[d] * x_im[j] for d, j in terms)
        straight = total(f_nq[d] * x_im[j] for d, j in terms)
        turned = total(f_im[d] * x_re[j] for d, j in terms)
        if adjoint:
            return direct + crossed, straight - turned
        return direct - crossed, straight + turned

    forward_and_adjoint(slice(0, 8), slice(BLOCK, BLOCK + 8), first_tile)

    def products(tile, carry):
        low = pl.ds(pl.multiple_of(tile * 8, 8), 8)
        high = pl.ds(pl.multiple_of(BLOCK + tile * 8, 8), 8)
        f_re = [filt[d, 0, low, :] for d in range(blocks)]
        f_less = [filt[d, 1, low, :] for d in range(blocks)]
        f_more = [filt[d, 2, low, :] for d in range(blocks)]

        def other_tile(adjoint, x_re, x_im, terms):
            both = total(f_re[d] * (x_re[j] + x_im[j]) for d, j in terms)
            if adjoint:
                return (
                    both + total(f_less[d] * x_im[j] for d, j in terms),
                    both - total(f_more[d] * x_re[j] for d, j in terms),
                )
            return (
                both - total(f_more[d] * x_im[j] for d, j in terms),
                both + total(f_less[d] * x_re[j] for d, j in terms),
            )

        forward_and_adjoint(low, high, other_tile)
        return carry

    lax.fori_loop(1, BLOCK // 8, products, 0)

    table_copies[1].wait()
    for index in range(blocks):
        left = jnp.dot(
            leave[...], product[index].astype(jnp.bfloat16), preferred_element_type=jnp.float32
        )
        ordered[index * BLOCK : (index + 1) * BLOCK, :] = left.astype(jnp.bfloat16)

    sums = [jnp.zeros((8, LANES), jnp.float32)] * 3
    for index in range(stored):
        at = pl.multiple_of(order_ref[index] * rows, rows)
        block = ordered[pl.ds(at, rows), :]
        out_ref[index, :rows, :] = block
        grad_mixed = block[:, LANES:].astype(jnp.float32)
        inv_saved = inv[:, 2 * index + 1 : 2 * index + 2]
        normed = raw_ref[index, rows : 2 * rows, :].astype(jnp.float32) * inv_saved
        once = grad_mixed * normed
        for power, term in enumerate((grad_mixed, once, once * normed)):
            sums[power] = sums[power] + fold(term)

    sums = jnp.concatenate(
        [jnp.sum(total, axis=0, keepdims=True) for total in sums]
        + [jnp.zeros((5, LANES), jnp.float32)],
        axis=0,
    )
    known = known_ref[...].astype(jnp.bfloat16)
    top = sums.astype(jnp.bfloat16)
    rest = (sums - top.astype(jnp.float32)).astype(jnp.bfloat16)
    for index in range(stored):
        out_ref[index, rows : rows + 16, :] = known
        out_ref[index, rows + 16 :, :LANES] = top
        out_ref[index, rows + 16 :, LANES:] = rest
        out_copies[index].start()
    for copy in out_copies:
        copy.wait()


def convolve(where, order, gathered, raw, inv, known, params, spectra, tables):
    filt, edge = spectra
    stored = raw.shape[0]
    rows = raw.shape[1] // 3
    length = stored * rows
    blocks = length // BLOCK
    return pl.pallas_call(
        conv_kernel,
        out_shape=pltpu.HBM((stored, rows + 24, 2 * LANES), jnp.bfloat16),
        in_specs=[SMEM] * 3 + [VMEM] * 5 + [HBM] * 3,
        out_specs=HBM,
        scratch_shapes=[
            pltpu.VMEM(raw.shape, jnp.bfloat16),
            pltpu.VMEM((2 * BLOCK, BLOCK), jnp.bfloat16),
            pltpu.VMEM((BLOCK, 2 * BLOCK), jnp.bfloat16),
            pltpu.VMEM((stored, rows + 24, 2 * LANES), jnp.bfloat16),
            pltpu.VMEM((length, 2 * LANES), jnp.bfloat16),
            pltpu.VMEM((blocks, 2 * BLOCK, 2 * LANES), jnp.float32),
            pltpu.VMEM((blocks, 2 * BLOCK, 2 * LANES), jnp.float32),
            pltpu.VMEM((2 * stored, 128), jnp.float32),
            pltpu.VMEM((128, 128), jnp.float32),
            pltpu.SemaphoreType.DMA((stored,)),
            pltpu.SemaphoreType.DMA((2,)),
            pltpu.SemaphoreType.DMA((stored,)),
        ],
        name="convolve",
        compiler_params=pltpu.CompilerParams(vmem_limit_bytes=28 << 20),
    )(
        where, order, gathered, inv, known, params, in_vmem(filt), in_vmem(edge), in_hbm(raw),
        *[in_hbm(table) for table in tables],
    )


def forward_terms(at, inputs, conv, params_ref, inv_fwd):
    p = [params_ref[0, row : row + 1, at] for row in range(3)]
    query = inputs * inv_fwd * (p[0] * p[1]) + p[2]
    return inputs + query * conv


def backward_terms(at, saved, sconv, cot, grad_mixed, params_ref, inv_saved):
    p = [params_ref[0, row : row + 1, at] for row in range(7)]
    normed = saved * inv_saved
    mixed_grad = normed * (2.0 * p[0] * p[3] * p[5] * p[0]) + p[0] * (p[6] * p[3] + p[4] * p[5])
    grad_normed = cot * sconv * (p[1] * p[0]) + grad_mixed * mixed_grad
    return cot + inv_saved * grad_normed, grad_normed * normed


def leave_kernel(
    pipe_ref, inv_ref, back_ref, fwd_ref, saved_ref, sconv_ref, cot_ref, params_ref,
    send_ref, cross_ref, inv, acc,
):
    rows, width = fwd_ref.shape[1:]
    inv[...] = rows_to_columns(inv_ref[0:8, :])
    inv_fwd = inv[:, 0:1]
    inv_saved = inv[:, 1:2]

    def backward(send):
        cross = jnp.zeros((rows, LANES), jnp.float32)
        for group in range(width // LANES):
            at = pl.ds(group * LANES, LANES)
            partial, term = backward_terms(
                at,
                saved_ref[0, :, at].astype(jnp.float32),
                sconv_ref[0, :, at].astype(jnp.float32),
                cot_ref[0, :, at].astype(jnp.float32),
                back_ref[group, :rows, LANES:].astype(jnp.float32),
                params_ref,
                inv_saved,
            )
            cross = cross + term
            if send:
                send_ref[0, :, at] = partial.astype(jnp.bfloat16)
        acc[...] = cross

    @pl.when(pipe_ref[0] == 0)
    def _():
        for group in range(width // LANES):
            at = pl.ds(group * LANES, LANES)
            inputs = fwd_ref[0, :, at].astype(jnp.float32)
            conv = back_ref[group, :rows, :LANES].astype(jnp.float32)
            layer = forward_terms(at, inputs, conv, params_ref, inv_fwd)
            send_ref[0, :, at] = layer.astype(jnp.bfloat16)
        backward(False)

    @pl.when(pipe_ref[0] != 0)
    def _():
        backward(True)

    cross = columns_to_rows([jnp.sum(acc[...], axis=1, keepdims=True)])
    cross_ref[...] = cross * (inv_ref[1:2, :] * inv_ref[1:2, :] / D)


def leave(pipe, inv, back, fwd_in, saved_in, saved_conv, grad_out, mix_params):
    return pl.pallas_call(
        leave_kernel,
        out_shape=(
            pltpu.VMEM(fwd_in.shape, jnp.bfloat16),
            pltpu.VMEM((8, 128), jnp.float32),
        ),
        in_specs=[SMEM] + [VMEM] * 7,
        out_specs=(VMEM, VMEM),
        scratch_shapes=[pltpu.VMEM((fwd_in.shape[1], 128), jnp.float32)] * 2,
        name="leave",
        compiler_params=pltpu.CompilerParams(vmem_limit_bytes=24 << 20),
    )(
        pipe, inv, in_vmem(back),
        *[in_vmem(a) for a in (fwd_in, saved_in, saved_conv, grad_out)], mix_params,
    )


def forward_kernel(inv_ref, back_ref, fwd_ref, params_ref, layer_ref, grads_ref, known, inv):
    step = pl.program_id(0)
    rows = fwd_ref.shape[1]

    @pl.when(step == 0)
    def _():
        inv[...] = rows_to_columns(inv_ref[0:8, :])
        total = back_ref[0, rows : rows + 16, :].astype(jnp.float32)
        for index in range(1, back_ref.shape[0]):
            total = total + back_ref[index, rows : rows + 16, :].astype(jnp.float32)
        for row in range(16):
            known[row] = total[row : row + 1, :]

    wide = layer_ref.shape[2]
    groups = wide // LANES
    for group in range(groups):
        own = pl.ds(group * LANES, LANES)
        at = pl.ds(pl.multiple_of(step * wide + group * LANES, LANES), LANES)
        block = step * groups + group
        conv = back_ref[block, :rows, :LANES].astype(jnp.float32)
        inputs = fwd_ref[0, :, at].astype(jnp.float32)
        layer = forward_terms(own, inputs, conv, params_ref, inv[:, 0:1])
        layer_ref[0, :, own] = layer.astype(jnp.bfloat16)

        p = [params_ref[0, row : row + 1, own] for row in range(7)]
        extra = back_ref[block, rows + 16 :, :].astype(jnp.float32)
        extra = extra[:, :LANES] + extra[:, LANES:]
        m0, m1, m2 = extra[0:1], extra[1:2], extra[2:3]
        row = step * (groups // 2) + group // 2
        side = slice(group % 2 * LANES, (group % 2 + 1) * LANES)
        q0, q1 = known[row, :, side], known[row + 8, :, side]
        key_normed = p[0] * p[5] * m2 + p[6] * m1
        value_normed = p[0] * p[3] * m2 + p[4] * m1
        grads = [
            p[1] * q1 + p[3] * key_normed + p[5] * value_normed,
            p[0] * q1,
            q0,
            p[0] * key_normed,
            p[0] * p[5] * m1 + p[6] * m0,
            p[0] * value_normed,
            p[0] * p[3] * m1 + p[4] * m0,
        ]
        grads_ref[0, :, own] = jnp.concatenate(grads, axis=0)


def finish_forward(inv, back, fwd_in, mix_params):
    rows, width = fwd_in.shape[1:]
    wide = 512
    return pl.pallas_call(
        forward_kernel,
        out_shape=(
            jax.ShapeDtypeStruct(fwd_in.shape, jnp.bfloat16),
            jax.ShapeDtypeStruct(mix_params.shape, jnp.float32),
        ),
        grid=(width // wide,),
        in_specs=[VMEM] * 3 + [lane_spec(7, wide)],
        out_specs=(lane_spec(rows, wide), lane_spec(7, wide)),
        scratch_shapes=[
            pltpu.VMEM((16, 1, 2 * LANES), jnp.float32),
            pltpu.VMEM((rows, 128), jnp.float32),
        ],
        name="finish_forward",
        compiler_params=pltpu.CompilerParams(vmem_limit_bytes=16 << 20),
    )(inv, in_vmem(back), in_vmem(fwd_in), mix_params)


def backward_kernel(
    s0, s1, s2, s3, inv_ref, back_ref, saved_ref, sconv_ref, cot_ref, params_ref, peer_ref,
    grad_ref, term_ref, scale, inv,
):
    step = pl.program_id(0)

    @pl.when(step == 0)
    def _():
        scale[...] = rows_to_columns(s0[...] + s1[...] + s2[...] + s3[...])
        inv[...] = rows_to_columns(inv_ref[0:8, :])

    rows, wide = grad_ref.shape[1:]
    for group in range(wide // LANES):
        own = pl.ds(group * LANES, LANES)
        at = pl.ds(pl.multiple_of(step * wide + group * LANES, LANES), LANES)
        saved = saved_ref[0, :, at].astype(jnp.float32)
        partial, _ = backward_terms(
            own,
            saved,
            sconv_ref[0, :, at].astype(jnp.float32),
            cot_ref[0, :, at].astype(jnp.float32),
            back_ref[step * (wide // LANES) + group, :rows, LANES:].astype(jnp.float32),
            params_ref,
            inv[:, 1:2],
        )
        grad_ref[0, :, own] = (partial - saved * scale[:, 0:1]).astype(jnp.bfloat16)
        term_ref[:, at] = peer_ref[0, :, own].astype(jnp.float32) * scale[:, 1:2]


def finish_backward(scales, inv, back, saved_in, saved_conv, grad_out, mix_params, peer_saved):
    rows, width = saved_in.shape[1:]
    wide = 512
    spec = lane_spec(rows, wide)
    return pl.pallas_call(
        backward_kernel,
        out_shape=(
            jax.ShapeDtypeStruct(saved_in.shape, jnp.bfloat16),
            pltpu.VMEM((rows, width), jnp.float32),
        ),
        grid=(width // wide,),
        in_specs=[VMEM] * 9 + [lane_spec(7, wide), spec],
        out_specs=(spec, VMEM),
        scratch_shapes=[pltpu.VMEM((rows, 128), jnp.float32)] * 2,
        name="finish_backward",
        compiler_params=pltpu.CompilerParams(vmem_limit_bytes=16 << 20),
    )(
        *scales, inv, in_vmem(back),
        *[in_vmem(a) for a in (saved_in, saved_conv, grad_out)], mix_params, in_hbm(peer_saved),
    )


def received_kernel(value_ref, term_ref, out_ref):
    wide = out_ref.shape[2]
    for at in range(0, wide, LANES):
        own = pl.ds(at, LANES)
        source = pl.ds(pl.multiple_of(pl.program_id(0) * wide + at, LANES), LANES)
        value = value_ref[0, :, source].astype(jnp.float32)
        out_ref[0, :, own] = (value - term_ref[:, source]).astype(jnp.bfloat16)


def finish_received(value, term):
    rows, width = term.shape
    wide = 512
    return pl.pallas_call(
        received_kernel,
        out_shape=jax.ShapeDtypeStruct(value.shape, jnp.bfloat16),
        grid=(width // wide,),
        in_specs=[VMEM, VMEM],
        out_specs=lane_spec(rows, wide),
        name="received",
        compiler_params=pltpu.CompilerParams(vmem_limit_bytes=8 << 20),
    )(in_vmem(value), in_vmem(term))


def per_device(tables, fwd_in, saved_in, saved_conv, grad_out, filters, mix_params, span_order):
    where = lax.axis_index("seq").astype(jnp.int32).reshape(1)
    pipe = lax.axis_index("pipe").astype(jnp.int32).reshape(1)
    raw, sums = pack(fwd_in, saved_in, grad_out)
    raw = lax.all_to_all(raw, "seq", 0, 0)
    own_sums = sum(over_chan(sums))
    sums = own_sums[:2]
    sums = jnp.concatenate([sums, across(sums, 1)], axis=0)
    sums = jnp.concatenate([sums] + [round_ring(sums, apart) for apart in (1, 2, 3)], axis=0)
    inv = lax.rsqrt(jnp.concatenate([sums, across(sums, 8)], axis=0) / D + EPSILON)
    peer_saved = lax.ppermute(saved_in, "pipe", [(1, 0)])
    spectra = filter_spectra(where, filters, tables)
    known = early(own_sums, saved_in, saved_conv, grad_out)
    back = convolve(where, span_order, gather_order(), raw, inv, known, mix_params, spectra, tables)
    back = lax.all_to_all(back, "seq", 0, 0)
    outgoing, cross = leave(pipe, inv, back, fwd_in, saved_in, saved_conv, grad_out, mix_params)
    peer_cross = lax.ppermute(cross, "pipe", [(1, 0)])
    incoming = lax.ppermute(outgoing, "pipe", [(0, 1), (1, 0)])
    scales = over_chan(jnp.concatenate([cross[:1], peer_cross[:1], cross[:6]], axis=0))
    layer_out, param_grad = finish_forward(inv, back, fwd_in, mix_params)
    input_grad, term = finish_backward(
        scales, inv, back, saved_in, saved_conv, grad_out, mix_params, peer_saved
    )
    received = finish_received(incoming, term)
    return (layer_out, input_grad, param_grad, received)


def solution(mesh):
    tables = transform_tables()
    in_specs = (
        P("pipe", "seq", "chan"),
        P("pipe", "seq", "chan"),
        P("pipe", "seq", "chan"),
        P("pipe", "seq", "chan"),
        P("pipe", None, "chan"),
        P("pipe", None, "chan"),
        P(),
    )
    out_specs = (
        P("pipe", "seq", "chan"),
        P("pipe", "seq", "chan"),
        P("pipe", None, "chan"),
        P("pipe", "seq", "chan"),
    )
    return jax.shard_map(
        functools.partial(per_device, tuple(jnp.asarray(table) for table in tables)),
        mesh=mesh,
        in_specs=in_specs,
        out_specs=out_specs,
        check_vma=False,
    )
```

```python
import functools

import jax
import jax.numpy as jnp
import ml_dtypes
import numpy as np
from jax import lax
from jax.experimental import pallas as pl
from jax.experimental.pallas import tpu as pltpu
from jax.sharding import PartitionSpec as P


D = 8192
EPSILON = 1e-05
BLOCK = 256
LANES = 128


def transform_tables():
    period = 2 * BLOCK
    freq = np.arange(BLOCK)[:, None]
    time = np.arange(BLOCK)[None, :]
    angle = 2.0 * np.pi / period * (freq * time % period)
    real, imag = np.cos(angle), -np.sin(angle)
    imag[0] = np.where(np.arange(BLOCK) % 2 == 0, 1.0, -1.0)
    enter = np.concatenate([real, imag], axis=0)
    angle = 2.0 * np.pi / period * (freq * (time + BLOCK) % period)
    real, imag = 2.0 * np.cos(angle), -2.0 * np.sin(angle)
    real[0] = 1.0
    imag[0] = np.where(np.arange(BLOCK) % 2 == 0, 1.0, -1.0)
    leave = np.concatenate([real, imag], axis=0).T / period
    return tuple(table.astype(np.float32).astype(ml_dtypes.bfloat16) for table in (enter, leave))


def rows_to_columns(rows):
    return jnp.concatenate([rows] * 16, axis=0).T


def columns_to_rows(columns):
    lane = lax.broadcasted_iota(jnp.int32, (128, 128), 1)
    square = jnp.zeros((128, 128), jnp.float32)
    for index, column in enumerate(columns):
        square = jnp.where(lane == index, column, square)
    return square.T[:8]


VMEM = pl.BlockSpec(memory_space=pltpu.VMEM)
SMEM = pl.BlockSpec(memory_space=pltpu.SMEM)


def in_vmem(array):
    return pltpu.with_memory_space_constraint(array, pltpu.VMEM)


HBM = pl.BlockSpec(memory_space=pl.ANY)


def in_hbm(array):
    return pltpu.with_memory_space_constraint(array, pltpu.HBM)


def lane_spec(rows, wide):
    return pl.BlockSpec((1, rows, wide), lambda step, *_: (0, 0, step))


def whole(shape):
    return pl.BlockSpec(shape, lambda step, *_: (0,) * len(shape))


def pack_kernel(fwd_hbm, saved_hbm, cot_hbm, out_hbm, squares_ref, held, in_sem, out_sem):
    rows, width = held.shape[1:]
    steps = in_sem.shape[1]
    wide = width // steps
    sources = (fwd_hbm, saved_hbm, cot_hbm)
    arriving = [
        [
            pltpu.make_async_copy(
                source.at[0, :, pl.ds(step * wide, wide)],
                held.at[index, :, pl.ds(step * wide, wide)],
                in_sem.at[index, step],
            )
            for index, source in enumerate(sources)
        ]
        for step in range(steps)
    ]
    for copies in arriving:
        for copy in copies:
            copy.start()
    leaving = []
    totals = [jnp.zeros((rows, LANES), jnp.float32)] * 2
    for step, copies in enumerate(arriving):
        for index, copy in enumerate(copies):
            copy.wait()
            for group in range(step * wide // LANES, (step + 1) * wide // LANES):
                out = pltpu.make_async_copy(
                    held.at[index, :, pl.ds(group * LANES, LANES)],
                    out_hbm.at[group, pl.ds(index * rows, rows), :],
                    out_sem.at[index, group],
                )
                out.start()
                leaving.append(out)
        for index in range(2):
            for group in range(step * wide // LANES, (step + 1) * wide // LANES):
                value = held[index, :, group * LANES : (group + 1) * LANES].astype(jnp.float32)
                totals[index] = totals[index] + value * value
    squares_ref[...] = columns_to_rows([jnp.sum(total, axis=1, keepdims=True) for total in totals])
    for copy in leaving:
        copy.wait()


def pack(fwd_in, saved_in, grad_out):
    rows, width = fwd_in.shape[1:]
    return pl.pallas_call(
        pack_kernel,
        out_shape=(
            pltpu.HBM((width // LANES, 3 * rows, LANES), jnp.bfloat16),
            jax.ShapeDtypeStruct((8, 128), jnp.float32),
        ),
        in_specs=[HBM] * 3,
        out_specs=(HBM, VMEM),
        scratch_shapes=[
            pltpu.VMEM((3, rows, width), jnp.bfloat16),
            pltpu.SemaphoreType.DMA((3, 4)),
            pltpu.SemaphoreType.DMA((3, width // LANES)),
        ],
        name="pack",
        compiler_params=pltpu.CompilerParams(vmem_limit_bytes=16 << 20),
    )(in_hbm(fwd_in), in_hbm(saved_in), in_hbm(grad_out))


def over_chan(rows):
    count = lax.axis_size("chan")
    got = [rows]
    for apart in range(1, count):
        got.append(
            lax.ppermute(rows, "chan", [(low, (low + apart) % count) for low in range(count)])
        )
    return got


def across(rows, flip):
    count = lax.axis_size("seq")
    return lax.ppermute(rows, "seq", [(low, low ^ flip) for low in range(count)])


def from_chip(rows, side, back):
    count = lax.axis_size("seq")
    place = lambda low: (low // 8 ^ side) * 8 + (low + 2 * back) % 8
    return lax.ppermute(rows, "seq", [(low, place(low)) for low in range(count)])


def gather_order():
    own = lax.axis_index("seq").astype(jnp.int32)
    block = jnp.arange(16, dtype=jnp.int32)
    core = (block ^ own) & 1
    back = (own // 2 - block // 2) % 4
    side = (block // 8) ^ (own // 8)
    return side * 8 + back * 2 + core


def early_kernel(sums_ref, saved_ref, sconv_ref, cot_ref, out_ref, inv):
    step = pl.program_id(0)

    @pl.when(step == 0)
    def _():
        inv[...] = rows_to_columns(lax.rsqrt(sums_ref[...] / D + EPSILON))

    inv_saved = inv[:, 1:2]
    pairs = saved_ref.shape[2] // (2 * LANES)
    half = out_ref.shape[0] // 2
    for pair in range(pairs):
        at = pl.ds(pair * 2 * LANES, 2 * LANES)
        normed = saved_ref[0, :, at].astype(jnp.float32) * inv_saved
        grad_query = cot_ref[0, :, at].astype(jnp.float32) * sconv_ref[0, :, at].astype(jnp.float32)
        row = step * pairs + pair
        out_ref[pl.ds(row, 1), :] = jnp.sum(grad_query, axis=0, keepdims=True)
        out_ref[pl.ds(row + half, 1), :] = jnp.sum(grad_query * normed, axis=0, keepdims=True)


def early(sums, saved_in, saved_conv, grad_out):
    rows, width = saved_in.shape[1:]
    wide = 512
    return pl.pallas_call(
        early_kernel,
        out_shape=jax.ShapeDtypeStruct((width // LANES, 2 * LANES), jnp.float32),
        grid=(width // wide,),
        in_specs=[VMEM] + [lane_spec(rows, wide)] * 3,
        out_specs=whole((width // LANES, 2 * LANES)),
        scratch_shapes=[pltpu.VMEM((rows, 128), jnp.float32)],
        name="early",
        compiler_params=pltpu.CompilerParams(vmem_limit_bytes=12 << 20),
    )(sums, in_hbm(saved_in), in_hbm(saved_conv), in_hbm(grad_out))


def side_by_side(ref, index):
    at = 2 * index * BLOCK
    return jnp.concatenate([ref[at : at + BLOCK, :], ref[at + BLOCK : at + 2 * BLOCK, :]], axis=1)


def filter_kernel(where_ref, taps_ref, enter, filt):
    del where_ref
    freq = lax.broadcasted_iota(jnp.int32, (2 * BLOCK, LANES), 0)
    parity = jnp.where(freq % 2 == 0, 1.0, -1.0)
    earlier = None
    for pair in range(filt.shape[0] // 2):
        pair_spectra = jnp.dot(
            enter[...], side_by_side(taps_ref.at[0], pair), preferred_element_type=jnp.float32
        )
        for side in range(2):
            current = pair_spectra[:, side * LANES : (side + 1) * LANES]
            both = parity * current
            if earlier is not None:
                both = both + earlier
            earlier = current
            filt[2 * pair + side, 0] = both[:BLOCK]
            filt[2 * pair + side, 1] = both[BLOCK:]


def filter_spectra(where, filters, tables):
    length = filters.shape[1]
    shape = (length // BLOCK, 2, BLOCK, LANES)
    return pl.pallas_call(
        filter_kernel,
        out_shape=pltpu.VMEM(shape, jnp.float32),
        grid_spec=pltpu.PrefetchScalarGridSpec(
            num_scalar_prefetch=1,
            grid=(1,),
            in_specs=[pl.BlockSpec((1, length, LANES), lambda step, at: (0, 0, at[0]))]
            + [whole(tables[0].shape)],
            out_specs=VMEM,
        ),
        name="filter_spectra",
        compiler_params=pltpu.CompilerParams(vmem_limit_bytes=16 << 20),
    )(where, in_hbm(filters), in_hbm(tables[0]))


def fold(block):
    return jnp.sum(block.reshape(block.shape[0] // 8, 8, LANES), axis=0)


def conv_kernel(
    where_ref, order_ref, gathered_ref, inv_ref, known_ref, params_ref, filt, raw_hbm, enter_hbm,
    leave_hbm, out_hbm, raw_ref, enter, leave, out_ref, ordered, spectra, product, inv_rows, inv, raw_sem, table_sem, out_sem,
):
    stored = raw_ref.shape[0]
    raw_copies = [
        pltpu.make_async_copy(raw_hbm.at[index], raw_ref.at[index], raw_sem.at[index])
        for index in range(stored)
    ]
    table_copies = [
        pltpu.make_async_copy(source, target, table_sem.at[index])
        for index, (source, target) in enumerate(((enter_hbm, enter), (leave_hbm, leave)))
    ]
    out_copies = [
        pltpu.make_async_copy(out_ref.at[index], out_hbm.at[index], out_sem.at[index])
        for index in range(stored)
    ]
    for copy in raw_copies + table_copies:
        copy.start()
    rows = raw_ref.shape[1] // 3
    blocks = stored * rows // BLOCK
    lanes = pl.ds(pl.multiple_of(where_ref[0] * LANES, LANES), LANES)
    p = [params_ref[0, row : row + 1, lanes] for row in range(7)]

    gains = [p[0] * p[1], p[0] * p[3], p[0] * p[5]]
    for index in range(stored):
        inv_rows[2 * index : 2 * index + 2, :] = inv_ref[pl.ds(2 * gathered_ref[index], 2), :]
    inv[...] = jnp.concatenate([inv_rows[...]] * (128 // (2 * stored)), axis=0).T
    for index in range(stored):
        if index % 4 == 0:
            for copy in raw_copies[index : index + 4]:
                copy.wait()
        at = pl.multiple_of(order_ref[index] * rows, rows)
        inv_fwd = inv[:, 2 * index : 2 * index + 1]
        inv_saved = inv[:, 2 * index + 1 : 2 * index + 2]
        normed = raw_ref[index, :rows, :].astype(jnp.float32) * inv_fwd
        mixed = (normed * gains[1] + p[4]) * (normed * gains[2] + p[6])
        normed = raw_ref[index, rows : 2 * rows, :].astype(jnp.float32) * inv_saved
        cot = raw_ref[index, 2 * rows :, :].astype(jnp.float32)
        ordered[pl.ds(at, rows), :LANES] = mixed.astype(jnp.bfloat16)
        ordered[pl.ds(at, rows), LANES:] = (cot * (normed * gains[0] + p[2])).astype(jnp.bfloat16)

    table_copies[0].wait()
    for index in range(blocks):
        data = ordered[index * BLOCK : (index + 1) * BLOCK, :]
        spectra[index] = jnp.dot(enter[...], data, preferred_element_type=jnp.float32)

    def forward_and_adjoint(low, high, one_product):
        for adjoint in (False, True):
            lanes = slice(LANES, 2 * LANES) if adjoint else slice(0, LANES)
            x_re = [spectra[j, low, lanes] for j in range(blocks)]
            x_im = [spectra[j, high, lanes] for j in range(blocks)]
            for i in range(blocks):
                terms = range(i, blocks) if adjoint else range(i + 1)
                re, im = one_product(adjoint, x_re, x_im, [(abs(i - j), j) for j in terms])
                product[i, low, lanes] = re
                product[i, high, lanes] = im

    def total(terms):
        terms = list(terms)
        return functools.reduce(lambda one, two: one + two, terms)

    def first_tile(adjoint, x_re, x_im, terms):
        f_re = [filt[d, 0, 0:8, :] for d in range(blocks)]
        first = lax.broadcasted_iota(jnp.int32, (8, LANES), 0) == 0
        imag = [filt[d, 1, 0:8, :] for d in range(blocks)]
        f_im = [jnp.where(first, 0.0, value) for value in imag]
        f_nq = [jnp.where(first, value, f_re[d]) for d, value in enumerate(imag)]
        direct = total(f_re[d] * x_re[j] for d, j in terms)
        crossed = total(f_im[d] * x_im[j] for d, j in terms)
        straight = total(f_nq[d] * x_im[j] for d, j in terms)
        turned = total(f_im[d] * x_re[j] for d, j in terms)
        if adjoint:
            return direct + crossed, straight - turned
        return direct - crossed, straight + turned

    forward_and_adjoint(slice(0, 8), slice(BLOCK, BLOCK + 8), first_tile)

    def products(tile, carry):
        low = pl.ds(pl.multiple_of(tile * 8, 8), 8)
        high = pl.ds(pl.multiple_of(BLOCK + tile * 8, 8), 8)
        f_re = [filt[d, 0, low, :] for d in range(blocks)]
        f_im = [filt[d, 1, low, :] for d in range(blocks)]
        f_less = [f_im[d] - f_re[d] for d in range(blocks)]
        f_more = [f_im[d] + f_re[d] for d in range(blocks)]

        def other_tile(adjoint, x_re, x_im, terms):
            both = total(f_re[d] * (x_re[j] + x_im[j]) for d, j in terms)
            if adjoint:
                return (
                    both + total(f_less[d] * x_im[j] for d, j in terms),
                    both - total(f_more[d] * x_re[j] for d, j in terms),
                )
            return (
                both - total(f_more[d] * x_im[j] for d, j in terms),
                both + total(f_less[d] * x_re[j] for d, j in terms),
            )

        forward_and_adjoint(low, high, other_tile)
        return carry

    lax.fori_loop(1, BLOCK // 8, products, 0)

    table_copies[1].wait()
    for index in range(blocks):
        left = jnp.dot(
            leave[...], product[index].astype(jnp.bfloat16), preferred_element_type=jnp.float32
        )
        ordered[index * BLOCK : (index + 1) * BLOCK, :] = left.astype(jnp.bfloat16)

    sums = [jnp.zeros((8, LANES), jnp.float32)] * 3
    for index in range(stored):
        at = pl.multiple_of(order_ref[index] * rows, rows)
        block = ordered[pl.ds(at, rows), :]
        out_ref[index, :rows, :] = block
        grad_mixed = block[:, LANES:].astype(jnp.float32)
        inv_saved = inv[:, 2 * index + 1 : 2 * index + 2]
        normed = raw_ref[index, rows : 2 * rows, :].astype(jnp.float32) * inv_saved
        once = grad_mixed * normed
        for power, term in enumerate((grad_mixed, once, once * normed)):
            sums[power] = sums[power] + fold(term)

    sums = jnp.concatenate(
        [jnp.sum(total, axis=0, keepdims=True) for total in sums]
        + [jnp.zeros((5, LANES), jnp.float32)],
        axis=0,
    )
    known = known_ref[...].astype(jnp.bfloat16)
    top = sums.astype(jnp.bfloat16)
    rest = (sums - top.astype(jnp.float32)).astype(jnp.bfloat16)
    for index in range(stored):
        out_ref[index, rows : rows + 16, :] = known
        out_ref[index, rows + 16 :, :LANES] = top
        out_ref[index, rows + 16 :, LANES:] = rest
        out_copies[index].start()
    for copy in out_copies:
        copy.wait()


def convolve(where, order, gathered, raw, inv, known, params, spectra, tables):
    stored = raw.shape[0]
    rows = raw.shape[1] // 3
    length = stored * rows
    blocks = length // BLOCK
    return pl.pallas_call(
        conv_kernel,
        out_shape=pltpu.HBM((stored, rows + 24, 2 * LANES), jnp.bfloat16),
        in_specs=[SMEM] * 3 + [VMEM] * 4 + [HBM] * 3,
        out_specs=HBM,
        scratch_shapes=[
            pltpu.VMEM(raw.shape, jnp.bfloat16),
            pltpu.VMEM((2 * BLOCK, BLOCK), jnp.bfloat16),
            pltpu.VMEM((BLOCK, 2 * BLOCK), jnp.bfloat16),
            pltpu.VMEM((stored, rows + 24, 2 * LANES), jnp.bfloat16),
            pltpu.VMEM((length, 2 * LANES), jnp.bfloat16),
            pltpu.VMEM((blocks, 2 * BLOCK, 2 * LANES), jnp.float32),
            pltpu.VMEM((blocks, 2 * BLOCK, 2 * LANES), jnp.float32),
            pltpu.VMEM((2 * stored, 128), jnp.float32),
            pltpu.VMEM((128, 128), jnp.float32),
            pltpu.SemaphoreType.DMA((stored,)),
            pltpu.SemaphoreType.DMA((2,)),
            pltpu.SemaphoreType.DMA((stored,)),
        ],
        name="convolve",
        compiler_params=pltpu.CompilerParams(vmem_limit_bytes=28 << 20),
    )(
        where, order, gathered, inv, known, params, in_vmem(spectra), in_hbm(raw),
        *[in_hbm(table) for table in tables],
    )


def forward_terms(at, inputs, conv, params_ref, inv_fwd):
    p = [params_ref[0, row : row + 1, at] for row in range(3)]
    query = inputs * inv_fwd * (p[0] * p[1]) + p[2]
    return inputs + query * conv


def backward_terms(at, saved, sconv, cot, grad_mixed, params_ref, inv_saved):
    p = [params_ref[0, row : row + 1, at] for row in range(7)]
    normed = saved * inv_saved
    mixed_grad = normed * (2.0 * p[0] * p[3] * p[5] * p[0]) + p[0] * (p[6] * p[3] + p[4] * p[5])
    grad_normed = cot * sconv * (p[1] * p[0]) + grad_mixed * mixed_grad
    return cot + inv_saved * grad_normed, grad_normed * normed


def leave_kernel(
    pipe_ref, inv_ref, back_ref, fwd_ref, saved_ref, sconv_ref, cot_ref, params_ref,
    send_ref, cross_ref, inv, acc,
):
    rows, width = fwd_ref.shape[1:]
    inv[...] = rows_to_columns(inv_ref[0:8, :])
    inv_fwd = inv[:, 0:1]
    inv_saved = inv[:, 1:2]

    def backward(send):
        cross = jnp.zeros((rows, LANES), jnp.float32)
        for group in range(width // LANES):
            at = pl.ds(group * LANES, LANES)
            partial, term = backward_terms(
                at,
                saved_ref[0, :, at].astype(jnp.float32),
                sconv_ref[0, :, at].astype(jnp.float32),
                cot_ref[0, :, at].astype(jnp.float32),
                back_ref[group, :rows, LANES:].astype(jnp.float32),
                params_ref,
                inv_saved,
            )
            cross = cross + term
            if send:
                send_ref[0, :, at] = partial.astype(jnp.bfloat16)
        acc[...] = cross

    @pl.when(pipe_ref[0] == 0)
    def _():
        for group in range(width // LANES):
            at = pl.ds(group * LANES, LANES)
            inputs = fwd_ref[0, :, at].astype(jnp.float32)
            conv = back_ref[group, :rows, :LANES].astype(jnp.float32)
            layer = forward_terms(at, inputs, conv, params_ref, inv_fwd)
            send_ref[0, :, at] = layer.astype(jnp.bfloat16)
        backward(False)

    @pl.when(pipe_ref[0] != 0)
    def _():
        backward(True)

    cross = columns_to_rows([jnp.sum(acc[...], axis=1, keepdims=True)])
    cross_ref[...] = cross * (inv_ref[1:2, :] * inv_ref[1:2, :] / D)


def leave(pipe, inv, back, fwd_in, saved_in, saved_conv, grad_out, mix_params):
    return pl.pallas_call(
        leave_kernel,
        out_shape=(
            pltpu.VMEM(fwd_in.shape, jnp.bfloat16),
            pltpu.VMEM((8, 128), jnp.float32),
        ),
        in_specs=[SMEM] + [VMEM] * 7,
        out_specs=(VMEM, VMEM),
        scratch_shapes=[pltpu.VMEM((fwd_in.shape[1], 128), jnp.float32)] * 2,
        name="leave",
        compiler_params=pltpu.CompilerParams(vmem_limit_bytes=24 << 20),
    )(
        pipe, inv, in_vmem(back),
        *[in_vmem(a) for a in (fwd_in, saved_in, saved_conv, grad_out)], mix_params,
    )


def forward_kernel(inv_ref, back_ref, fwd_ref, params_ref, layer_ref, grads_ref, known, inv):
    step = pl.program_id(0)
    rows = fwd_ref.shape[1]

    @pl.when(step == 0)
    def _():
        inv[...] = rows_to_columns(inv_ref[0:8, :])
        total = back_ref[0, rows : rows + 16, :].astype(jnp.float32)
        for index in range(1, back_ref.shape[0]):
            total = total + back_ref[index, rows : rows + 16, :].astype(jnp.float32)
        for row in range(16):
            known[row] = total[row : row + 1, :]

    wide = layer_ref.shape[2]
    groups = wide // LANES
    for group in range(groups):
        own = pl.ds(group * LANES, LANES)
        at = pl.ds(pl.multiple_of(step * wide + group * LANES, LANES), LANES)
        block = step * groups + group
        conv = back_ref[block, :rows, :LANES].astype(jnp.float32)
        inputs = fwd_ref[0, :, at].astype(jnp.float32)
        layer = forward_terms(own, inputs, conv, params_ref, inv[:, 0:1])
        layer_ref[0, :, own] = layer.astype(jnp.bfloat16)

        p = [params_ref[0, row : row + 1, own] for row in range(7)]
        extra = back_ref[block, rows + 16 :, :].astype(jnp.float32)
        extra = extra[:, :LANES] + extra[:, LANES:]
        m0, m1, m2 = extra[0:1], extra[1:2], extra[2:3]
        row = step * (groups // 2) + group // 2
        side = slice(group % 2 * LANES, (group % 2 + 1) * LANES)
        q0, q1 = known[row, :, side], known[row + 8, :, side]
        key_normed = p[0] * p[5] * m2 + p[6] * m1
        value_normed = p[0] * p[3] * m2 + p[4] * m1
        grads = [
            p[1] * q1 + p[3] * key_normed + p[5] * value_normed,
            p[0] * q1,
            q0,
            p[0] * key_normed,
            p[0] * p[5] * m1 + p[6] * m0,
            p[0] * value_normed,
            p[0] * p[3] * m1 + p[4] * m0,
        ]
        grads_ref[0, :, own] = jnp.concatenate(grads, axis=0)


def finish_forward(inv, back, fwd_in, mix_params):
    rows, width = fwd_in.shape[1:]
    wide = 512
    return pl.pallas_call(
        forward_kernel,
        out_shape=(
            jax.ShapeDtypeStruct(fwd_in.shape, jnp.bfloat16),
            jax.ShapeDtypeStruct(mix_params.shape, jnp.float32),
        ),
        grid=(width // wide,),
        in_specs=[VMEM] * 3 + [lane_spec(7, wide)],
        out_specs=(lane_spec(rows, wide), lane_spec(7, wide)),
        scratch_shapes=[
            pltpu.VMEM((16, 1, 2 * LANES), jnp.float32),
            pltpu.VMEM((rows, 128), jnp.float32),
        ],
        name="finish_forward",
        compiler_params=pltpu.CompilerParams(vmem_limit_bytes=16 << 20),
    )(inv, in_vmem(back), in_vmem(fwd_in), mix_params)


def backward_kernel(
    s0, s1, s2, s3, inv_ref, back_ref, saved_ref, sconv_ref, cot_ref, params_ref, peer_ref,
    grad_ref, term_ref, scale, inv,
):
    step = pl.program_id(0)

    @pl.when(step == 0)
    def _():
        scale[...] = rows_to_columns(s0[...] + s1[...] + s2[...] + s3[...])
        inv[...] = rows_to_columns(inv_ref[0:8, :])

    rows, wide = grad_ref.shape[1:]
    for group in range(wide // LANES):
        own = pl.ds(group * LANES, LANES)
        at = pl.ds(pl.multiple_of(step * wide + group * LANES, LANES), LANES)
        saved = saved_ref[0, :, at].astype(jnp.float32)
        partial, _ = backward_terms(
            own,
            saved,
            sconv_ref[0, :, at].astype(jnp.float32),
            cot_ref[0, :, at].astype(jnp.float32),
            back_ref[step * (wide // LANES) + group, :rows, LANES:].astype(jnp.float32),
            params_ref,
            inv[:, 1:2],
        )
        grad_ref[0, :, own] = (partial - saved * scale[:, 0:1]).astype(jnp.bfloat16)
        term_ref[:, at] = peer_ref[0, :, own].astype(jnp.float32) * scale[:, 1:2]


def finish_backward(scales, inv, back, saved_in, saved_conv, grad_out, mix_params, peer_saved):
    rows, width = saved_in.shape[1:]
    wide = 512
    spec = lane_spec(rows, wide)
    return pl.pallas_call(
        backward_kernel,
        out_shape=(
            jax.ShapeDtypeStruct(saved_in.shape, jnp.bfloat16),
            pltpu.VMEM((rows, width), jnp.float32),
        ),
        grid=(width // wide,),
        in_specs=[VMEM] * 9 + [lane_spec(7, wide), spec],
        out_specs=(spec, VMEM),
        scratch_shapes=[pltpu.VMEM((rows, 128), jnp.float32)] * 2,
        name="finish_backward",
        compiler_params=pltpu.CompilerParams(vmem_limit_bytes=16 << 20),
    )(
        *scales, inv, in_vmem(back),
        *[in_vmem(a) for a in (saved_in, saved_conv, grad_out)], mix_params, in_hbm(peer_saved),
    )


def received_kernel(value_ref, term_ref, out_ref):
    wide = out_ref.shape[2]
    for at in range(0, wide, LANES):
        own = pl.ds(at, LANES)
        source = pl.ds(pl.multiple_of(pl.program_id(0) * wide + at, LANES), LANES)
        value = value_ref[0, :, source].astype(jnp.float32)
        out_ref[0, :, own] = (value - term_ref[:, source]).astype(jnp.bfloat16)


def finish_received(value, term):
    rows, width = term.shape
    wide = 512
    return pl.pallas_call(
        received_kernel,
        out_shape=jax.ShapeDtypeStruct(value.shape, jnp.bfloat16),
        grid=(width // wide,),
        in_specs=[VMEM, VMEM],
        out_specs=lane_spec(rows, wide),
        name="received",
        compiler_params=pltpu.CompilerParams(vmem_limit_bytes=8 << 20),
    )(in_vmem(value), in_vmem(term))


def per_device(tables, fwd_in, saved_in, saved_conv, grad_out, filters, mix_params, span_order):
    where = lax.axis_index("seq").astype(jnp.int32).reshape(1)
    pipe = lax.axis_index("pipe").astype(jnp.int32).reshape(1)
    raw, sums = pack(fwd_in, saved_in, grad_out)
    raw = lax.all_to_all(raw, "seq", 0, 0)
    own_sums = sum(over_chan(sums))
    sums = own_sums[:2]
    sums = jnp.concatenate([sums, across(sums, 1)], axis=0)
    chips = [(side, back) for side in range(2) for back in range(4)]
    far = [from_chip(sums, *chip) if any(chip) else sums for chip in chips]
    inv = lax.rsqrt(jnp.concatenate(far, axis=0) / D + EPSILON)
    peer_saved = lax.ppermute(saved_in, "pipe", [(1, 0)])
    spectra = filter_spectra(where, filters, tables)
    known = early(own_sums, saved_in, saved_conv, grad_out)
    back = convolve(where, span_order, gather_order(), raw, inv, known, mix_params, spectra, tables)
    back = lax.all_to_all(back, "seq", 0, 0)
    outgoing, cross = leave(pipe, inv, back, fwd_in, saved_in, saved_conv, grad_out, mix_params)
    peer_cross = lax.ppermute(cross, "pipe", [(1, 0)])
    incoming = lax.ppermute(outgoing, "pipe", [(0, 1), (1, 0)])
    scales = over_chan(jnp.concatenate([cross[:1], peer_cross[:1], cross[:6]], axis=0))
    layer_out, param_grad = finish_forward(inv, back, fwd_in, mix_params)
    input_grad, term = finish_backward(
        scales, inv, back, saved_in, saved_conv, grad_out, mix_params, peer_saved
    )
    received = finish_received(incoming, term)
    return (layer_out, input_grad, param_grad, received)


def solution(mesh):
    tables = transform_tables()
    in_specs = (
        P("pipe", "seq", "chan"),
        P("pipe", "seq", "chan"),
        P("pipe", "seq", "chan"),
        P("pipe", "seq", "chan"),
        P("pipe", None, "chan"),
        P("pipe", None, "chan"),
        P(),
    )
    out_specs = (
        P("pipe", "seq", "chan"),
        P("pipe", "seq", "chan"),
        P("pipe", None, "chan"),
        P("pipe", "seq", "chan"),
    )
    return jax.shard_map(
        functools.partial(per_device, tuple(jnp.asarray(table) for table in tables)),
        mesh=mesh,
        in_specs=in_specs,
        out_specs=out_specs,
        check_vma=False,
    )
```

```python
import functools

import jax
import jax.numpy as jnp
import ml_dtypes
import numpy as np
from jax import lax
from jax.experimental import pallas as pl
from jax.experimental.pallas import tpu as pltpu
from jax.sharding import PartitionSpec as P


D = 8192
EPSILON = 1e-05
BLOCK = 256
LANES = 128


def transform_tables():
    period = 2 * BLOCK
    freq = np.arange(BLOCK)[:, None]
    time = np.arange(BLOCK)[None, :]
    angle = 2.0 * np.pi / period * (freq * time % period)
    real, imag = np.cos(angle), -np.sin(angle)
    imag[0] = np.where(np.arange(BLOCK) % 2 == 0, 1.0, -1.0)
    enter = np.concatenate([real, imag], axis=0)
    angle = 2.0 * np.pi / period * (freq * (time + BLOCK) % period)
    real, imag = 2.0 * np.cos(angle), -2.0 * np.sin(angle)
    real[0] = 1.0
    imag[0] = np.where(np.arange(BLOCK) % 2 == 0, 1.0, -1.0)
    leave = np.concatenate([real, imag], axis=0).T / period
    return tuple(table.astype(np.float32).astype(ml_dtypes.bfloat16) for table in (enter, leave))


def rows_to_columns(rows):
    return jnp.concatenate([rows] * 16, axis=0).T


def columns_to_rows(columns):
    lane = lax.broadcasted_iota(jnp.int32, (128, 128), 1)
    square = jnp.zeros((128, 128), jnp.float32)
    for index, column in enumerate(columns):
        square = jnp.where(lane == index, column, square)
    return square.T[:8]


VMEM = pl.BlockSpec(memory_space=pltpu.VMEM)
SMEM = pl.BlockSpec(memory_space=pltpu.SMEM)


def in_vmem(array):
    return pltpu.with_memory_space_constraint(array, pltpu.VMEM)


HBM = pl.BlockSpec(memory_space=pl.ANY)


def in_hbm(array):
    return pltpu.with_memory_space_constraint(array, pltpu.HBM)


def lane_spec(rows, wide):
    return pl.BlockSpec((1, rows, wide), lambda step, *_: (0, 0, step))


def whole(shape):
    return pl.BlockSpec(shape, lambda step, *_: (0,) * len(shape))


def pack_kernel(fwd_hbm, saved_hbm, cot_hbm, out_hbm, squares_ref, held, in_sem, out_sem):
    rows, width = held.shape[1:]
    steps = in_sem.shape[1]
    wide = width // steps
    sources = (fwd_hbm, saved_hbm, cot_hbm)
    arriving = [
        [
            pltpu.make_async_copy(
                source.at[0, :, pl.ds(step * wide, wide)],
                held.at[index, :, pl.ds(step * wide, wide)],
                in_sem.at[index, step],
            )
            for index, source in enumerate(sources)
        ]
        for step in range(steps)
    ]
    for copies in arriving:
        for copy in copies:
            copy.start()
    leaving = []
    totals = [jnp.zeros((rows, LANES), jnp.float32)] * 2
    for step, copies in enumerate(arriving):
        for index, copy in enumerate(copies):
            copy.wait()
            for group in range(step * wide // LANES, (step + 1) * wide // LANES):
                out = pltpu.make_async_copy(
                    held.at[index, :, pl.ds(group * LANES, LANES)],
                    out_hbm.at[group, pl.ds(index * rows, rows), :],
                    out_sem.at[index, group],
                )
                out.start()
                leaving.append(out)
        for index in range(2):
            for group in range(step * wide // LANES, (step + 1) * wide // LANES):
                value = held[index, :, group * LANES : (group + 1) * LANES].astype(jnp.float32)
                totals[index] = totals[index] + value * value
    squares_ref[...] = columns_to_rows([jnp.sum(total, axis=1, keepdims=True) for total in totals])
    for copy in leaving:
        copy.wait()


def pack(fwd_in, saved_in, grad_out):
    rows, width = fwd_in.shape[1:]
    return pl.pallas_call(
        pack_kernel,
        out_shape=(
            pltpu.HBM((width // LANES, 3 * rows, LANES), jnp.bfloat16),
            jax.ShapeDtypeStruct((8, 128), jnp.float32),
        ),
        in_specs=[HBM] * 3,
        out_specs=(HBM, VMEM),
        scratch_shapes=[
            pltpu.VMEM((3, rows, width), jnp.bfloat16),
            pltpu.SemaphoreType.DMA((3, 4)),
            pltpu.SemaphoreType.DMA((3, width // LANES)),
        ],
        name="pack",
        compiler_params=pltpu.CompilerParams(vmem_limit_bytes=16 << 20),
    )(in_hbm(fwd_in), in_hbm(saved_in), in_hbm(grad_out))


def over_chan(rows):
    count = lax.axis_size("chan")
    got = [rows]
    for apart in range(1, count):
        got.append(
            lax.ppermute(rows, "chan", [(low, (low + apart) % count) for low in range(count)])
        )
    return got


def across(rows, flip):
    count = lax.axis_size("seq")
    return lax.ppermute(rows, "seq", [(low, low ^ flip) for low in range(count)])


def round_ring(rows, apart):
    count = lax.axis_size("seq")
    place = lambda low: low // 8 * 8 + (low + 2 * apart) % 8
    return lax.ppermute(rows, "seq", [(low, place(low)) for low in range(count)])


def gather_order():
    own = lax.axis_index("seq").astype(jnp.int32)
    block = jnp.arange(16, dtype=jnp.int32)
    core = (block ^ own) & 1
    back = (own // 2 - block // 2) % 4
    side = (block // 8) ^ (own // 8)
    return side * 8 + back * 2 + core


def early_kernel(sums_ref, saved_ref, sconv_ref, cot_ref, out_ref, inv):
    step = pl.program_id(0)

    @pl.when(step == 0)
    def _():
        inv[...] = rows_to_columns(lax.rsqrt(sums_ref[...] / D + EPSILON))

    inv_saved = inv[:, 1:2]
    pairs = saved_ref.shape[2] // (2 * LANES)
    half = out_ref.shape[0] // 2
    for pair in range(pairs):
        at = pl.ds(pair * 2 * LANES, 2 * LANES)
        normed = saved_ref[0, :, at].astype(jnp.float32) * inv_saved
        grad_query = cot_ref[0, :, at].astype(jnp.float32) * sconv_ref[0, :, at].astype(jnp.float32)
        row = step * pairs + pair
        out_ref[pl.ds(row, 1), :] = jnp.sum(grad_query, axis=0, keepdims=True)
        out_ref[pl.ds(row + half, 1), :] = jnp.sum(grad_query * normed, axis=0, keepdims=True)


def early(sums, saved_in, saved_conv, grad_out):
    rows, width = saved_in.shape[1:]
    wide = 512
    return pl.pallas_call(
        early_kernel,
        out_shape=jax.ShapeDtypeStruct((width // LANES, 2 * LANES), jnp.float32),
        grid=(width // wide,),
        in_specs=[VMEM] + [lane_spec(rows, wide)] * 3,
        out_specs=whole((width // LANES, 2 * LANES)),
        scratch_shapes=[pltpu.VMEM((rows, 128), jnp.float32)],
        name="early",
        compiler_params=pltpu.CompilerParams(vmem_limit_bytes=12 << 20),
    )(sums, in_hbm(saved_in), in_hbm(saved_conv), in_hbm(grad_out))


def side_by_side(ref, index):
    at = 2 * index * BLOCK
    return jnp.concatenate([ref[at : at + BLOCK, :], ref[at + BLOCK : at + 2 * BLOCK, :]], axis=1)


def filter_kernel(where_ref, taps_ref, enter, filt):
    del where_ref
    freq = lax.broadcasted_iota(jnp.int32, (2 * BLOCK, LANES), 0)
    parity = jnp.where(freq % 2 == 0, 1.0, -1.0)
    earlier = None
    for pair in range(filt.shape[0] // 2):
        pair_spectra = jnp.dot(
            enter[...], side_by_side(taps_ref.at[0], pair), preferred_element_type=jnp.float32
        )
        for side in range(2):
            current = pair_spectra[:, side * LANES : (side + 1) * LANES]
            both = parity * current
            if earlier is not None:
                both = both + earlier
            earlier = current
            filt[2 * pair + side, 0] = both[:BLOCK]
            filt[2 * pair + side, 1] = both[BLOCK:]


def filter_spectra(where, filters, tables):
    length = filters.shape[1]
    shape = (length // BLOCK, 2, BLOCK, LANES)
    return pl.pallas_call(
        filter_kernel,
        out_shape=pltpu.VMEM(shape, jnp.float32),
        grid_spec=pltpu.PrefetchScalarGridSpec(
            num_scalar_prefetch=1,
            grid=(1,),
            in_specs=[pl.BlockSpec((1, length, LANES), lambda step, at: (0, 0, at[0]))]
            + [whole(tables[0].shape)],
            out_specs=VMEM,
        ),
        name="filter_spectra",
        compiler_params=pltpu.CompilerParams(vmem_limit_bytes=16 << 20),
    )(where, in_hbm(filters), in_hbm(tables[0]))


def fold(block):
    return jnp.sum(block.reshape(block.shape[0] // 8, 8, LANES), axis=0)


def conv_kernel(
    where_ref, order_ref, gathered_ref, inv_ref, known_ref, params_ref, filt, raw_hbm, enter_hbm,
    leave_hbm, out_hbm, raw_ref, enter, leave, out_ref, ordered, spectra, product, inv_rows, inv, raw_sem, table_sem, out_sem,
):
    stored = raw_ref.shape[0]
    raw_copies = [
        pltpu.make_async_copy(raw_hbm.at[index], raw_ref.at[index], raw_sem.at[index])
        for index in range(stored)
    ]
    table_copies = [
        pltpu.make_async_copy(source, target, table_sem.at[index])
        for index, (source, target) in enumerate(((enter_hbm, enter), (leave_hbm, leave)))
    ]
    out_copies = [
        pltpu.make_async_copy(out_ref.at[index], out_hbm.at[index], out_sem.at[index])
        for index in range(stored)
    ]
    for copy in raw_copies + table_copies:
        copy.start()
    rows = raw_ref.shape[1] // 3
    blocks = stored * rows // BLOCK
    lanes = pl.ds(pl.multiple_of(where_ref[0] * LANES, LANES), LANES)
    p = [params_ref[0, row : row + 1, lanes] for row in range(7)]

    gains = [p[0] * p[1], p[0] * p[3], p[0] * p[5]]
    for index in range(stored):
        inv_rows[2 * index : 2 * index + 2, :] = inv_ref[pl.ds(2 * gathered_ref[index], 2), :]
    inv[...] = jnp.concatenate([inv_rows[...]] * (128 // (2 * stored)), axis=0).T
    for index in range(stored):
        if index % 4 == 0:
            for copy in raw_copies[index : index + 4]:
                copy.wait()
        at = pl.multiple_of(order_ref[index] * rows, rows)
        inv_fwd = inv[:, 2 * index : 2 * index + 1]
        inv_saved = inv[:, 2 * index + 1 : 2 * index + 2]
        normed = raw_ref[index, :rows, :].astype(jnp.float32) * inv_fwd
        mixed = (normed * gains[1] + p[4]) * (normed * gains[2] + p[6])
        normed = raw_ref[index, rows : 2 * rows, :].astype(jnp.float32) * inv_saved
        cot = raw_ref[index, 2 * rows :, :].astype(jnp.float32)
        ordered[pl.ds(at, rows), :LANES] = mixed.astype(jnp.bfloat16)
        ordered[pl.ds(at, rows), LANES:] = (cot * (normed * gains[0] + p[2])).astype(jnp.bfloat16)

    table_copies[0].wait()
    for index in range(blocks):
        data = ordered[index * BLOCK : (index + 1) * BLOCK, :]
        spectra[index] = jnp.dot(enter[...], data, preferred_element_type=jnp.float32)

    def forward_and_adjoint(low, high, one_product):
        for adjoint in (False, True):
            lanes = slice(LANES, 2 * LANES) if adjoint else slice(0, LANES)
            x_re = [spectra[j, low, lanes] for j in range(blocks)]
            x_im = [spectra[j, high, lanes] for j in range(blocks)]
            for i in range(blocks):
                terms = range(i, blocks) if adjoint else range(i + 1)
                re, im = one_product(adjoint, x_re, x_im, [(abs(i - j), j) for j in terms])
                product[i, low, lanes] = re
                product[i, high, lanes] = im

    def total(terms):
        terms = list(terms)
        return functools.reduce(lambda one, two: one + two, terms)

    def first_tile(adjoint, x_re, x_im, terms):
        f_re = [filt[d, 0, 0:8, :] for d in range(blocks)]
        first = lax.broadcasted_iota(jnp.int32, (8, LANES), 0) == 0
        imag = [filt[d, 1, 0:8, :] for d in range(blocks)]
        f_im = [jnp.where(first, 0.0, value) for value in imag]
        f_nq = [jnp.where(first, value, f_re[d]) for d, value in enumerate(imag)]
        direct = total(f_re[d] * x_re[j] for d, j in terms)
        crossed = total(f_im[d] * x_im[j] for d, j in terms)
        straight = total(f_nq[d] * x_im[j] for d, j in terms)
        turned = total(f_im[d] * x_re[j] for d, j in terms)
        if adjoint:
            return direct + crossed, straight - turned
        return direct - crossed, straight + turned

    forward_and_adjoint(slice(0, 8), slice(BLOCK, BLOCK + 8), first_tile)

    def products(tile, carry):
        low = pl.ds(pl.multiple_of(tile * 8, 8), 8)
        high = pl.ds(pl.multiple_of(BLOCK + tile * 8, 8), 8)
        f_re = [filt[d, 0, low, :] for d in range(blocks)]
        f_im = [filt[d, 1, low, :] for d in range(blocks)]
        f_less = [f_im[d] - f_re[d] for d in range(blocks)]
        f_more = [f_im[d] + f_re[d] for d in range(blocks)]

        def other_tile(adjoint, x_re, x_im, terms):
            both = total(f_re[d] * (x_re[j] + x_im[j]) for d, j in terms)
            if adjoint:
                return (
                    both + total(f_less[d] * x_im[j] for d, j in terms),
                    both - total(f_more[d] * x_re[j] for d, j in terms),
                )
            return (
                both - total(f_more[d] * x_im[j] for d, j in terms),
                both + total(f_less[d] * x_re[j] for d, j in terms),
            )

        forward_and_adjoint(low, high, other_tile)
        return carry

    lax.fori_loop(1, BLOCK // 8, products, 0)

    table_copies[1].wait()
    for index in range(blocks):
        left = jnp.dot(
            leave[...], product[index].astype(jnp.bfloat16), preferred_element_type=jnp.float32
        )
        ordered[index * BLOCK : (index + 1) * BLOCK, :] = left.astype(jnp.bfloat16)

    sums = [jnp.zeros((8, LANES), jnp.float32)] * 3
    for index in range(stored):
        at = pl.multiple_of(order_ref[index] * rows, rows)
        block = ordered[pl.ds(at, rows), :]
        out_ref[index, :rows, :] = block
        grad_mixed = block[:, LANES:].astype(jnp.float32)
        inv_saved = inv[:, 2 * index + 1 : 2 * index + 2]
        normed = raw_ref[index, rows : 2 * rows, :].astype(jnp.float32) * inv_saved
        once = grad_mixed * normed
        for power, term in enumerate((grad_mixed, once, once * normed)):
            sums[power] = sums[power] + fold(term)

    sums = jnp.concatenate(
        [jnp.sum(total, axis=0, keepdims=True) for total in sums]
        + [jnp.zeros((5, LANES), jnp.float32)],
        axis=0,
    )
    known = known_ref[...].astype(jnp.bfloat16)
    top = sums.astype(jnp.bfloat16)
    rest = (sums - top.astype(jnp.float32)).astype(jnp.bfloat16)
    for index in range(stored):
        out_ref[index, rows : rows + 16, :] = known
        out_ref[index, rows + 16 :, :LANES] = top
        out_ref[index, rows + 16 :, LANES:] = rest
        out_copies[index].start()
    for copy in out_copies:
        copy.wait()


def convolve(where, order, gathered, raw, inv, known, params, spectra, tables):
    stored = raw.shape[0]
    rows = raw.shape[1] // 3
    length = stored * rows
    blocks = length // BLOCK
    return pl.pallas_call(
        conv_kernel,
        out_shape=pltpu.HBM((stored, rows + 24, 2 * LANES), jnp.bfloat16),
        in_specs=[SMEM] * 3 + [VMEM] * 4 + [HBM] * 3,
        out_specs=HBM,
        scratch_shapes=[
            pltpu.VMEM(raw.shape, jnp.bfloat16),
            pltpu.VMEM((2 * BLOCK, BLOCK), jnp.bfloat16),
            pltpu.VMEM((BLOCK, 2 * BLOCK), jnp.bfloat16),
            pltpu.VMEM((stored, rows + 24, 2 * LANES), jnp.bfloat16),
            pltpu.VMEM((length, 2 * LANES), jnp.bfloat16),
            pltpu.VMEM((blocks, 2 * BLOCK, 2 * LANES), jnp.float32),
            pltpu.VMEM((blocks, 2 * BLOCK, 2 * LANES), jnp.float32),
            pltpu.VMEM((2 * stored, 128), jnp.float32),
            pltpu.VMEM((128, 128), jnp.float32),
            pltpu.SemaphoreType.DMA((stored,)),
            pltpu.SemaphoreType.DMA((2,)),
            pltpu.SemaphoreType.DMA((stored,)),
        ],
        name="convolve",
        compiler_params=pltpu.CompilerParams(vmem_limit_bytes=28 << 20),
    )(
        where, order, gathered, inv, known, params, in_vmem(spectra), in_hbm(raw),
        *[in_hbm(table) for table in tables],
    )


def forward_terms(at, inputs, conv, params_ref, inv_fwd):
    p = [params_ref[0, row : row + 1, at] for row in range(3)]
    query = inputs * inv_fwd * (p[0] * p[1]) + p[2]
    return inputs + query * conv


def backward_terms(at, saved, sconv, cot, grad_mixed, params_ref, inv_saved):
    p = [params_ref[0, row : row + 1, at] for row in range(7)]
    normed = saved * inv_saved
    mixed_grad = normed * (2.0 * p[0] * p[3] * p[5] * p[0]) + p[0] * (p[6] * p[3] + p[4] * p[5])
    grad_normed = cot * sconv * (p[1] * p[0]) + grad_mixed * mixed_grad
    return cot + inv_saved * grad_normed, grad_normed * normed


def leave_kernel(
    pipe_ref, inv_ref, back_ref, fwd_hbm, saved_ref, sconv_ref, cot_ref, params_ref,
    send_ref, keep_ref, cross_ref, inv, acc, fwd_ref, fwd_sem,
):
    rows, width = fwd_ref.shape[1:]
    fwd_copy = pltpu.make_async_copy(fwd_hbm, fwd_ref, fwd_sem)
    fwd_copy.start()
    inv[...] = rows_to_columns(inv_ref[0:8, :])
    inv_fwd = inv[:, 0:1]
    inv_saved = inv[:, 1:2]

    def both(layer_ref, partial_ref):
        cross = jnp.zeros((rows, LANES), jnp.float32)
        for group in range(width // LANES):
            at = pl.ds(group * LANES, LANES)
            partial, term = backward_terms(
                at,
                saved_ref[0, :, at].astype(jnp.float32),
                sconv_ref[0, :, at].astype(jnp.float32),
                cot_ref[0, :, at].astype(jnp.float32),
                back_ref[group, :rows, LANES:].astype(jnp.float32),
                params_ref,
                inv_saved,
            )
            cross = cross + term
            partial_ref[0, :, at] = partial.astype(jnp.bfloat16)
        acc[...] = cross
        fwd_copy.wait()
        for group in range(width // LANES):
            at = pl.ds(group * LANES, LANES)
            inputs = fwd_ref[0, :, at].astype(jnp.float32)
            conv = back_ref[group, :rows, :LANES].astype(jnp.float32)
            layer = forward_terms(at, inputs, conv, params_ref, inv_fwd)
            layer_ref[0, :, at] = layer.astype(jnp.bfloat16)

    @pl.when(pipe_ref[0] == 0)
    def _():
        both(send_ref, keep_ref)

    @pl.when(pipe_ref[0] != 0)
    def _():
        both(keep_ref, send_ref)

    cross = columns_to_rows([jnp.sum(acc[...], axis=1, keepdims=True)])
    cross_ref[...] = cross * (inv_ref[1:2, :] * inv_ref[1:2, :] / D)


def leave(pipe, inv, back, fwd_in, saved_in, saved_conv, grad_out, mix_params):
    return pl.pallas_call(
        leave_kernel,
        out_shape=(
            pltpu.VMEM(fwd_in.shape, jnp.bfloat16),
            pltpu.VMEM(fwd_in.shape, jnp.bfloat16),
            pltpu.VMEM((8, 128), jnp.float32),
        ),
        in_specs=[SMEM] + [VMEM] * 2 + [HBM] + [VMEM] * 4,
        out_specs=(VMEM, VMEM, VMEM),
        scratch_shapes=[pltpu.VMEM((fwd_in.shape[1], 128), jnp.float32)] * 2
        + [pltpu.VMEM(fwd_in.shape, jnp.bfloat16), pltpu.SemaphoreType.DMA],
        name="leave",
        compiler_params=pltpu.CompilerParams(vmem_limit_bytes=24 << 20),
    )(
        pipe, inv, in_vmem(back), in_hbm(fwd_in),
        *[in_vmem(a) for a in (saved_in, saved_conv, grad_out)], mix_params,
    )


def finish_kernel(
    pipe_ref, s0, s1, s2, s3, back_ref, send_ref, keep_ref, saved_ref, params_ref, peer_ref,
    layer_hbm, grad_ref, grads_ref, term_ref, scale, known, layer_sem,
):
    step = pl.program_id(0)
    first = pipe_ref[0] == 0
    rows, wide = grad_ref.shape[1:]
    sent = pltpu.make_async_copy(send_ref, layer_hbm, layer_sem)
    kept = pltpu.make_async_copy(keep_ref, layer_hbm, layer_sem)

    @pl.when(step == 0)
    def _():
        @pl.when(first)
        def _():
            sent.start()

        @pl.when(jnp.logical_not(first))
        def _():
            kept.start()

        scale[...] = rows_to_columns(s0[...] + s1[...] + s2[...] + s3[...])
        total = back_ref[0, rows : rows + 16, :].astype(jnp.float32)
        for index in range(1, back_ref.shape[0]):
            total = total + back_ref[index, rows : rows + 16, :].astype(jnp.float32)
        for row in range(16):
            known[row] = total[row : row + 1, :]

    groups = wide // LANES
    for group in range(groups):
        own = pl.ds(group * LANES, LANES)
        at = pl.ds(pl.multiple_of(step * wide + group * LANES, LANES), LANES)
        partial = jnp.where(first, keep_ref[0, :, at], send_ref[0, :, at]).astype(jnp.float32)
        saved = saved_ref[0, :, at].astype(jnp.float32)
        grad_ref[0, :, own] = (partial - saved * scale[:, 0:1]).astype(jnp.bfloat16)
        term_ref[:, at] = peer_ref[0, :, own].astype(jnp.float32) * scale[:, 1:2]

        p = [params_ref[0, row : row + 1, own] for row in range(7)]
        extra = back_ref[step * groups + group, rows + 16 :, :].astype(jnp.float32)
        extra = extra[:, :LANES] + extra[:, LANES:]
        m0, m1, m2 = extra[0:1], extra[1:2], extra[2:3]
        row = step * (groups // 2) + group // 2
        side = slice(group % 2 * LANES, (group % 2 + 1) * LANES)
        q0, q1 = known[row, :, side], known[row + 8, :, side]
        key_normed = p[0] * p[5] * m2 + p[6] * m1
        value_normed = p[0] * p[3] * m2 + p[4] * m1
        grads = [
            p[1] * q1 + p[3] * key_normed + p[5] * value_normed,
            p[0] * q1,
            q0,
            p[0] * key_normed,
            p[0] * p[5] * m1 + p[6] * m0,
            p[0] * value_normed,
            p[0] * p[3] * m1 + p[4] * m0,
        ]
        grads_ref[0, :, own] = jnp.concatenate(grads, axis=0)

    @pl.when(step == pl.num_programs(0) - 1)
    def _():
        @pl.when(first)
        def _():
            sent.wait()

        @pl.when(jnp.logical_not(first))
        def _():
            kept.wait()


def finish(pipe, scales, back, send, keep, saved_in, mix_params, peer_saved):
    rows, width = saved_in.shape[1:]
    wide = 512
    spec, params = lane_spec(rows, wide), lane_spec(7, wide)
    return pl.pallas_call(
        finish_kernel,
        out_shape=(
            pltpu.HBM(saved_in.shape, jnp.bfloat16),
            jax.ShapeDtypeStruct(saved_in.shape, jnp.bfloat16),
            jax.ShapeDtypeStruct(mix_params.shape, jnp.float32),
            pltpu.VMEM((rows, width), jnp.float32),
        ),
        grid=(width // wide,),
        in_specs=[SMEM] + [VMEM] * 8 + [params, spec],
        out_specs=(HBM, spec, params, VMEM),
        scratch_shapes=[
            pltpu.VMEM((rows, 128), jnp.float32),
            pltpu.VMEM((16, 1, 2 * LANES), jnp.float32),
            pltpu.SemaphoreType.DMA,
        ],
        name="finish",
        compiler_params=pltpu.CompilerParams(vmem_limit_bytes=16 << 20),
    )(
        pipe, *scales, in_vmem(back), in_vmem(send), in_vmem(keep), in_vmem(saved_in),
        mix_params, in_hbm(peer_saved),
    )


def received_kernel(value_ref, term_ref, out_ref):
    wide = out_ref.shape[2]
    for at in range(0, wide, LANES):
        own = pl.ds(at, LANES)
        source = pl.ds(pl.multiple_of(pl.program_id(0) * wide + at, LANES), LANES)
        value = value_ref[0, :, source].astype(jnp.float32)
        out_ref[0, :, own] = (value - term_ref[:, source]).astype(jnp.bfloat16)


def finish_received(value, term):
    rows, width = term.shape
    wide = 512
    return pl.pallas_call(
        received_kernel,
        out_shape=jax.ShapeDtypeStruct(value.shape, jnp.bfloat16),
        grid=(width // wide,),
        in_specs=[VMEM, VMEM],
        out_specs=lane_spec(rows, wide),
        name="received",
        compiler_params=pltpu.CompilerParams(vmem_limit_bytes=8 << 20),
    )(in_vmem(value), in_vmem(term))


def per_device(tables, fwd_in, saved_in, saved_conv, grad_out, filters, mix_params, span_order):
    where = lax.axis_index("seq").astype(jnp.int32).reshape(1)
    pipe = lax.axis_index("pipe").astype(jnp.int32).reshape(1)
    raw, sums = pack(fwd_in, saved_in, grad_out)
    raw = lax.all_to_all(raw, "seq", 0, 0)
    own_sums = sum(over_chan(sums))
    sums = own_sums[:2]
    sums = jnp.concatenate([sums, across(sums, 1)], axis=0)
    sums = jnp.concatenate([sums] + [round_ring(sums, apart) for apart in (1, 2, 3)], axis=0)
    inv = lax.rsqrt(jnp.concatenate([sums, across(sums, 8)], axis=0) / D + EPSILON)
    peer_saved = lax.ppermute(saved_in, "pipe", [(1, 0)])
    spectra = filter_spectra(where, filters, tables)
    known = early(own_sums, saved_in, saved_conv, grad_out)
    back = convolve(where, span_order, gather_order(), raw, inv, known, mix_params, spectra, tables)
    back = lax.all_to_all(back, "seq", 0, 0)
    outgoing, keep, cross = leave(
        pipe, inv, back, fwd_in, saved_in, saved_conv, grad_out, mix_params
    )
    peer_cross = lax.ppermute(cross, "pipe", [(1, 0)])
    incoming = lax.ppermute(outgoing, "pipe", [(0, 1), (1, 0)])
    scales = over_chan(jnp.concatenate([cross[:1], peer_cross[:1], cross[:6]], axis=0))
    layer_out, input_grad, param_grad, term = finish(
        pipe, scales, back, outgoing, keep, saved_in, mix_params, peer_saved
    )
    received = finish_received(incoming, term)
    return (layer_out, input_grad, param_grad, received)


def solution(mesh):
    tables = transform_tables()
    in_specs = (
        P("pipe", "seq", "chan"),
        P("pipe", "seq", "chan"),
        P("pipe", "seq", "chan"),
        P("pipe", "seq", "chan"),
        P("pipe", None, "chan"),
        P("pipe", None, "chan"),
        P(),
    )
    out_specs = (
        P("pipe", "seq", "chan"),
        P("pipe", "seq", "chan"),
        P("pipe", None, "chan"),
        P("pipe", "seq", "chan"),
    )
    return jax.shard_map(
        functools.partial(per_device, tuple(jnp.asarray(table) for table in tables)),
        mesh=mesh,
        in_specs=in_specs,
        out_specs=out_specs,
        check_vma=False,
    )
```

```python
import functools

import jax
import jax.numpy as jnp
import ml_dtypes
import numpy as np
from jax import lax
from jax.experimental import pallas as pl
from jax.experimental.pallas import tpu as pltpu
from jax.sharding import PartitionSpec as P


D = 8192
EPSILON = 1e-05
BLOCK = 256
LANES = 128


def transform_tables():
    period = 2 * BLOCK
    freq = np.arange(BLOCK)[:, None]
    time = np.arange(BLOCK)[None, :]
    angle = 2.0 * np.pi / period * (freq * time % period)
    real, imag = np.cos(angle), -np.sin(angle)
    imag[0] = np.where(np.arange(BLOCK) % 2 == 0, 1.0, -1.0)
    enter = np.concatenate([real, imag], axis=0)
    angle = 2.0 * np.pi / period * (freq * (time + BLOCK) % period)
    real, imag = 2.0 * np.cos(angle), -2.0 * np.sin(angle)
    real[0] = 1.0
    imag[0] = np.where(np.arange(BLOCK) % 2 == 0, 1.0, -1.0)
    leave = np.concatenate([real, imag], axis=0).T / period
    return tuple(table.astype(np.float32).astype(ml_dtypes.bfloat16) for table in (enter, leave))


def rows_to_columns(rows):
    return jnp.concatenate([rows] * 16, axis=0).T


def columns_to_rows(columns):
    lane = lax.broadcasted_iota(jnp.int32, (128, 128), 1)
    square = jnp.zeros((128, 128), jnp.float32)
    for index, column in enumerate(columns):
        square = jnp.where(lane == index, column, square)
    return square.T[:8]


VMEM = pl.BlockSpec(memory_space=pltpu.VMEM)
SMEM = pl.BlockSpec(memory_space=pltpu.SMEM)


def in_vmem(array):
    return pltpu.with_memory_space_constraint(array, pltpu.VMEM)


HBM = pl.BlockSpec(memory_space=pl.ANY)


def in_hbm(array):
    return pltpu.with_memory_space_constraint(array, pltpu.HBM)


def lane_spec(rows, wide):
    return pl.BlockSpec((1, rows, wide), lambda step, *_: (0, 0, step))


def whole(shape):
    return pl.BlockSpec(shape, lambda step, *_: (0,) * len(shape))


def pack_kernel(fwd_hbm, saved_hbm, cot_hbm, out_hbm, squares_ref, held, in_sem, out_sem):
    rows, width = held.shape[1:]
    steps = in_sem.shape[1]
    wide = width // steps
    sources = (fwd_hbm, saved_hbm, cot_hbm)
    arriving = [
        [
            pltpu.make_async_copy(
                source.at[0, :, pl.ds(step * wide, wide)],
                held.at[index, :, pl.ds(step * wide, wide)],
                in_sem.at[index, step],
            )
            for index, source in enumerate(sources)
        ]
        for step in range(steps)
    ]
    for copies in arriving:
        for copy in copies:
            copy.start()
    leaving = []
    totals = [jnp.zeros((rows, LANES), jnp.float32)] * 2
    for step, copies in enumerate(arriving):
        for index, copy in enumerate(copies):
            copy.wait()
            for group in range(step * wide // LANES, (step + 1) * wide // LANES):
                out = pltpu.make_async_copy(
                    held.at[index, :, pl.ds(group * LANES, LANES)],
                    out_hbm.at[group, pl.ds(index * rows, rows), :],
                    out_sem.at[index, group],
                )
                out.start()
                leaving.append(out)
        for index in range(2):
            for group in range(step * wide // LANES, (step + 1) * wide // LANES):
                value = held[index, :, group * LANES : (group + 1) * LANES].astype(jnp.float32)
                totals[index] = totals[index] + value * value
    squares_ref[...] = columns_to_rows([jnp.sum(total, axis=1, keepdims=True) for total in totals])
    for copy in leaving:
        copy.wait()


def pack(fwd_in, saved_in, grad_out):
    rows, width = fwd_in.shape[1:]
    return pl.pallas_call(
        pack_kernel,
        out_shape=(
            pltpu.HBM((width // LANES, 3 * rows, LANES), jnp.bfloat16),
            jax.ShapeDtypeStruct((8, 128), jnp.float32),
        ),
        in_specs=[HBM] * 3,
        out_specs=(HBM, VMEM),
        scratch_shapes=[
            pltpu.VMEM((3, rows, width), jnp.bfloat16),
            pltpu.SemaphoreType.DMA((3, 4)),
            pltpu.SemaphoreType.DMA((3, width // LANES)),
        ],
        name="pack",
        compiler_params=pltpu.CompilerParams(vmem_limit_bytes=16 << 20),
    )(in_hbm(fwd_in), in_hbm(saved_in), in_hbm(grad_out))


def over_chan(rows):
    count = lax.axis_size("chan")
    got = [rows]
    for apart in range(1, count):
        got.append(
            lax.ppermute(rows, "chan", [(low, (low + apart) % count) for low in range(count)])
        )
    return got


def across(rows, flip):
    count = lax.axis_size("seq")
    return lax.ppermute(rows, "seq", [(low, low ^ flip) for low in range(count)])


def round_ring(rows, apart):
    count = lax.axis_size("seq")
    place = lambda low: low // 8 * 8 + (low + 2 * apart) % 8
    return lax.ppermute(rows, "seq", [(low, place(low)) for low in range(count)])


def gather_order():
    own = lax.axis_index("seq").astype(jnp.int32)
    block = jnp.arange(16, dtype=jnp.int32)
    core = (block ^ own) & 1
    back = (own // 2 - block // 2) % 4
    side = (block // 8) ^ (own // 8)
    return side * 8 + back * 2 + core


def early_kernel(sums_ref, saved_ref, sconv_ref, cot_ref, out_ref, inv):
    step = pl.program_id(0)

    @pl.when(step == 0)
    def _():
        inv[...] = rows_to_columns(lax.rsqrt(sums_ref[...] / D + EPSILON))

    inv_saved = inv[:, 1:2]
    pairs = saved_ref.shape[2] // (2 * LANES)
    half = out_ref.shape[0] // 2
    for pair in range(pairs):
        at = pl.ds(pair * 2 * LANES, 2 * LANES)
        normed = saved_ref[0, :, at].astype(jnp.float32) * inv_saved
        grad_query = cot_ref[0, :, at].astype(jnp.float32) * sconv_ref[0, :, at].astype(jnp.float32)
        row = step * pairs + pair
        out_ref[pl.ds(row, 1), :] = jnp.sum(grad_query, axis=0, keepdims=True)
        out_ref[pl.ds(row + half, 1), :] = jnp.sum(grad_query * normed, axis=0, keepdims=True)


def early(sums, saved_in, saved_conv, grad_out):
    rows, width = saved_in.shape[1:]
    wide = 512
    return pl.pallas_call(
        early_kernel,
        out_shape=jax.ShapeDtypeStruct((width // LANES, 2 * LANES), jnp.float32),
        grid=(width // wide,),
        in_specs=[VMEM] + [lane_spec(rows, wide)] * 3,
        out_specs=whole((width // LANES, 2 * LANES)),
        scratch_shapes=[pltpu.VMEM((rows, 128), jnp.float32)],
        name="early",
        compiler_params=pltpu.CompilerParams(vmem_limit_bytes=12 << 20),
    )(sums, in_hbm(saved_in), in_hbm(saved_conv), in_hbm(grad_out))


def side_by_side(ref, index):
    at = 2 * index * BLOCK
    return jnp.concatenate([ref[at : at + BLOCK, :], ref[at + BLOCK : at + 2 * BLOCK, :]], axis=1)


def filter_kernel(where_ref, taps_ref, enter, filt):
    del where_ref
    freq = lax.broadcasted_iota(jnp.int32, (2 * BLOCK, LANES), 0)
    parity = jnp.where(freq % 2 == 0, 1.0, -1.0)
    earlier = None
    for pair in range(filt.shape[0] // 2):
        pair_spectra = jnp.dot(
            enter[...], side_by_side(taps_ref.at[0], pair), preferred_element_type=jnp.float32
        )
        for side in range(2):
            current = pair_spectra[:, side * LANES : (side + 1) * LANES]
            both = parity * current
            if earlier is not None:
                both = both + earlier
            earlier = current
            filt[2 * pair + side, 0] = both[:BLOCK]
            filt[2 * pair + side, 1] = both[BLOCK:]


def filter_spectra(where, filters, tables):
    length = filters.shape[1]
    shape = (length // BLOCK, 2, BLOCK, LANES)
    return pl.pallas_call(
        filter_kernel,
        out_shape=pltpu.HBM(shape, jnp.float32),
        grid_spec=pltpu.PrefetchScalarGridSpec(
            num_scalar_prefetch=1,
            grid=(1,),
            in_specs=[pl.BlockSpec((1, length, LANES), lambda step, at: (0, 0, at[0]))]
            + [whole(tables[0].shape)],
            out_specs=whole(shape),
        ),
        name="filter_spectra",
        compiler_params=pltpu.CompilerParams(vmem_limit_bytes=16 << 20),
    )(where, in_hbm(filters), in_hbm(tables[0]))


def fold(block):
    return jnp.sum(block.reshape(block.shape[0] // 8, 8, LANES), axis=0)


def conv_kernel(
    where_ref, order_ref, gathered_ref, inv_ref, known_ref, params_ref, filt_hbm, raw_hbm, enter_hbm,
    leave_hbm, out_hbm, raw_ref, filt, enter, leave, out_ref, ordered, spectra, product, inv_rows, inv, raw_sem, table_sem, out_sem,
):
    stored = raw_ref.shape[0]
    raw_copies = [
        pltpu.make_async_copy(raw_hbm.at[index], raw_ref.at[index], raw_sem.at[index])
        for index in range(stored)
    ]
    table_copies = [
        pltpu.make_async_copy(source, target, table_sem.at[index])
        for index, (source, target) in enumerate(
            ((enter_hbm, enter), (leave_hbm, leave), (filt_hbm, filt))
        )
    ]
    out_copies = [
        pltpu.make_async_copy(out_ref.at[index], out_hbm.at[index], out_sem.at[index])
        for index in range(stored)
    ]
    for copy in raw_copies + table_copies:
        copy.start()
    rows = raw_ref.shape[1] // 3
    blocks = stored * rows // BLOCK
    lanes = pl.ds(pl.multiple_of(where_ref[0] * LANES, LANES), LANES)
    p = [params_ref[0, row : row + 1, lanes] for row in range(7)]

    gains = [p[0] * p[1], p[0] * p[3], p[0] * p[5]]
    for index in range(stored):
        inv_rows[2 * index : 2 * index + 2, :] = inv_ref[pl.ds(2 * gathered_ref[index], 2), :]
    inv[...] = jnp.concatenate([inv_rows[...]] * (128 // (2 * stored)), axis=0).T
    for index in range(stored):
        if index % 4 == 0:
            for copy in raw_copies[index : index + 4]:
                copy.wait()
        at = pl.multiple_of(order_ref[index] * rows, rows)
        inv_fwd = inv[:, 2 * index : 2 * index + 1]
        inv_saved = inv[:, 2 * index + 1 : 2 * index + 2]
        normed = raw_ref[index, :rows, :].astype(jnp.float32) * inv_fwd
        mixed = (normed * gains[1] + p[4]) * (normed * gains[2] + p[6])
        normed = raw_ref[index, rows : 2 * rows, :].astype(jnp.float32) * inv_saved
        cot = raw_ref[index, 2 * rows :, :].astype(jnp.float32)
        ordered[pl.ds(at, rows), :LANES] = mixed.astype(jnp.bfloat16)
        ordered[pl.ds(at, rows), LANES:] = (cot * (normed * gains[0] + p[2])).astype(jnp.bfloat16)

    table_copies[0].wait()
    for index in range(blocks):
        data = ordered[index * BLOCK : (index + 1) * BLOCK, :]
        spectra[index] = jnp.dot(enter[...], data, preferred_element_type=jnp.float32)

    table_copies[2].wait()

    def forward_and_adjoint(low, high, one_product):
        for adjoint in (False, True):
            lanes = slice(LANES, 2 * LANES) if adjoint else slice(0, LANES)
            x_re = [spectra[j, low, lanes] for j in range(blocks)]
            x_im = [spectra[j, high, lanes] for j in range(blocks)]
            for i in range(blocks):
                terms = range(i, blocks) if adjoint else range(i + 1)
                re, im = one_product(adjoint, x_re, x_im, [(abs(i - j), j) for j in terms])
                product[i, low, lanes] = re
                product[i, high, lanes] = im

    def total(terms):
        terms = list(terms)
        return functools.reduce(lambda one, two: one + two, terms)

    def first_tile(adjoint, x_re, x_im, terms):
        f_re = [filt[d, 0, 0:8, :] for d in range(blocks)]
        first = lax.broadcasted_iota(jnp.int32, (8, LANES), 0) == 0
        imag = [filt[d, 1, 0:8, :] for d in range(blocks)]
        f_im = [jnp.where(first, 0.0, value) for value in imag]
        f_nq = [jnp.where(first, value, f_re[d]) for d, value in enumerate(imag)]
        direct = total(f_re[d] * x_re[j] for d, j in terms)
        crossed = total(f_im[d] * x_im[j] for d, j in terms)
        straight = total(f_nq[d] * x_im[j] for d, j in terms)
        turned = total(f_im[d] * x_re[j] for d, j in terms)
        if adjoint:
            return direct + crossed, straight - turned
        return direct - crossed, straight + turned

    forward_and_adjoint(slice(0, 8), slice(BLOCK, BLOCK + 8), first_tile)

    def products(tile, carry):
        low = pl.ds(pl.multiple_of(tile * 8, 8), 8)
        high = pl.ds(pl.multiple_of(BLOCK + tile * 8, 8), 8)
        f_re = [filt[d, 0, low, :] for d in range(blocks)]
        f_im = [filt[d, 1, low, :] for d in range(blocks)]
        f_less = [f_im[d] - f_re[d] for d in range(blocks)]
        f_more = [f_im[d] + f_re[d] for d in range(blocks)]

        def other_tile(adjoint, x_re, x_im, terms):
            both = total(f_re[d] * (x_re[j] + x_im[j]) for d, j in terms)
            if adjoint:
                return (
                    both + total(f_less[d] * x_im[j] for d, j in terms),
                    both - total(f_more[d] * x_re[j] for d, j in terms),
                )
            return (
                both - total(f_more[d] * x_im[j] for d, j in terms),
                both + total(f_less[d] * x_re[j] for d, j in terms),
            )

        forward_and_adjoint(low, high, other_tile)
        return carry

    lax.fori_loop(1, BLOCK // 8, products, 0)

    table_copies[1].wait()
    for index in range(blocks):
        left = jnp.dot(
            leave[...], product[index].astype(jnp.bfloat16), preferred_element_type=jnp.float32
        )
        ordered[index * BLOCK : (index + 1) * BLOCK, :] = left.astype(jnp.bfloat16)

    sums = [jnp.zeros((8, LANES), jnp.float32)] * 3
    for index in range(stored):
        at = pl.multiple_of(order_ref[index] * rows, rows)
        block = ordered[pl.ds(at, rows), :]
        out_ref[index, :rows, :] = block
        grad_mixed = block[:, LANES:].astype(jnp.float32)
        inv_saved = inv[:, 2 * index + 1 : 2 * index + 2]
        normed = raw_ref[index, rows : 2 * rows, :].astype(jnp.float32) * inv_saved
        once = grad_mixed * normed
        for power, term in enumerate((grad_mixed, once, once * normed)):
            sums[power] = sums[power] + fold(term)

    sums = jnp.concatenate(
        [jnp.sum(total, axis=0, keepdims=True) for total in sums]
        + [jnp.zeros((5, LANES), jnp.float32)],
        axis=0,
    )
    known = known_ref[...].astype(jnp.bfloat16)
    top = sums.astype(jnp.bfloat16)
    rest = (sums - top.astype(jnp.float32)).astype(jnp.bfloat16)
    for index in range(stored):
        out_ref[index, rows : rows + 16, :] = known
        out_ref[index, rows + 16 :, :LANES] = top
        out_ref[index, rows + 16 :, LANES:] = rest
        out_copies[index].start()
    for copy in out_copies:
        copy.wait()


def convolve(where, order, gathered, raw, inv, known, params, spectra, tables):
    stored = raw.shape[0]
    rows = raw.shape[1] // 3
    length = stored * rows
    blocks = length // BLOCK
    return pl.pallas_call(
        conv_kernel,
        out_shape=pltpu.HBM((stored, rows + 24, 2 * LANES), jnp.bfloat16),
        in_specs=[SMEM] * 3 + [VMEM] * 3 + [HBM] * 4,
        out_specs=HBM,
        scratch_shapes=[
            pltpu.VMEM(raw.shape, jnp.bfloat16),
            pltpu.VMEM(spectra.shape, jnp.float32),
            pltpu.VMEM((2 * BLOCK, BLOCK), jnp.bfloat16),
            pltpu.VMEM((BLOCK, 2 * BLOCK), jnp.bfloat16),
            pltpu.VMEM((stored, rows + 24, 2 * LANES), jnp.bfloat16),
            pltpu.VMEM((length, 2 * LANES), jnp.bfloat16),
            pltpu.VMEM((blocks, 2 * BLOCK, 2 * LANES), jnp.float32),
            pltpu.VMEM((blocks, 2 * BLOCK, 2 * LANES), jnp.float32),
            pltpu.VMEM((2 * stored, 128), jnp.float32),
            pltpu.VMEM((128, 128), jnp.float32),
            pltpu.SemaphoreType.DMA((stored,)),
            pltpu.SemaphoreType.DMA((3,)),
            pltpu.SemaphoreType.DMA((stored,)),
        ],
        name="convolve",
        compiler_params=pltpu.CompilerParams(vmem_limit_bytes=28 << 20),
    )(
        where, order, gathered, inv, known, params, in_hbm(spectra), in_hbm(raw),
        *[in_hbm(table) for table in tables],
    )


def forward_terms(at, inputs, conv, params_ref, inv_fwd):
    p = [params_ref[0, row : row + 1, at] for row in range(3)]
    query = inputs * inv_fwd * (p[0] * p[1]) + p[2]
    return inputs + query * conv


def backward_terms(at, saved, sconv, cot, grad_mixed, params_ref, inv_saved):
    p = [params_ref[0, row : row + 1, at] for row in range(7)]
    normed = saved * inv_saved
    mixed_grad = normed * (2.0 * p[0] * p[3] * p[5] * p[0]) + p[0] * (p[6] * p[3] + p[4] * p[5])
    grad_normed = cot * sconv * (p[1] * p[0]) + grad_mixed * mixed_grad
    return cot + inv_saved * grad_normed, grad_normed * normed


def leave_kernel(
    pipe_ref, inv_ref, back_ref, fwd_hbm, saved_ref, sconv_ref, cot_ref, params_ref,
    send_ref, keep_ref, cross_ref, inv, acc, fwd_ref, fwd_sem,
):
    rows, width = fwd_ref.shape[1:]
    fwd_copy = pltpu.make_async_copy(fwd_hbm, fwd_ref, fwd_sem)
    fwd_copy.start()
    inv[...] = rows_to_columns(inv_ref[0:8, :])
    inv_fwd = inv[:, 0:1]
    inv_saved = inv[:, 1:2]

    def both(layer_ref, partial_ref):
        cross = jnp.zeros((rows, LANES), jnp.float32)
        for group in range(width // LANES):
            at = pl.ds(group * LANES, LANES)
            partial, term = backward_terms(
                at,
                saved_ref[0, :, at].astype(jnp.float32),
                sconv_ref[0, :, at].astype(jnp.float32),
                cot_ref[0, :, at].astype(jnp.float32),
                back_ref[group, :rows, LANES:].astype(jnp.float32),
                params_ref,
                inv_saved,
            )
            cross = cross + term
            partial_ref[0, :, at] = partial.astype(jnp.bfloat16)
        acc[...] = cross
        fwd_copy.wait()
        for group in range(width // LANES):
            at = pl.ds(group * LANES, LANES)
            inputs = fwd_ref[0, :, at].astype(jnp.float32)
            conv = back_ref[group, :rows, :LANES].astype(jnp.float32)
            layer = forward_terms(at, inputs, conv, params_ref, inv_fwd)
            layer_ref[0, :, at] = layer.astype(jnp.bfloat16)

    @pl.when(pipe_ref[0] == 0)
    def _():
        both(send_ref, keep_ref)

    @pl.when(pipe_ref[0] != 0)
    def _():
        both(keep_ref, send_ref)

    cross = columns_to_rows([jnp.sum(acc[...], axis=1, keepdims=True)])
    cross_ref[...] = cross * (inv_ref[1:2, :] * inv_ref[1:2, :] / D)


def leave(pipe, inv, back, fwd_in, saved_in, saved_conv, grad_out, mix_params):
    return pl.pallas_call(
        leave_kernel,
        out_shape=(
            pltpu.VMEM(fwd_in.shape, jnp.bfloat16),
            pltpu.VMEM(fwd_in.shape, jnp.bfloat16),
            pltpu.VMEM((8, 128), jnp.float32),
        ),
        in_specs=[SMEM] + [VMEM] * 2 + [HBM] + [VMEM] * 4,
        out_specs=(VMEM, VMEM, VMEM),
        scratch_shapes=[pltpu.VMEM((fwd_in.shape[1], 128), jnp.float32)] * 2
        + [pltpu.VMEM(fwd_in.shape, jnp.bfloat16), pltpu.SemaphoreType.DMA],
        name="leave",
        compiler_params=pltpu.CompilerParams(vmem_limit_bytes=24 << 20),
    )(
        pipe, inv, in_vmem(back), in_hbm(fwd_in),
        *[in_vmem(a) for a in (saved_in, saved_conv, grad_out)], mix_params,
    )


def rows_kernel(
    pipe_ref, back_ref, send_ref, keep_ref, params_ref, layer_hbm, grads_ref, layer_sem
):
    first = pipe_ref[0] == 0
    stored, rows = back_ref.shape[0], send_ref.shape[1]
    sent = pltpu.make_async_copy(send_ref, layer_hbm, layer_sem)
    kept = pltpu.make_async_copy(keep_ref, layer_hbm, layer_sem)

    @pl.when(first)
    def _():
        sent.start()

    @pl.when(jnp.logical_not(first))
    def _():
        kept.start()

    known = back_ref[0, rows : rows + 16, :].astype(jnp.float32)
    for index in range(1, stored):
        known = known + back_ref[index, rows : rows + 16, :].astype(jnp.float32)
    for group in range(stored):
        own = pl.ds(group * LANES, LANES)
        p = [params_ref[0, row : row + 1, own] for row in range(7)]
        extra = back_ref[group, rows + 16 :, :].astype(jnp.float32)
        extra = extra[:, :LANES] + extra[:, LANES:]
        m0, m1, m2 = extra[0:1], extra[1:2], extra[2:3]
        row, side = group // 2, slice(group % 2 * LANES, (group % 2 + 1) * LANES)
        q0, q1 = known[row : row + 1, side], known[row + 8 : row + 9, side]
        key_normed = p[0] * p[5] * m2 + p[6] * m1
        value_normed = p[0] * p[3] * m2 + p[4] * m1
        grads = [
            p[1] * q1 + p[3] * key_normed + p[5] * value_normed,
            p[0] * q1,
            q0,
            p[0] * key_normed,
            p[0] * p[5] * m1 + p[6] * m0,
            p[0] * value_normed,
            p[0] * p[3] * m1 + p[4] * m0,
        ]
        grads_ref[0, :, own] = jnp.concatenate(grads, axis=0)

    @pl.when(first)
    def _():
        sent.wait()

    @pl.when(jnp.logical_not(first))
    def _():
        kept.wait()


def finish_rows(pipe, back, send, keep, mix_params):
    return pl.pallas_call(
        rows_kernel,
        out_shape=(
            pltpu.HBM(send.shape, jnp.bfloat16),
            jax.ShapeDtypeStruct(mix_params.shape, jnp.float32),
        ),
        in_specs=[SMEM] + [VMEM] * 4,
        out_specs=(HBM, VMEM),
        scratch_shapes=[pltpu.SemaphoreType.DMA],
        name="finish_rows",
        compiler_params=pltpu.CompilerParams(vmem_limit_bytes=8 << 20),
    )(pipe, in_vmem(back), in_vmem(send), in_vmem(keep), mix_params)


def cross_kernel(
    pipe_ref, s0, s1, s2, s3, send_ref, keep_ref, saved_ref, peer_ref, grad_ref, term_ref, scale
):
    step = pl.program_id(0)
    first = pipe_ref[0] == 0

    @pl.when(step == 0)
    def _():
        scale[...] = rows_to_columns(s0[...] + s1[...] + s2[...] + s3[...])

    wide = grad_ref.shape[2]
    for group in range(wide // LANES):
        own = pl.ds(group * LANES, LANES)
        at = pl.ds(pl.multiple_of(step * wide + group * LANES, LANES), LANES)
        partial = jnp.where(first, keep_ref[0, :, at], send_ref[0, :, at]).astype(jnp.float32)
        saved = saved_ref[0, :, at].astype(jnp.float32)
        grad_ref[0, :, own] = (partial - saved * scale[:, 0:1]).astype(jnp.bfloat16)
        term_ref[:, at] = peer_ref[0, :, at].astype(jnp.float32) * scale[:, 1:2]


def finish_cross(pipe, scales, send, keep, saved_in, peer_saved):
    rows, width = saved_in.shape[1:]
    wide = 512
    spec = lane_spec(rows, wide)
    return pl.pallas_call(
        cross_kernel,
        out_shape=(
            jax.ShapeDtypeStruct(saved_in.shape, jnp.bfloat16),
            pltpu.VMEM((rows, width), jnp.float32),
        ),
        grid=(width // wide,),
        in_specs=[SMEM] + [VMEM] * 8,
        out_specs=(spec, VMEM),
        scratch_shapes=[pltpu.VMEM((rows, 128), jnp.float32)],
        name="finish_cross",
        compiler_params=pltpu.CompilerParams(vmem_limit_bytes=8 << 20),
    )(pipe, *scales, in_vmem(send), in_vmem(keep), in_vmem(saved_in), in_vmem(peer_saved))


def received_kernel(value_ref, term_ref, out_ref):
    wide = out_ref.shape[2]
    for at in range(0, wide, LANES):
        own = pl.ds(at, LANES)
        source = pl.ds(pl.multiple_of(pl.program_id(0) * wide + at, LANES), LANES)
        value = value_ref[0, :, source].astype(jnp.float32)
        out_ref[0, :, own] = (value - term_ref[:, source]).astype(jnp.bfloat16)


def finish_received(value, term):
    rows, width = term.shape
    wide = 512
    return pl.pallas_call(
        received_kernel,
        out_shape=jax.ShapeDtypeStruct(value.shape, jnp.bfloat16),
        grid=(width // wide,),
        in_specs=[VMEM, VMEM],
        out_specs=lane_spec(rows, wide),
        name="received",
        compiler_params=pltpu.CompilerParams(vmem_limit_bytes=8 << 20),
    )(in_vmem(value), in_vmem(term))


def per_device(tables, fwd_in, saved_in, saved_conv, grad_out, filters, mix_params, span_order):
    where = lax.axis_index("seq").astype(jnp.int32).reshape(1)
    pipe = lax.axis_index("pipe").astype(jnp.int32).reshape(1)
    raw, sums = pack(fwd_in, saved_in, grad_out)
    raw = lax.all_to_all(raw, "seq", 0, 0)
    own_sums = sum(over_chan(sums))
    sums = own_sums[:2]
    sums = jnp.concatenate([sums, across(sums, 1)], axis=0)
    sums = jnp.concatenate([sums] + [round_ring(sums, apart) for apart in (1, 2, 3)], axis=0)
    inv = lax.rsqrt(jnp.concatenate([sums, across(sums, 8)], axis=0) / D + EPSILON)
    peer_saved = lax.ppermute(saved_in, "pipe", [(1, 0)])
    spectra = filter_spectra(where, filters, tables)
    known = early(own_sums, saved_in, saved_conv, grad_out)
    back = convolve(where, span_order, gather_order(), raw, inv, known, mix_params, spectra, tables)
    back = lax.all_to_all(back, "seq", 0, 0)
    outgoing, keep, cross = leave(
        pipe, inv, back, fwd_in, saved_in, saved_conv, grad_out, mix_params
    )
    peer_cross = lax.ppermute(cross, "pipe", [(1, 0)])
    incoming = lax.ppermute(outgoing, "pipe", [(0, 1), (1, 0)])
    scales = over_chan(jnp.concatenate([cross[:1], peer_cross[:1], cross[:6]], axis=0))
    layer_out, param_grad = finish_rows(pipe, back, outgoing, keep, mix_params)
    input_grad, term = finish_cross(pipe, scales, outgoing, keep, saved_in, peer_saved)
    received = finish_received(incoming, term)
    return (layer_out, input_grad, param_grad, received)


def solution(mesh):
    tables = transform_tables()
    in_specs = (
        P("pipe", "seq", "chan"),
        P("pipe", "seq", "chan"),
        P("pipe", "seq", "chan"),
        P("pipe", "seq", "chan"),
        P("pipe", None, "chan"),
        P("pipe", None, "chan"),
        P(),
    )
    out_specs = (
        P("pipe", "seq", "chan"),
        P("pipe", "seq", "chan"),
        P("pipe", None, "chan"),
        P("pipe", "seq", "chan"),
    )
    return jax.shard_map(
        functools.partial(per_device, tuple(jnp.asarray(table) for table in tables)),
        mesh=mesh,
        in_specs=in_specs,
        out_specs=out_specs,
        check_vma=False,
    )
```

```python
import functools

import jax
import jax.numpy as jnp
import ml_dtypes
import numpy as np
from jax import lax
from jax.experimental import pallas as pl
from jax.experimental.pallas import tpu as pltpu
from jax.sharding import PartitionSpec as P


D = 8192
EPSILON = 1e-05
BLOCK = 256
LANES = 128


def transform_tables():
    period = 2 * BLOCK
    freq = np.arange(BLOCK)[:, None]
    time = np.arange(BLOCK)[None, :]
    angle = 2.0 * np.pi / period * (freq * time % period)
    real, imag = np.cos(angle), -np.sin(angle)
    imag[0] = np.where(np.arange(BLOCK) % 2 == 0, 1.0, -1.0)
    enter = np.concatenate([real, imag], axis=0)
    angle = 2.0 * np.pi / period * (freq * (time + BLOCK) % period)
    real, imag = 2.0 * np.cos(angle), -2.0 * np.sin(angle)
    real[0] = 1.0
    imag[0] = np.where(np.arange(BLOCK) % 2 == 0, 1.0, -1.0)
    leave = np.concatenate([real, imag], axis=0).T / period
    return tuple(table.astype(np.float32).astype(ml_dtypes.bfloat16) for table in (enter, leave))


def rows_to_columns(rows):
    return jnp.concatenate([rows] * 16, axis=0).T


def columns_to_rows(columns):
    lane = lax.broadcasted_iota(jnp.int32, (128, 128), 1)
    square = jnp.zeros((128, 128), jnp.float32)
    for index, column in enumerate(columns):
        square = jnp.where(lane == index, column, square)
    return square.T[:8]


VMEM = pl.BlockSpec(memory_space=pltpu.VMEM)
SMEM = pl.BlockSpec(memory_space=pltpu.SMEM)


def in_vmem(array):
    return pltpu.with_memory_space_constraint(array, pltpu.VMEM)


HBM = pl.BlockSpec(memory_space=pl.ANY)


def in_hbm(array):
    return pltpu.with_memory_space_constraint(array, pltpu.HBM)


def lane_spec(rows, wide):
    return pl.BlockSpec((1, rows, wide), lambda step, *_: (0, 0, step))


def whole(shape):
    return pl.BlockSpec(shape, lambda step, *_: (0,) * len(shape))


def pack_kernel(fwd_hbm, saved_hbm, cot_hbm, out_hbm, squares_ref, held, in_sem, out_sem):
    rows, width = held.shape[1:]
    steps = in_sem.shape[1]
    wide = width // steps
    sources = (fwd_hbm, saved_hbm, cot_hbm)
    arriving = [
        [
            pltpu.make_async_copy(
                source.at[0, :, pl.ds(step * wide, wide)],
                held.at[index, :, pl.ds(step * wide, wide)],
                in_sem.at[index, step],
            )
            for index, source in enumerate(sources[:2])
        ]
        for step in range(steps)
    ]
    leaving = [
        pltpu.make_async_copy(
            source.at[0, :, pl.ds(group * LANES, LANES)],
            out_hbm.at[group, pl.ds(index * rows, rows), :],
            out_sem.at[index, group],
        )
        for group in range(width // LANES)
        for index, source in enumerate(sources)
    ]
    for copy in sum(arriving, []) + leaving:
        copy.start()
    totals = [jnp.zeros((rows, LANES), jnp.float32)] * 2
    for step, copies in enumerate(arriving):
        for index, copy in enumerate(copies):
            copy.wait()
            for group in range(step * wide // LANES, (step + 1) * wide // LANES):
                value = held[index, :, group * LANES : (group + 1) * LANES].astype(jnp.float32)
                totals[index] = totals[index] + value * value
    squares_ref[...] = columns_to_rows([jnp.sum(total, axis=1, keepdims=True) for total in totals])
    for copy in leaving:
        copy.wait()


def pack(fwd_in, saved_in, grad_out):
    rows, width = fwd_in.shape[1:]
    return pl.pallas_call(
        pack_kernel,
        out_shape=(
            pltpu.HBM((width // LANES, 3 * rows, LANES), jnp.bfloat16),
            jax.ShapeDtypeStruct((8, 128), jnp.float32),
        ),
        in_specs=[HBM] * 3,
        out_specs=(HBM, VMEM),
        scratch_shapes=[
            pltpu.VMEM((2, rows, width), jnp.bfloat16),
            pltpu.SemaphoreType.DMA((2, 4)),
            pltpu.SemaphoreType.DMA((3, width // LANES)),
        ],
        name="pack",
        compiler_params=pltpu.CompilerParams(vmem_limit_bytes=16 << 20),
    )(in_hbm(fwd_in), in_hbm(saved_in), in_hbm(grad_out))


def over_chan(rows):
    count = lax.axis_size("chan")
    got = [rows]
    for apart in range(1, count):
        got.append(
            lax.ppermute(rows, "chan", [(low, (low + apart) % count) for low in range(count)])
        )
    return got


def across(rows, flip):
    count = lax.axis_size("seq")
    return lax.ppermute(rows, "seq", [(low, low ^ flip) for low in range(count)])


def round_ring(rows, apart):
    count = lax.axis_size("seq")
    place = lambda low: low // 8 * 8 + (low + 2 * apart) % 8
    return lax.ppermute(rows, "seq", [(low, place(low)) for low in range(count)])


def gather_order():
    own = lax.axis_index("seq").astype(jnp.int32)
    block = jnp.arange(16, dtype=jnp.int32)
    core = (block ^ own) & 1
    back = (own // 2 - block // 2) % 4
    side = (block // 8) ^ (own // 8)
    return back * 4 + side * 2 + core


def early_kernel(sums_ref, saved_ref, sconv_ref, cot_ref, out_ref, inv):
    step = pl.program_id(0)

    @pl.when(step == 0)
    def _():
        inv[...] = rows_to_columns(lax.rsqrt(sums_ref[...] / D + EPSILON))

    inv_saved = inv[:, 1:2]
    pairs = saved_ref.shape[2] // (2 * LANES)
    half = out_ref.shape[0] // 2
    for pair in range(pairs):
        at = pl.ds(pair * 2 * LANES, 2 * LANES)
        normed = saved_ref[0, :, at].astype(jnp.float32) * inv_saved
        grad_query = cot_ref[0, :, at].astype(jnp.float32) * sconv_ref[0, :, at].astype(jnp.float32)
        row = step * pairs + pair
        out_ref[pl.ds(row, 1), :] = jnp.sum(grad_query, axis=0, keepdims=True)
        out_ref[pl.ds(row + half, 1), :] = jnp.sum(grad_query * normed, axis=0, keepdims=True)


def early(sums, saved_in, saved_conv, grad_out):
    rows, width = saved_in.shape[1:]
    wide = 512
    return pl.pallas_call(
        early_kernel,
        out_shape=jax.ShapeDtypeStruct((width // LANES, 2 * LANES), jnp.float32),
        grid=(width // wide,),
        in_specs=[VMEM] + [lane_spec(rows, wide)] * 3,
        out_specs=whole((width // LANES, 2 * LANES)),
        scratch_shapes=[pltpu.VMEM((rows, 128), jnp.float32)],
        name="early",
        compiler_params=pltpu.CompilerParams(vmem_limit_bytes=12 << 20),
    )(sums, in_hbm(saved_in), in_hbm(saved_conv), in_hbm(grad_out))


def side_by_side(ref, index):
    at = 2 * index * BLOCK
    return jnp.concatenate([ref[at : at + BLOCK, :], ref[at + BLOCK : at + 2 * BLOCK, :]], axis=1)


def filter_kernel(where_ref, taps_ref, enter, filt):
    del where_ref
    freq = lax.broadcasted_iota(jnp.int32, (2 * BLOCK, LANES), 0)
    parity = jnp.where(freq % 2 == 0, 1.0, -1.0)
    earlier = None
    for pair in range(filt.shape[0] // 2):
        pair_spectra = jnp.dot(
            enter[...], side_by_side(taps_ref.at[0], pair), preferred_element_type=jnp.float32
        )
        for side in range(2):
            current = pair_spectra[:, side * LANES : (side + 1) * LANES]
            both = parity * current
            if earlier is not None:
                both = both + earlier
            earlier = current
            filt[2 * pair + side, 0] = both[:BLOCK]
            filt[2 * pair + side, 1] = both[BLOCK:]


def filter_spectra(where, filters, tables):
    length = filters.shape[1]
    shape = (length // BLOCK, 2, BLOCK, LANES)
    return pl.pallas_call(
        filter_kernel,
        out_shape=pltpu.HBM(shape, jnp.float32),
        grid_spec=pltpu.PrefetchScalarGridSpec(
            num_scalar_prefetch=1,
            grid=(1,),
            in_specs=[pl.BlockSpec((1, length, LANES), lambda step, at: (0, 0, at[0]))]
            + [whole(tables[0].shape)],
            out_specs=whole(shape),
        ),
        name="filter_spectra",
        compiler_params=pltpu.CompilerParams(vmem_limit_bytes=16 << 20),
    )(where, in_hbm(filters), in_hbm(tables[0]))


def fold(block):
    return jnp.sum(block.reshape(block.shape[0] // 8, 8, LANES), axis=0)


def conv_kernel(
    where_ref, order_ref, gathered_ref, inv_ref, known_ref, params_ref, filt_hbm, raw_hbm, enter_hbm,
    leave_hbm, out_hbm, raw_ref, filt, enter, leave, out_ref, ordered, spectra, product, inv_rows, inv, raw_sem, table_sem, out_sem,
):
    stored = raw_ref.shape[0]
    raw_copies = [
        pltpu.make_async_copy(raw_hbm.at[index], raw_ref.at[index], raw_sem.at[index])
        for index in range(stored)
    ]
    table_copies = [
        pltpu.make_async_copy(source, target, table_sem.at[index])
        for index, (source, target) in enumerate(
            ((enter_hbm, enter), (leave_hbm, leave), (filt_hbm, filt))
        )
    ]
    out_copies = [
        pltpu.make_async_copy(out_ref.at[index], out_hbm.at[index], out_sem.at[index])
        for index in range(stored)
    ]
    for copy in raw_copies + table_copies:
        copy.start()
    rows = raw_ref.shape[1] // 3
    blocks = stored * rows // BLOCK
    lanes = pl.ds(pl.multiple_of(where_ref[0] * LANES, LANES), LANES)
    p = [params_ref[0, row : row + 1, lanes] for row in range(7)]

    gains = [p[0] * p[1], p[0] * p[3], p[0] * p[5]]
    for index in range(stored):
        inv_rows[2 * index : 2 * index + 2, :] = inv_ref[pl.ds(2 * gathered_ref[index], 2), :]
    inv[...] = jnp.concatenate([inv_rows[...]] * (128 // (2 * stored)), axis=0).T
    for index in range(stored):
        if index % 4 == 0:
            for copy in raw_copies[index : index + 4]:
                copy.wait()
        at = pl.multiple_of(order_ref[index] * rows, rows)
        inv_fwd = inv[:, 2 * index : 2 * index + 1]
        inv_saved = inv[:, 2 * index + 1 : 2 * index + 2]
        normed = raw_ref[index, :rows, :].astype(jnp.float32) * inv_fwd
        mixed = (normed * gains[1] + p[4]) * (normed * gains[2] + p[6])
        normed = raw_ref[index, rows : 2 * rows, :].astype(jnp.float32) * inv_saved
        cot = raw_ref[index, 2 * rows :, :].astype(jnp.float32)
        ordered[pl.ds(at, rows), :LANES] = mixed.astype(jnp.bfloat16)
        ordered[pl.ds(at, rows), LANES:] = (cot * (normed * gains[0] + p[2])).astype(jnp.bfloat16)

    table_copies[0].wait()
    for index in range(blocks):
        data = ordered[index * BLOCK : (index + 1) * BLOCK, :]
        spectra[index] = jnp.dot(enter[...], data, preferred_element_type=jnp.float32)

    table_copies[2].wait()

    def forward_and_adjoint(low, high, one_product):
        for adjoint in (False, True):
            lanes = slice(LANES, 2 * LANES) if adjoint else slice(0, LANES)
            x_re = [spectra[j, low, lanes] for j in range(blocks)]
            x_im = [spectra[j, high, lanes] for j in range(blocks)]
            for i in range(blocks):
                terms = range(i, blocks) if adjoint else range(i + 1)
                re, im = one_product(adjoint, x_re, x_im, [(abs(i - j), j) for j in terms])
                product[i, low, lanes] = re
                product[i, high, lanes] = im

    def total(terms):
        terms = list(terms)
        return functools.reduce(lambda one, two: one + two, terms)

    def first_tile(adjoint, x_re, x_im, terms):
        f_re = [filt[d, 0, 0:8, :] for d in range(blocks)]
        first = lax.broadcasted_iota(jnp.int32, (8, LANES), 0) == 0
        imag = [filt[d, 1, 0:8, :] for d in range(blocks)]
        f_im = [jnp.where(first, 0.0, value) for value in imag]
        f_nq = [jnp.where(first, value, f_re[d]) for d, value in enumerate(imag)]
        direct = total(f_re[d] * x_re[j] for d, j in terms)
        crossed = total(f_im[d] * x_im[j] for d, j in terms)
        straight = total(f_nq[d] * x_im[j] for d, j in terms)
        turned = total(f_im[d] * x_re[j] for d, j in terms)
        if adjoint:
            return direct + crossed, straight - turned
        return direct - crossed, straight + turned

    forward_and_adjoint(slice(0, 8), slice(BLOCK, BLOCK + 8), first_tile)

    def products(tile, carry):
        low = pl.ds(pl.multiple_of(tile * 8, 8), 8)
        high = pl.ds(pl.multiple_of(BLOCK + tile * 8, 8), 8)
        f_re = [filt[d, 0, low, :] for d in range(blocks)]
        f_im = [filt[d, 1, low, :] for d in range(blocks)]
        f_less = [f_im[d] - f_re[d] for d in range(blocks)]
        f_more = [f_im[d] + f_re[d] for d in range(blocks)]

        def other_tile(adjoint, x_re, x_im, terms):
            both = total(f_re[d] * (x_re[j] + x_im[j]) for d, j in terms)
            if adjoint:
                return (
                    both + total(f_less[d] * x_im[j] for d, j in terms),
                    both - total(f_more[d] * x_re[j] for d, j in terms),
                )
            return (
                both - total(f_more[d] * x_im[j] for d, j in terms),
                both + total(f_less[d] * x_re[j] for d, j in terms),
            )

        forward_and_adjoint(low, high, other_tile)
        return carry

    lax.fori_loop(1, BLOCK // 8, products, 0)

    table_copies[1].wait()
    for index in range(blocks):
        left = jnp.dot(
            leave[...], product[index].astype(jnp.bfloat16), preferred_element_type=jnp.float32
        )
        ordered[index * BLOCK : (index + 1) * BLOCK, :] = left.astype(jnp.bfloat16)

    sums = [jnp.zeros((8, LANES), jnp.float32)] * 3
    for index in range(stored):
        at = pl.multiple_of(order_ref[index] * rows, rows)
        block = ordered[pl.ds(at, rows), :]
        out_ref[index, :rows, :] = block
        grad_mixed = block[:, LANES:].astype(jnp.float32)
        inv_saved = inv[:, 2 * index + 1 : 2 * index + 2]
        normed = raw_ref[index, rows : 2 * rows, :].astype(jnp.float32) * inv_saved
        once = grad_mixed * normed
        for power, term in enumerate((grad_mixed, once, once * normed)):
            sums[power] = sums[power] + fold(term)

    sums = jnp.concatenate(
        [jnp.sum(total, axis=0, keepdims=True) for total in sums]
        + [jnp.zeros((5, LANES), jnp.float32)],
        axis=0,
    )
    known = known_ref[...].astype(jnp.bfloat16)
    top = sums.astype(jnp.bfloat16)
    rest = (sums - top.astype(jnp.float32)).astype(jnp.bfloat16)
    for index in range(stored):
        out_ref[index, rows : rows + 16, :] = known
        out_ref[index, rows + 16 :, :LANES] = top
        out_ref[index, rows + 16 :, LANES:] = rest
        out_copies[index].start()
    for copy in out_copies:
        copy.wait()


def convolve(where, order, gathered, raw, inv, known, params, spectra, tables):
    stored = raw.shape[0]
    rows = raw.shape[1] // 3
    length = stored * rows
    blocks = length // BLOCK
    return pl.pallas_call(
        conv_kernel,
        out_shape=pltpu.HBM((stored, rows + 24, 2 * LANES), jnp.bfloat16),
        in_specs=[SMEM] * 3 + [VMEM] * 3 + [HBM] * 4,
        out_specs=HBM,
        scratch_shapes=[
            pltpu.VMEM(raw.shape, jnp.bfloat16),
            pltpu.VMEM(spectra.shape, jnp.float32),
            pltpu.VMEM((2 * BLOCK, BLOCK), jnp.bfloat16),
            pltpu.VMEM((BLOCK, 2 * BLOCK), jnp.bfloat16),
            pltpu.VMEM((stored, rows + 24, 2 * LANES), jnp.bfloat16),
            pltpu.VMEM((length, 2 * LANES), jnp.bfloat16),
            pltpu.VMEM((blocks, 2 * BLOCK, 2 * LANES), jnp.float32),
            pltpu.VMEM((blocks, 2 * BLOCK, 2 * LANES), jnp.float32),
            pltpu.VMEM((2 * stored, 128), jnp.float32),
            pltpu.VMEM((128, 128), jnp.float32),
            pltpu.SemaphoreType.DMA((stored,)),
            pltpu.SemaphoreType.DMA((3,)),
            pltpu.SemaphoreType.DMA((stored,)),
        ],
        name="convolve",
        compiler_params=pltpu.CompilerParams(vmem_limit_bytes=28 << 20),
    )(
        where, order, gathered, inv, known, params, in_hbm(spectra), in_hbm(raw),
        *[in_hbm(table) for table in tables],
    )


def forward_terms(at, inputs, conv, params_ref, inv_fwd):
    p = [params_ref[0, row : row + 1, at] for row in range(3)]
    query = inputs * inv_fwd * (p[0] * p[1]) + p[2]
    return inputs + query * conv


def backward_terms(at, saved, sconv, cot, grad_mixed, params_ref, inv_saved):
    p = [params_ref[0, row : row + 1, at] for row in range(7)]
    normed = saved * inv_saved
    mixed_grad = normed * (2.0 * p[0] * p[3] * p[5] * p[0]) + p[0] * (p[6] * p[3] + p[4] * p[5])
    grad_normed = cot * sconv * (p[1] * p[0]) + grad_mixed * mixed_grad
    return cot + inv_saved * grad_normed, grad_normed * normed


def leave_kernel(
    pipe_ref, inv_ref, back_ref, fwd_hbm, saved_ref, sconv_ref, cot_ref, params_ref,
    send_ref, keep_ref, cross_ref, inv, acc, fwd_ref, fwd_sem,
):
    rows, width = fwd_ref.shape[1:]
    fwd_copy = pltpu.make_async_copy(fwd_hbm, fwd_ref, fwd_sem)
    fwd_copy.start()
    inv[...] = rows_to_columns(inv_ref[0:8, :])
    inv_fwd = inv[:, 0:1]
    inv_saved = inv[:, 1:2]

    def both(layer_ref, partial_ref):
        cross = jnp.zeros((rows, LANES), jnp.float32)
        for group in range(width // LANES):
            at = pl.ds(group * LANES, LANES)
            partial, term = backward_terms(
                at,
                saved_ref[0, :, at].astype(jnp.float32),
                sconv_ref[0, :, at].astype(jnp.float32),
                cot_ref[0, :, at].astype(jnp.float32),
                back_ref[group, :rows, LANES:].astype(jnp.float32),
                params_ref,
                inv_saved,
            )
            cross = cross + term
            partial_ref[0, :, at] = partial.astype(jnp.bfloat16)
        acc[...] = cross
        fwd_copy.wait()
        for group in range(width // LANES):
            at = pl.ds(group * LANES, LANES)
            inputs = fwd_ref[0, :, at].astype(jnp.float32)
            conv = back_ref[group, :rows, :LANES].astype(jnp.float32)
            layer = forward_terms(at, inputs, conv, params_ref, inv_fwd)
            layer_ref[0, :, at] = layer.astype(jnp.bfloat16)

    @pl.when(pipe_ref[0] == 0)
    def _():
        both(send_ref, keep_ref)

    @pl.when(pipe_ref[0] != 0)
    def _():
        both(keep_ref, send_ref)

    cross = columns_to_rows([jnp.sum(acc[...], axis=1, keepdims=True)])
    cross_ref[...] = cross * (inv_ref[1:2, :] * inv_ref[1:2, :] / D)


def leave(pipe, inv, back, fwd_in, saved_in, saved_conv, grad_out, mix_params):
    return pl.pallas_call(
        leave_kernel,
        out_shape=(
            pltpu.VMEM(fwd_in.shape, jnp.bfloat16),
            pltpu.VMEM(fwd_in.shape, jnp.bfloat16),
            pltpu.VMEM((8, 128), jnp.float32),
        ),
        in_specs=[SMEM] + [VMEM] * 2 + [HBM] + [VMEM] * 4,
        out_specs=(VMEM, VMEM, VMEM),
        scratch_shapes=[pltpu.VMEM((fwd_in.shape[1], 128), jnp.float32)] * 2
        + [pltpu.VMEM(fwd_in.shape, jnp.bfloat16), pltpu.SemaphoreType.DMA],
        name="leave",
        compiler_params=pltpu.CompilerParams(vmem_limit_bytes=24 << 20),
    )(
        pipe, inv, in_vmem(back), in_hbm(fwd_in),
        *[in_vmem(a) for a in (saved_in, saved_conv, grad_out)], mix_params,
    )


def rows_kernel(
    pipe_ref, back_ref, send_ref, keep_ref, params_ref, layer_hbm, grads_ref, layer_sem
):
    first = pipe_ref[0] == 0
    stored, rows = back_ref.shape[0], send_ref.shape[1]
    sent = pltpu.make_async_copy(send_ref, layer_hbm, layer_sem)
    kept = pltpu.make_async_copy(keep_ref, layer_hbm, layer_sem)

    @pl.when(first)
    def _():
        sent.start()

    @pl.when(jnp.logical_not(first))
    def _():
        kept.start()

    known = back_ref[0, rows : rows + 16, :].astype(jnp.float32)
    for index in range(1, stored):
        known = known + back_ref[index, rows : rows + 16, :].astype(jnp.float32)
    for group in range(stored):
        own = pl.ds(group * LANES, LANES)
        p = [params_ref[0, row : row + 1, own] for row in range(7)]
        extra = back_ref[group, rows + 16 :, :].astype(jnp.float32)
        extra = extra[:, :LANES] + extra[:, LANES:]
        m0, m1, m2 = extra[0:1], extra[1:2], extra[2:3]
        row, side = group // 2, slice(group % 2 * LANES, (group % 2 + 1) * LANES)
        q0, q1 = known[row : row + 1, side], known[row + 8 : row + 9, side]
        key_normed = p[0] * p[5] * m2 + p[6] * m1
        value_normed = p[0] * p[3] * m2 + p[4] * m1
        grads = [
            p[1] * q1 + p[3] * key_normed + p[5] * value_normed,
            p[0] * q1,
            q0,
            p[0] * key_normed,
            p[0] * p[5] * m1 + p[6] * m0,
            p[0] * value_normed,
            p[0] * p[3] * m1 + p[4] * m0,
        ]
        grads_ref[0, :, own] = jnp.concatenate(grads, axis=0)

    @pl.when(first)
    def _():
        sent.wait()

    @pl.when(jnp.logical_not(first))
    def _():
        kept.wait()


def finish_rows(pipe, back, send, keep, mix_params):
    return pl.pallas_call(
        rows_kernel,
        out_shape=(
            pltpu.HBM(send.shape, jnp.bfloat16),
            jax.ShapeDtypeStruct(mix_params.shape, jnp.float32),
        ),
        in_specs=[SMEM] + [VMEM] * 4,
        out_specs=(HBM, VMEM),
        scratch_shapes=[pltpu.SemaphoreType.DMA],
        name="finish_rows",
        compiler_params=pltpu.CompilerParams(vmem_limit_bytes=8 << 20),
    )(pipe, in_vmem(back), in_vmem(send), in_vmem(keep), mix_params)


def cross_kernel(
    pipe_ref, s0, s1, s2, s3, send_ref, keep_ref, saved_ref, peer_ref, grad_ref, term_ref, scale
):
    step = pl.program_id(0)
    first = pipe_ref[0] == 0

    @pl.when(step == 0)
    def _():
        scale[...] = rows_to_columns(s0[...] + s1[...] + s2[...] + s3[...])

    wide = grad_ref.shape[2]
    for group in range(wide // LANES):
        own = pl.ds(group * LANES, LANES)
        at = pl.ds(pl.multiple_of(step * wide + group * LANES, LANES), LANES)
        partial = jnp.where(first, keep_ref[0, :, at], send_ref[0, :, at]).astype(jnp.float32)
        saved = saved_ref[0, :, at].astype(jnp.float32)
        grad_ref[0, :, own] = (partial - saved * scale[:, 0:1]).astype(jnp.bfloat16)
        term_ref[:, at] = peer_ref[0, :, at].astype(jnp.float32) * scale[:, 1:2]


def finish_cross(pipe, scales, send, keep, saved_in, peer_saved):
    rows, width = saved_in.shape[1:]
    wide = 512
    spec = lane_spec(rows, wide)
    return pl.pallas_call(
        cross_kernel,
        out_shape=(
            jax.ShapeDtypeStruct(saved_in.shape, jnp.bfloat16),
            pltpu.VMEM((rows, width), jnp.float32),
        ),
        grid=(width // wide,),
        in_specs=[SMEM] + [VMEM] * 8,
        out_specs=(spec, VMEM),
        scratch_shapes=[pltpu.VMEM((rows, 128), jnp.float32)],
        name="finish_cross",
        compiler_params=pltpu.CompilerParams(vmem_limit_bytes=8 << 20),
    )(pipe, *scales, in_vmem(send), in_vmem(keep), in_vmem(saved_in), in_vmem(peer_saved))


def received_kernel(value_ref, term_ref, out_hbm, out_ref, out_sem):
    steps = out_sem.shape[0]
    wide = out_ref.shape[1] // steps
    copies = []
    for step in range(steps):
        for at in range(step * wide, (step + 1) * wide, LANES):
            own = pl.ds(at, LANES)
            value = value_ref[0, :, own].astype(jnp.float32)
            out_ref[:, own] = (value - term_ref[:, own]).astype(jnp.bfloat16)
        chunk = pl.ds(step * wide, wide)
        copy = pltpu.make_async_copy(
            out_ref.at[:, chunk], out_hbm.at[0, :, chunk], out_sem.at[step]
        )
        copy.start()
        copies.append(copy)
    for copy in copies:
        copy.wait()


def finish_received(value, term):
    rows, width = term.shape
    return pl.pallas_call(
        received_kernel,
        out_shape=pltpu.HBM(value.shape, jnp.bfloat16),
        in_specs=[VMEM, VMEM],
        out_specs=HBM,
        scratch_shapes=[
            pltpu.VMEM((rows, width), jnp.bfloat16),
            pltpu.SemaphoreType.DMA((8,)),
        ],
        name="received",
        compiler_params=pltpu.CompilerParams(vmem_limit_bytes=8 << 20),
    )(in_vmem(value), in_vmem(term))


def per_device(tables, fwd_in, saved_in, saved_conv, grad_out, filters, mix_params, span_order):
    where = lax.axis_index("seq").astype(jnp.int32).reshape(1)
    pipe = lax.axis_index("pipe").astype(jnp.int32).reshape(1)
    raw, sums = pack(fwd_in, saved_in, grad_out)
    raw = lax.all_to_all(raw, "seq", 0, 0)
    own_sums = sum(over_chan(sums))
    sums = own_sums[:2]
    sums = jnp.concatenate([sums, across(sums, 1)], axis=0)
    sums = jnp.concatenate([sums, across(sums, 8)], axis=0)
    sums = jnp.concatenate([sums] + [round_ring(sums, apart) for apart in (1, 2, 3)], axis=0)
    inv = lax.rsqrt(sums / D + EPSILON)
    peer_saved = lax.ppermute(saved_in, "pipe", [(1, 0)])
    spectra = filter_spectra(where, filters, tables)
    known = early(own_sums, saved_in, saved_conv, grad_out)
    back = convolve(where, span_order, gather_order(), raw, inv, known, mix_params, spectra, tables)
    back = lax.all_to_all(back, "seq", 0, 0)
    outgoing, keep, cross = leave(
        pipe, inv, back, fwd_in, saved_in, saved_conv, grad_out, mix_params
    )
    peer_cross = lax.ppermute(cross, "pipe", [(1, 0)])
    incoming = lax.ppermute(outgoing, "pipe", [(0, 1), (1, 0)])
    scales = over_chan(jnp.concatenate([cross[:1], peer_cross[:1], cross[:6]], axis=0))
    layer_out, param_grad = finish_rows(pipe, back, outgoing, keep, mix_params)
    input_grad, term = finish_cross(pipe, scales, outgoing, keep, saved_in, peer_saved)
    received = finish_received(incoming, term)
    return (layer_out, input_grad, param_grad, received)


def solution(mesh):
    tables = transform_tables()
    in_specs = (
        P("pipe", "seq", "chan"),
        P("pipe", "seq", "chan"),
        P("pipe", "seq", "chan"),
        P("pipe", "seq", "chan"),
        P("pipe", None, "chan"),
        P("pipe", None, "chan"),
        P(),
    )
    out_specs = (
        P("pipe", "seq", "chan"),
        P("pipe", "seq", "chan"),
        P("pipe", None, "chan"),
        P("pipe", "seq", "chan"),
    )
    return jax.shard_map(
        functools.partial(per_device, tuple(jnp.asarray(table) for table in tables)),
        mesh=mesh,
        in_specs=in_specs,
        out_specs=out_specs,
        check_vma=False,
    )
```

```python
import functools

import jax
import jax.numpy as jnp
import ml_dtypes
import numpy as np
from jax import lax
from jax.experimental import pallas as pl
from jax.experimental.pallas import tpu as pltpu
from jax.sharding import PartitionSpec as P


D = 8192
EPSILON = 1e-05
BLOCK = 256
LANES = 128


def transform_tables():
    period = 2 * BLOCK
    freq = np.arange(BLOCK)[:, None]
    time = np.arange(BLOCK)[None, :]
    angle = 2.0 * np.pi / period * (freq * time % period)
    real, imag = np.cos(angle), -np.sin(angle)
    imag[0] = np.where(np.arange(BLOCK) % 2 == 0, 1.0, -1.0)
    enter = np.concatenate([real, imag], axis=0)
    angle = 2.0 * np.pi / period * (freq * (time + BLOCK) % period)
    real, imag = 2.0 * np.cos(angle), -2.0 * np.sin(angle)
    real[0] = 1.0
    imag[0] = np.where(np.arange(BLOCK) % 2 == 0, 1.0, -1.0)
    leave = np.concatenate([real, imag], axis=0).T / period
    return tuple(table.astype(np.float32).astype(ml_dtypes.bfloat16) for table in (enter, leave))


def rows_to_columns(rows):
    return jnp.concatenate([rows] * 16, axis=0).T


def columns_to_rows(columns):
    lane = lax.broadcasted_iota(jnp.int32, (128, 128), 1)
    square = jnp.zeros((128, 128), jnp.float32)
    for index, column in enumerate(columns):
        square = jnp.where(lane == index, column, square)
    return square.T[:8]


VMEM = pl.BlockSpec(memory_space=pltpu.VMEM)
SMEM = pl.BlockSpec(memory_space=pltpu.SMEM)


def in_vmem(array):
    return pltpu.with_memory_space_constraint(array, pltpu.VMEM)


HBM = pl.BlockSpec(memory_space=pl.ANY)


def in_hbm(array):
    return pltpu.with_memory_space_constraint(array, pltpu.HBM)


def lane_spec(rows, wide):
    return pl.BlockSpec((1, rows, wide), lambda step, *_: (0, 0, step))


def whole(shape):
    return pl.BlockSpec(shape, lambda step, *_: (0,) * len(shape))


def pack_kernel(fwd_hbm, saved_hbm, cot_hbm, out_hbm, squares_ref, held, in_sem, out_sem):
    rows, width = held.shape[1:]
    steps = in_sem.shape[1]
    wide = width // steps
    sources = (fwd_hbm, saved_hbm, cot_hbm)
    arriving = [
        [
            pltpu.make_async_copy(
                source.at[0, :, pl.ds(step * wide, wide)],
                held.at[index, :, pl.ds(step * wide, wide)],
                in_sem.at[index, step],
            )
            for index, source in enumerate(sources)
        ]
        for step in range(steps)
    ]
    for copies in arriving:
        for copy in copies:
            copy.start()
    leaving = []
    totals = [jnp.zeros((rows, LANES), jnp.float32)] * 2
    for step, copies in enumerate(arriving):
        for index, copy in enumerate(copies):
            copy.wait()
            for group in range(step * wide // LANES, (step + 1) * wide // LANES):
                out = pltpu.make_async_copy(
                    held.at[index, :, pl.ds(group * LANES, LANES)],
                    out_hbm.at[group, pl.ds(index * rows, rows), :],
                    out_sem.at[index, group],
                )
                out.start()
                leaving.append(out)
        for index in range(2):
            for group in range(step * wide // LANES, (step + 1) * wide // LANES):
                value = held[index, :, group * LANES : (group + 1) * LANES].astype(jnp.float32)
                totals[index] = totals[index] + value * value
    squares_ref[...] = columns_to_rows([jnp.sum(total, axis=1, keepdims=True) for total in totals])
    for copy in leaving:
        copy.wait()


def pack(fwd_in, saved_in, grad_out):
    rows, width = fwd_in.shape[1:]
    return pl.pallas_call(
        pack_kernel,
        out_shape=(
            pltpu.HBM((width // LANES, 3 * rows, LANES), jnp.bfloat16),
            jax.ShapeDtypeStruct((8, 128), jnp.float32),
        ),
        in_specs=[HBM] * 3,
        out_specs=(HBM, VMEM),
        scratch_shapes=[
            pltpu.VMEM((3, rows, width), jnp.bfloat16),
            pltpu.SemaphoreType.DMA((3, 4)),
            pltpu.SemaphoreType.DMA((3, width // LANES)),
        ],
        name="pack",
        compiler_params=pltpu.CompilerParams(vmem_limit_bytes=16 << 20),
    )(in_hbm(fwd_in), in_hbm(saved_in), in_hbm(grad_out))


def over_chan(rows):
    count = lax.axis_size("chan")
    got = [rows]
    for apart in range(1, count):
        got.append(
            lax.ppermute(rows, "chan", [(low, (low + apart) % count) for low in range(count)])
        )
    return got


def across(rows, flip):
    count = lax.axis_size("seq")
    return lax.ppermute(rows, "seq", [(low, low ^ flip) for low in range(count)])


def round_ring(rows, apart):
    count = lax.axis_size("seq")
    place = lambda low: low // 8 * 8 + (low + 2 * apart) % 8
    return lax.ppermute(rows, "seq", [(low, place(low)) for low in range(count)])


def gather_order():
    own = lax.axis_index("seq").astype(jnp.int32)
    block = jnp.arange(16, dtype=jnp.int32)
    core = (block ^ own) & 1
    back = (own // 2 - block // 2) % 4
    side = (block // 8) ^ (own // 8)
    return side * 8 + back * 2 + core


def early_kernel(sums_ref, saved_ref, sconv_ref, cot_ref, out_ref, inv):
    step = pl.program_id(0)

    @pl.when(step == 0)
    def _():
        inv[...] = rows_to_columns(lax.rsqrt(sums_ref[...] / D + EPSILON))

    inv_saved = inv[:, 1:2]
    pairs = saved_ref.shape[2] // (2 * LANES)
    half = out_ref.shape[0] // 2
    for pair in range(pairs):
        at = pl.ds(pair * 2 * LANES, 2 * LANES)
        normed = saved_ref[0, :, at].astype(jnp.float32) * inv_saved
        grad_query = cot_ref[0, :, at].astype(jnp.float32) * sconv_ref[0, :, at].astype(jnp.float32)
        row = step * pairs + pair
        out_ref[pl.ds(row, 1), :] = jnp.sum(grad_query, axis=0, keepdims=True)
        out_ref[pl.ds(row + half, 1), :] = jnp.sum(grad_query * normed, axis=0, keepdims=True)


def early(sums, saved_in, saved_conv, grad_out):
    rows, width = saved_in.shape[1:]
    wide = 512
    return pl.pallas_call(
        early_kernel,
        out_shape=jax.ShapeDtypeStruct((width // LANES, 2 * LANES), jnp.float32),
        grid=(width // wide,),
        in_specs=[VMEM] + [lane_spec(rows, wide)] * 3,
        out_specs=whole((width // LANES, 2 * LANES)),
        scratch_shapes=[pltpu.VMEM((rows, 128), jnp.float32)],
        name="early",
        compiler_params=pltpu.CompilerParams(vmem_limit_bytes=12 << 20),
    )(sums, in_hbm(saved_in), in_hbm(saved_conv), in_hbm(grad_out))


def side_by_side(ref, index):
    at = 2 * index * BLOCK
    return jnp.concatenate([ref[at : at + BLOCK, :], ref[at + BLOCK : at + 2 * BLOCK, :]], axis=1)


def filter_kernel(where_ref, taps_ref, enter, filt):
    del where_ref
    freq = lax.broadcasted_iota(jnp.int32, (2 * BLOCK, LANES), 0)
    parity = jnp.where(freq % 2 == 0, 1.0, -1.0)
    earlier = None
    for pair in range(filt.shape[0] // 2):
        pair_spectra = jnp.dot(
            enter[...], side_by_side(taps_ref.at[0], pair), preferred_element_type=jnp.float32
        )
        for side in range(2):
            current = pair_spectra[:, side * LANES : (side + 1) * LANES]
            both = parity * current
            if earlier is not None:
                both = both + earlier
            earlier = current
            filt[2 * pair + side, 0] = both[:BLOCK]
            filt[2 * pair + side, 1] = both[BLOCK:]


def filter_spectra(where, filters, tables):
    length = filters.shape[1]
    shape = (length // BLOCK, 2, BLOCK, LANES)
    return pl.pallas_call(
        filter_kernel,
        out_shape=pltpu.HBM(shape, jnp.float32),
        grid_spec=pltpu.PrefetchScalarGridSpec(
            num_scalar_prefetch=1,
            grid=(1,),
            in_specs=[pl.BlockSpec((1, length, LANES), lambda step, at: (0, 0, at[0]))]
            + [whole(tables[0].shape)],
            out_specs=whole(shape),
        ),
        name="filter_spectra",
        compiler_params=pltpu.CompilerParams(vmem_limit_bytes=16 << 20),
    )(where, in_hbm(filters), in_hbm(tables[0]))


def fold(block):
    return jnp.sum(block.reshape(block.shape[0] // 8, 8, LANES), axis=0)


def conv_kernel(
    where_ref, order_ref, gathered_ref, inv_ref, known_ref, params_ref, filt_hbm, raw_hbm, enter_hbm,
    leave_hbm, out_hbm, raw_ref, filt, enter, leave, out_ref, ordered, spectra, product, inv_rows, inv, raw_sem, table_sem, out_sem,
):
    stored = raw_ref.shape[0]
    raw_copies = [
        pltpu.make_async_copy(raw_hbm.at[index], raw_ref.at[index], raw_sem.at[index])
        for index in range(stored)
    ]
    table_copies = [
        pltpu.make_async_copy(source, target, table_sem.at[index])
        for index, (source, target) in enumerate(
            ((enter_hbm, enter), (leave_hbm, leave), (filt_hbm, filt))
        )
    ]
    out_copies = [
        pltpu.make_async_copy(out_ref.at[index], out_hbm.at[index], out_sem.at[index])
        for index in range(stored)
    ]
    for copy in raw_copies + table_copies:
        copy.start()
    rows = raw_ref.shape[1] // 3
    blocks = stored * rows // BLOCK
    lanes = pl.ds(pl.multiple_of(where_ref[0] * LANES, LANES), LANES)
    p = [params_ref[0, row : row + 1, lanes] for row in range(7)]

    gains = [p[0] * p[1], p[0] * p[3], p[0] * p[5]]
    for index in range(stored):
        inv_rows[2 * index : 2 * index + 2, :] = inv_ref[pl.ds(2 * gathered_ref[index], 2), :]
    inv[...] = jnp.concatenate([inv_rows[...]] * (128 // (2 * stored)), axis=0).T
    for index in range(stored):
        if index % 4 == 0:
            for copy in raw_copies[index : index + 4]:
                copy.wait()
        at = pl.multiple_of(order_ref[index] * rows, rows)
        inv_fwd = inv[:, 2 * index : 2 * index + 1]
        inv_saved = inv[:, 2 * index + 1 : 2 * index + 2]
        normed = raw_ref[index, :rows, :].astype(jnp.float32) * inv_fwd
        mixed = (normed * gains[1] + p[4]) * (normed * gains[2] + p[6])
        normed = raw_ref[index, rows : 2 * rows, :].astype(jnp.float32) * inv_saved
        cot = raw_ref[index, 2 * rows :, :].astype(jnp.float32)
        ordered[pl.ds(at, rows), :LANES] = mixed.astype(jnp.bfloat16)
        ordered[pl.ds(at, rows), LANES:] = (cot * (normed * gains[0] + p[2])).astype(jnp.bfloat16)

    table_copies[0].wait()
    for index in range(blocks):
        data = ordered[index * BLOCK : (index + 1) * BLOCK, :]
        spectra[index] = jnp.dot(enter[...], data, preferred_element_type=jnp.float32)

    table_copies[2].wait()

    def forward_and_adjoint(low, high, one_product):
        for adjoint in (False, True):
            lanes = slice(LANES, 2 * LANES) if adjoint else slice(0, LANES)
            x_re = [spectra[j, low, lanes] for j in range(blocks)]
            x_im = [spectra[j, high, lanes] for j in range(blocks)]
            for i in range(blocks):
                terms = range(i, blocks) if adjoint else range(i + 1)
                re, im = one_product(adjoint, x_re, x_im, [(abs(i - j), j) for j in terms])
                product[i, low, lanes] = re
                product[i, high, lanes] = im

    def total(terms):
        terms = list(terms)
        return functools.reduce(lambda one, two: one + two, terms)

    def first_tile(adjoint, x_re, x_im, terms):
        f_re = [filt[d, 0, 0:8, :] for d in range(blocks)]
        first = lax.broadcasted_iota(jnp.int32, (8, LANES), 0) == 0
        imag = [filt[d, 1, 0:8, :] for d in range(blocks)]
        f_im = [jnp.where(first, 0.0, value) for value in imag]
        f_nq = [jnp.where(first, value, f_re[d]) for d, value in enumerate(imag)]
        direct = total(f_re[d] * x_re[j] for d, j in terms)
        crossed = total(f_im[d] * x_im[j] for d, j in terms)
        straight = total(f_nq[d] * x_im[j] for d, j in terms)
        turned = total(f_im[d] * x_re[j] for d, j in terms)
        if adjoint:
            return direct + crossed, straight - turned
        return direct - crossed, straight + turned

    forward_and_adjoint(slice(0, 8), slice(BLOCK, BLOCK + 8), first_tile)

    def products(tile, carry):
        low = pl.ds(pl.multiple_of(tile * 8, 8), 8)
        high = pl.ds(pl.multiple_of(BLOCK + tile * 8, 8), 8)
        f_re = [filt[d, 0, low, :] for d in range(blocks)]
        f_im = [filt[d, 1, low, :] for d in range(blocks)]
        f_less = [f_im[d] - f_re[d] for d in range(blocks)]
        f_more = [f_im[d] + f_re[d] for d in range(blocks)]

        def other_tile(adjoint, x_re, x_im, terms):
            both = total(f_re[d] * (x_re[j] + x_im[j]) for d, j in terms)
            if adjoint:
                return (
                    both + total(f_less[d] * x_im[j] for d, j in terms),
                    both - total(f_more[d] * x_re[j] for d, j in terms),
                )
            return (
                both - total(f_more[d] * x_im[j] for d, j in terms),
                both + total(f_less[d] * x_re[j] for d, j in terms),
            )

        forward_and_adjoint(low, high, other_tile)
        return carry

    lax.fori_loop(1, BLOCK // 8, products, 0)

    table_copies[1].wait()
    for index in range(blocks):
        left = jnp.dot(
            leave[...], product[index].astype(jnp.bfloat16), preferred_element_type=jnp.float32
        )
        ordered[index * BLOCK : (index + 1) * BLOCK, :] = left.astype(jnp.bfloat16)

    sums = [jnp.zeros((8, LANES), jnp.float32)] * 3
    for index in range(stored):
        at = pl.multiple_of(order_ref[index] * rows, rows)
        block = ordered[pl.ds(at, rows), :]
        out_ref[index, :rows, :] = block
        grad_mixed = block[:, LANES:].astype(jnp.float32)
        inv_saved = inv[:, 2 * index + 1 : 2 * index + 2]
        normed = raw_ref[index, rows : 2 * rows, :].astype(jnp.float32) * inv_saved
        once = grad_mixed * normed
        for power, term in enumerate((grad_mixed, once, once * normed)):
            sums[power] = sums[power] + fold(term)

    sums = jnp.concatenate(
        [jnp.sum(total, axis=0, keepdims=True) for total in sums]
        + [jnp.zeros((5, LANES), jnp.float32)],
        axis=0,
    )
    known = known_ref[...].astype(jnp.bfloat16)
    top = sums.astype(jnp.bfloat16)
    rest = (sums - top.astype(jnp.float32)).astype(jnp.bfloat16)
    for index in range(stored):
        out_ref[index, rows : rows + 16, :] = known
        out_ref[index, rows + 16 :, :LANES] = top
        out_ref[index, rows + 16 :, LANES:] = rest
        out_copies[index].start()
    for copy in out_copies:
        copy.wait()


def convolve(where, order, gathered, raw, inv, known, params, spectra, tables):
    stored = raw.shape[0]
    rows = raw.shape[1] // 3
    length = stored * rows
    blocks = length // BLOCK
    return pl.pallas_call(
        conv_kernel,
        out_shape=pltpu.HBM((stored, rows + 24, 2 * LANES), jnp.bfloat16),
        in_specs=[SMEM] * 3 + [VMEM] * 3 + [HBM] * 4,
        out_specs=HBM,
        scratch_shapes=[
            pltpu.VMEM(raw.shape, jnp.bfloat16),
            pltpu.VMEM(spectra.shape, jnp.float32),
            pltpu.VMEM((2 * BLOCK, BLOCK), jnp.bfloat16),
            pltpu.VMEM((BLOCK, 2 * BLOCK), jnp.bfloat16),
            pltpu.VMEM((stored, rows + 24, 2 * LANES), jnp.bfloat16),
            pltpu.VMEM((length, 2 * LANES), jnp.bfloat16),
            pltpu.VMEM((blocks, 2 * BLOCK, 2 * LANES), jnp.float32),
            pltpu.VMEM((blocks, 2 * BLOCK, 2 * LANES), jnp.float32),
            pltpu.VMEM((2 * stored, 128), jnp.float32),
            pltpu.VMEM((128, 128), jnp.float32),
            pltpu.SemaphoreType.DMA((stored,)),
            pltpu.SemaphoreType.DMA((3,)),
            pltpu.SemaphoreType.DMA((stored,)),
        ],
        name="convolve",
        compiler_params=pltpu.CompilerParams(vmem_limit_bytes=28 << 20),
    )(
        where, order, gathered, inv, known, params, in_hbm(spectra), in_hbm(raw),
        *[in_hbm(table) for table in tables],
    )


def forward_terms(at, inputs, conv, params_ref, inv_fwd):
    p = [params_ref[0, row : row + 1, at] for row in range(3)]
    query = inputs * inv_fwd * (p[0] * p[1]) + p[2]
    return inputs + query * conv


def backward_terms(at, saved, sconv, cot, grad_mixed, params_ref, inv_saved):
    p = [params_ref[0, row : row + 1, at] for row in range(7)]
    normed = saved * inv_saved
    mixed_grad = normed * (2.0 * p[0] * p[3] * p[5] * p[0]) + p[0] * (p[6] * p[3] + p[4] * p[5])
    grad_normed = cot * sconv * (p[1] * p[0]) + grad_mixed * mixed_grad
    return cot + inv_saved * grad_normed, grad_normed * normed


def leave_kernel(
    pipe_ref, inv_ref, back_ref, fwd_hbm, saved_ref, sconv_ref, cot_ref, params_ref,
    send_ref, keep_ref, cross_ref, inv, acc, fwd_ref, fwd_sem,
):
    rows, width = fwd_ref.shape[1:]
    fwd_copy = pltpu.make_async_copy(fwd_hbm, fwd_ref, fwd_sem)
    fwd_copy.start()
    inv[...] = rows_to_columns(inv_ref[0:8, :])
    inv_fwd = inv[:, 0:1]
    inv_saved = inv[:, 1:2]

    def both(layer_ref, partial_ref):
        cross = jnp.zeros((rows, LANES), jnp.float32)
        for group in range(width // LANES):
            at = pl.ds(group * LANES, LANES)
            partial, term = backward_terms(
                at,
                saved_ref[0, :, at].astype(jnp.float32),
                sconv_ref[0, :, at].astype(jnp.float32),
                cot_ref[0, :, at].astype(jnp.float32),
                back_ref[group, :rows, LANES:].astype(jnp.float32),
                params_ref,
                inv_saved,
            )
            cross = cross + term
            partial_ref[0, :, at] = partial.astype(jnp.bfloat16)
        acc[...] = cross
        fwd_copy.wait()
        for group in range(width // LANES):
            at = pl.ds(group * LANES, LANES)
            inputs = fwd_ref[0, :, at].astype(jnp.float32)
            conv = back_ref[group, :rows, :LANES].astype(jnp.float32)
            layer = forward_terms(at, inputs, conv, params_ref, inv_fwd)
            layer_ref[0, :, at] = layer.astype(jnp.bfloat16)

    @pl.when(pipe_ref[0] == 0)
    def _():
        both(send_ref, keep_ref)

    @pl.when(pipe_ref[0] != 0)
    def _():
        both(keep_ref, send_ref)

    cross = columns_to_rows([jnp.sum(acc[...], axis=1, keepdims=True)])
    cross_ref[...] = cross * (inv_ref[1:2, :] * inv_ref[1:2, :] / D)


def leave(pipe, inv, back, fwd_in, saved_in, saved_conv, grad_out, mix_params):
    return pl.pallas_call(
        leave_kernel,
        out_shape=(
            pltpu.VMEM(fwd_in.shape, jnp.bfloat16),
            pltpu.VMEM(fwd_in.shape, jnp.bfloat16),
            pltpu.VMEM((8, 128), jnp.float32),
        ),
        in_specs=[SMEM] + [VMEM] * 2 + [HBM] + [VMEM] * 4,
        out_specs=(VMEM, VMEM, VMEM),
        scratch_shapes=[pltpu.VMEM((fwd_in.shape[1], 128), jnp.float32)] * 2
        + [pltpu.VMEM(fwd_in.shape, jnp.bfloat16), pltpu.SemaphoreType.DMA],
        name="leave",
        compiler_params=pltpu.CompilerParams(vmem_limit_bytes=24 << 20),
    )(
        pipe, inv, in_vmem(back), in_hbm(fwd_in),
        *[in_vmem(a) for a in (saved_in, saved_conv, grad_out)], mix_params,
    )


def rows_kernel(
    pipe_ref, back_ref, send_ref, keep_ref, params_ref, layer_hbm, grads_ref, layer_sem
):
    first = pipe_ref[0] == 0
    stored, rows = back_ref.shape[0], send_ref.shape[1]
    sent = pltpu.make_async_copy(send_ref, layer_hbm, layer_sem)
    kept = pltpu.make_async_copy(keep_ref, layer_hbm, layer_sem)

    @pl.when(first)
    def _():
        sent.start()

    @pl.when(jnp.logical_not(first))
    def _():
        kept.start()

    known = back_ref[0, rows : rows + 16, :].astype(jnp.float32)
    for index in range(1, stored):
        known = known + back_ref[index, rows : rows + 16, :].astype(jnp.float32)
    for group in range(stored):
        own = pl.ds(group * LANES, LANES)
        p = [params_ref[0, row : row + 1, own] for row in range(7)]
        extra = back_ref[group, rows + 16 :, :].astype(jnp.float32)
        extra = extra[:, :LANES] + extra[:, LANES:]
        m0, m1, m2 = extra[0:1], extra[1:2], extra[2:3]
        row, side = group // 2, slice(group % 2 * LANES, (group % 2 + 1) * LANES)
        q0, q1 = known[row : row + 1, side], known[row + 8 : row + 9, side]
        key_normed = p[0] * p[5] * m2 + p[6] * m1
        value_normed = p[0] * p[3] * m2 + p[4] * m1
        grads = [
            p[1] * q1 + p[3] * key_normed + p[5] * value_normed,
            p[0] * q1,
            q0,
            p[0] * key_normed,
            p[0] * p[5] * m1 + p[6] * m0,
            p[0] * value_normed,
            p[0] * p[3] * m1 + p[4] * m0,
        ]
        grads_ref[0, :, own] = jnp.concatenate(grads, axis=0)

    @pl.when(first)
    def _():
        sent.wait()

    @pl.when(jnp.logical_not(first))
    def _():
        kept.wait()


def finish_rows(pipe, back, send, keep, mix_params):
    return pl.pallas_call(
        rows_kernel,
        out_shape=(
            pltpu.HBM(send.shape, jnp.bfloat16),
            jax.ShapeDtypeStruct(mix_params.shape, jnp.float32),
        ),
        in_specs=[SMEM] + [VMEM] * 4,
        out_specs=(HBM, VMEM),
        scratch_shapes=[pltpu.SemaphoreType.DMA],
        name="finish_rows",
        compiler_params=pltpu.CompilerParams(vmem_limit_bytes=8 << 20),
    )(pipe, in_vmem(back), in_vmem(send), in_vmem(keep), mix_params)


def cross_kernel(
    pipe_ref, s0, s1, s2, s3, send_ref, keep_ref, saved_ref, peer_ref, grad_hbm, term_ref,
    grad_ref, scale, grad_sem,
):
    first = pipe_ref[0] == 0
    steps = grad_sem.shape[0]
    wide = grad_ref.shape[1] // steps
    scale[...] = rows_to_columns(s0[...] + s1[...] + s2[...] + s3[...])
    copies = []
    for step in range(steps):
        for group in range(step * wide, (step + 1) * wide, LANES):
            at = pl.ds(group, LANES)
            partial = jnp.where(first, keep_ref[0, :, at], send_ref[0, :, at]).astype(jnp.float32)
            saved = saved_ref[0, :, at].astype(jnp.float32)
            grad_ref[:, at] = (partial - saved * scale[:, 0:1]).astype(jnp.bfloat16)
        chunk = pl.ds(step * wide, wide)
        copy = pltpu.make_async_copy(
            grad_ref.at[:, chunk], grad_hbm.at[0, :, chunk], grad_sem.at[step]
        )
        copy.start()
        copies.append(copy)
    for group in range(0, grad_ref.shape[1], LANES):
        at = pl.ds(group, LANES)
        term_ref[:, at] = peer_ref[0, :, at].astype(jnp.float32) * scale[:, 1:2]
    for copy in copies:
        copy.wait()


def finish_cross(pipe, scales, send, keep, saved_in, peer_saved):
    rows, width = saved_in.shape[1:]
    return pl.pallas_call(
        cross_kernel,
        out_shape=(
            pltpu.HBM(saved_in.shape, jnp.bfloat16),
            pltpu.VMEM((rows, width), jnp.float32),
        ),
        in_specs=[SMEM] + [VMEM] * 8,
        out_specs=(HBM, VMEM),
        scratch_shapes=[
            pltpu.VMEM((rows, width), jnp.bfloat16),
            pltpu.VMEM((rows, 128), jnp.float32),
            pltpu.SemaphoreType.DMA((4,)),
        ],
        name="finish_cross",
        compiler_params=pltpu.CompilerParams(vmem_limit_bytes=8 << 20),
    )(pipe, *scales, in_vmem(send), in_vmem(keep), in_vmem(saved_in), in_vmem(peer_saved))


def received_kernel(value_ref, term_ref, out_hbm, out_ref, out_sem):
    steps = out_sem.shape[0]
    wide = out_ref.shape[1] // steps
    copies = []
    for step in range(steps):
        for at in range(step * wide, (step + 1) * wide, LANES):
            own = pl.ds(at, LANES)
            value = value_ref[0, :, own].astype(jnp.float32)
            out_ref[:, own] = (value - term_ref[:, own]).astype(jnp.bfloat16)
        chunk = pl.ds(step * wide, wide)
        copy = pltpu.make_async_copy(
            out_ref.at[:, chunk], out_hbm.at[0, :, chunk], out_sem.at[step]
        )
        copy.start()
        copies.append(copy)
    for copy in copies:
        copy.wait()


def finish_received(value, term):
    rows, width = term.shape
    return pl.pallas_call(
        received_kernel,
        out_shape=pltpu.HBM(value.shape, jnp.bfloat16),
        in_specs=[VMEM, VMEM],
        out_specs=HBM,
        scratch_shapes=[
            pltpu.VMEM((rows, width), jnp.bfloat16),
            pltpu.SemaphoreType.DMA((8,)),
        ],
        name="received",
        compiler_params=pltpu.CompilerParams(vmem_limit_bytes=8 << 20),
    )(in_vmem(value), in_vmem(term))


def per_device(tables, fwd_in, saved_in, saved_conv, grad_out, filters, mix_params, span_order):
    where = lax.axis_index("seq").astype(jnp.int32).reshape(1)
    pipe = lax.axis_index("pipe").astype(jnp.int32).reshape(1)
    raw, sums = pack(fwd_in, saved_in, grad_out)
    raw = lax.all_to_all(raw, "seq", 0, 0)
    own_sums = sum(over_chan(sums))
    sums = own_sums[:2]
    sums = jnp.concatenate([sums, across(sums, 1)], axis=0)
    sums = jnp.concatenate([sums] + [round_ring(sums, apart) for apart in (1, 2, 3)], axis=0)
    inv = lax.rsqrt(jnp.concatenate([sums, across(sums, 8)], axis=0) / D + EPSILON)
    peer_saved = lax.ppermute(saved_in, "pipe", [(1, 0)])
    spectra = filter_spectra(where, filters, tables)
    known = early(own_sums, saved_in, saved_conv, grad_out)
    back = convolve(where, span_order, gather_order(), raw, inv, known, mix_params, spectra, tables)
    back = lax.all_to_all(back, "seq", 0, 0)
    outgoing, keep, cross = leave(
        pipe, inv, back, fwd_in, saved_in, saved_conv, grad_out, mix_params
    )
    peer_cross = lax.ppermute(cross, "pipe", [(1, 0)])
    incoming = lax.ppermute(outgoing, "pipe", [(0, 1), (1, 0)])
    scales = over_chan(jnp.concatenate([cross[:1], peer_cross[:1], cross[:6]], axis=0))
    layer_out, param_grad = finish_rows(pipe, back, outgoing, keep, mix_params)
    input_grad, term = finish_cross(pipe, scales, outgoing, keep, saved_in, peer_saved)
    received = finish_received(incoming, term)
    return (layer_out, input_grad, param_grad, received)


def solution(mesh):
    tables = transform_tables()
    in_specs = (
        P("pipe", "seq", "chan"),
        P("pipe", "seq", "chan"),
        P("pipe", "seq", "chan"),
        P("pipe", "seq", "chan"),
        P("pipe", None, "chan"),
        P("pipe", None, "chan"),
        P(),
    )
    out_specs = (
        P("pipe", "seq", "chan"),
        P("pipe", "seq", "chan"),
        P("pipe", None, "chan"),
        P("pipe", "seq", "chan"),
    )
    return jax.shard_map(
        functools.partial(per_device, tuple(jnp.asarray(table) for table in tables)),
        mesh=mesh,
        in_specs=in_specs,
        out_specs=out_specs,
        check_vma=False,
    )
```

```python
import functools

import jax
import jax.numpy as jnp
import ml_dtypes
import numpy as np
from jax import lax
from jax.experimental import pallas as pl
from jax.experimental.pallas import tpu as pltpu
from jax.sharding import PartitionSpec as P


D = 8192
EPSILON = 1e-05
BLOCK = 256
LANES = 128


def transform_tables():
    period = 2 * BLOCK
    freq = np.arange(BLOCK)[:, None]
    time = np.arange(BLOCK)[None, :]
    angle = 2.0 * np.pi / period * (freq * time % period)
    real, imag = np.cos(angle), -np.sin(angle)
    imag[0] = np.where(np.arange(BLOCK) % 2 == 0, 1.0, -1.0)
    enter = np.concatenate([real, imag], axis=0)
    angle = 2.0 * np.pi / period * (freq * (time + BLOCK) % period)
    real, imag = 2.0 * np.cos(angle), -2.0 * np.sin(angle)
    real[0] = 1.0
    imag[0] = np.where(np.arange(BLOCK) % 2 == 0, 1.0, -1.0)
    leave = np.concatenate([real, imag], axis=0).T / period
    return tuple(table.astype(np.float32).astype(ml_dtypes.bfloat16) for table in (enter, leave))


def rows_to_columns(rows):
    return jnp.concatenate([rows] * 16, axis=0).T


def columns_to_rows(columns):
    lane = lax.broadcasted_iota(jnp.int32, (128, 128), 1)
    square = jnp.zeros((128, 128), jnp.float32)
    for index, column in enumerate(columns):
        square = jnp.where(lane == index, column, square)
    return square.T[:8]


VMEM = pl.BlockSpec(memory_space=pltpu.VMEM)
SMEM = pl.BlockSpec(memory_space=pltpu.SMEM)


def in_vmem(array):
    return pltpu.with_memory_space_constraint(array, pltpu.VMEM)


HBM = pl.BlockSpec(memory_space=pl.ANY)


def in_hbm(array):
    return pltpu.with_memory_space_constraint(array, pltpu.HBM)


def lane_spec(rows, wide):
    return pl.BlockSpec((1, rows, wide), lambda step, *_: (0, 0, step))


def whole(shape):
    return pl.BlockSpec(shape, lambda step, *_: (0,) * len(shape))


def pack_kernel(fwd_hbm, saved_hbm, cot_hbm, out_hbm, squares_ref, held, in_sem, out_sem):
    rows, width = held.shape[1:]
    steps = in_sem.shape[1]
    wide = width // steps
    sources = (fwd_hbm, saved_hbm, cot_hbm)
    arriving = [
        [
            pltpu.make_async_copy(
                source.at[0, :, pl.ds(step * wide, wide)],
                held.at[index, :, pl.ds(step * wide, wide)],
                in_sem.at[index, step],
            )
            for index, source in enumerate(sources)
        ]
        for step in range(steps)
    ]
    for copies in arriving:
        for copy in copies:
            copy.start()
    leaving = []
    totals = [jnp.zeros((rows, LANES), jnp.float32)] * 2
    for step, copies in enumerate(arriving):
        for index, copy in enumerate(copies):
            copy.wait()
            for group in range(step * wide // LANES, (step + 1) * wide // LANES):
                out = pltpu.make_async_copy(
                    held.at[index, :, pl.ds(group * LANES, LANES)],
                    out_hbm.at[group, pl.ds(index * rows, rows), :],
                    out_sem.at[index, group],
                )
                out.start()
                leaving.append(out)
        for index in range(2):
            for group in range(step * wide // LANES, (step + 1) * wide // LANES):
                value = held[index, :, group * LANES : (group + 1) * LANES].astype(jnp.float32)
                totals[index] = totals[index] + value * value
    squares_ref[...] = columns_to_rows([jnp.sum(total, axis=1, keepdims=True) for total in totals])
    for copy in leaving:
        copy.wait()


def pack(fwd_in, saved_in, grad_out):
    rows, width = fwd_in.shape[1:]
    return pl.pallas_call(
        pack_kernel,
        out_shape=(
            pltpu.HBM((width // LANES, 3 * rows, LANES), jnp.bfloat16),
            jax.ShapeDtypeStruct((8, 128), jnp.float32),
        ),
        in_specs=[HBM] * 3,
        out_specs=(HBM, VMEM),
        scratch_shapes=[
            pltpu.VMEM((3, rows, width), jnp.bfloat16),
            pltpu.SemaphoreType.DMA((3, 4)),
            pltpu.SemaphoreType.DMA((3, width // LANES)),
        ],
        name="pack",
        compiler_params=pltpu.CompilerParams(vmem_limit_bytes=16 << 20),
    )(in_hbm(fwd_in), in_hbm(saved_in), in_hbm(grad_out))


def over_chan(rows):
    count = lax.axis_size("chan")
    got = [rows]
    for apart in range(1, count):
        got.append(
            lax.ppermute(rows, "chan", [(low, (low + apart) % count) for low in range(count)])
        )
    return got


def across(rows, flip):
    count = lax.axis_size("seq")
    return lax.ppermute(rows, "seq", [(low, low ^ flip) for low in range(count)])


def round_ring(rows, apart):
    count = lax.axis_size("seq")
    place = lambda low: low // 8 * 8 + (low + 2 * apart) % 8
    return lax.ppermute(rows, "seq", [(low, place(low)) for low in range(count)])


def gather_order():
    own = lax.axis_index("seq").astype(jnp.int32)
    block = jnp.arange(16, dtype=jnp.int32)
    core = (block ^ own) & 1
    back = (own // 2 - block // 2) % 4
    side = (block // 8) ^ (own // 8)
    return side * 8 + back * 2 + core


def early_kernel(sums_ref, saved_ref, sconv_ref, cot_ref, out_ref, inv):
    step = pl.program_id(0)

    @pl.when(step == 0)
    def _():
        inv[...] = rows_to_columns(lax.rsqrt(sums_ref[...] / D + EPSILON))

    inv_saved = inv[:, 1:2]
    pairs = saved_ref.shape[2] // (2 * LANES)
    half = out_ref.shape[0] // 2
    for pair in range(pairs):
        at = pl.ds(pair * 2 * LANES, 2 * LANES)
        normed = saved_ref[0, :, at].astype(jnp.float32) * inv_saved
        grad_query = cot_ref[0, :, at].astype(jnp.float32) * sconv_ref[0, :, at].astype(jnp.float32)
        row = step * pairs + pair
        out_ref[pl.ds(row, 1), :] = jnp.sum(grad_query, axis=0, keepdims=True)
        out_ref[pl.ds(row + half, 1), :] = jnp.sum(grad_query * normed, axis=0, keepdims=True)


def early(sums, saved_in, saved_conv, grad_out):
    rows, width = saved_in.shape[1:]
    wide = 512
    return pl.pallas_call(
        early_kernel,
        out_shape=jax.ShapeDtypeStruct((width // LANES, 2 * LANES), jnp.float32),
        grid=(width // wide,),
        in_specs=[VMEM] + [lane_spec(rows, wide)] * 3,
        out_specs=whole((width // LANES, 2 * LANES)),
        scratch_shapes=[pltpu.VMEM((rows, 128), jnp.float32)],
        name="early",
        compiler_params=pltpu.CompilerParams(vmem_limit_bytes=12 << 20),
    )(sums, in_hbm(saved_in), in_hbm(saved_conv), in_hbm(grad_out))


def side_by_side(ref, index):
    at = 2 * index * BLOCK
    return jnp.concatenate([ref[at : at + BLOCK, :], ref[at + BLOCK : at + 2 * BLOCK, :]], axis=1)


def filter_kernel(where_ref, taps_ref, enter, filt):
    del where_ref
    freq = lax.broadcasted_iota(jnp.int32, (2 * BLOCK, LANES), 0)
    parity = jnp.where(freq % 2 == 0, 1.0, -1.0)
    earlier = None
    for pair in range(filt.shape[0] // 2):
        pair_spectra = jnp.dot(
            enter[...], side_by_side(taps_ref.at[0], pair), preferred_element_type=jnp.float32
        )
        for side in range(2):
            current = pair_spectra[:, side * LANES : (side + 1) * LANES]
            both = parity * current
            if earlier is not None:
                both = both + earlier
            earlier = current
            filt[2 * pair + side, 0] = both[:BLOCK]
            filt[2 * pair + side, 1] = both[BLOCK:]


def filter_spectra(where, filters, tables):
    length = filters.shape[1]
    shape = (length // BLOCK, 2, BLOCK, LANES)
    return pl.pallas_call(
        filter_kernel,
        out_shape=pltpu.HBM(shape, jnp.float32),
        grid_spec=pltpu.PrefetchScalarGridSpec(
            num_scalar_prefetch=1,
            grid=(1,),
            in_specs=[pl.BlockSpec((1, length, LANES), lambda step, at: (0, 0, at[0]))]
            + [whole(tables[0].shape)],
            out_specs=whole(shape),
        ),
        name="filter_spectra",
        compiler_params=pltpu.CompilerParams(vmem_limit_bytes=16 << 20),
    )(where, in_hbm(filters), in_hbm(tables[0]))


def fold(block):
    return jnp.sum(block.reshape(block.shape[0] // 8, 8, LANES), axis=0)


def conv_kernel(
    where_ref, order_ref, gathered_ref, inv_ref, known_ref, params_ref, filt_hbm, raw_hbm, enter_hbm,
    leave_hbm, out_hbm, raw_ref, filt, enter, leave, out_ref, ordered, spectra, product, inv_rows, inv, raw_sem, table_sem, out_sem,
):
    stored = raw_ref.shape[0]
    raw_copies = [
        pltpu.make_async_copy(raw_hbm.at[index], raw_ref.at[index], raw_sem.at[index])
        for index in range(stored)
    ]
    table_copies = [
        pltpu.make_async_copy(source, target, table_sem.at[index])
        for index, (source, target) in enumerate(
            ((enter_hbm, enter), (leave_hbm, leave), (filt_hbm, filt))
        )
    ]
    out_copies = [
        pltpu.make_async_copy(out_ref.at[index], out_hbm.at[index], out_sem.at[index])
        for index in range(stored)
    ]
    for copy in raw_copies + table_copies:
        copy.start()
    rows = raw_ref.shape[1] // 3
    blocks = stored * rows // BLOCK
    lanes = pl.ds(pl.multiple_of(where_ref[0] * LANES, LANES), LANES)
    p = [params_ref[0, row : row + 1, lanes] for row in range(7)]

    gains = [p[0] * p[1], p[0] * p[3], p[0] * p[5]]
    for index in range(stored):
        inv_rows[2 * index : 2 * index + 2, :] = inv_ref[pl.ds(2 * gathered_ref[index], 2), :]
    inv[...] = jnp.concatenate([inv_rows[...]] * (128 // (2 * stored)), axis=0).T
    for index in range(stored):
        if index % 4 == 0:
            for copy in raw_copies[index : index + 4]:
                copy.wait()
        at = pl.multiple_of(order_ref[index] * rows, rows)
        inv_fwd = inv[:, 2 * index : 2 * index + 1]
        inv_saved = inv[:, 2 * index + 1 : 2 * index + 2]
        normed = raw_ref[index, :rows, :].astype(jnp.float32) * inv_fwd
        mixed = (normed * gains[1] + p[4]) * (normed * gains[2] + p[6])
        normed = raw_ref[index, rows : 2 * rows, :].astype(jnp.float32) * inv_saved
        cot = raw_ref[index, 2 * rows :, :].astype(jnp.float32)
        ordered[pl.ds(at, rows), :LANES] = mixed.astype(jnp.bfloat16)
        ordered[pl.ds(at, rows), LANES:] = (cot * (normed * gains[0] + p[2])).astype(jnp.bfloat16)

    table_copies[0].wait()
    for index in range(blocks):
        data = ordered[index * BLOCK : (index + 1) * BLOCK, :]
        spectra[index] = jnp.dot(enter[...], data, preferred_element_type=jnp.float32)

    table_copies[2].wait()

    def forward_and_adjoint(low, high, one_product):
        for adjoint in (False, True):
            lanes = slice(LANES, 2 * LANES) if adjoint else slice(0, LANES)
            x_re = [spectra[j, low, lanes] for j in range(blocks)]
            x_im = [spectra[j, high, lanes] for j in range(blocks)]
            for i in range(blocks):
                terms = range(i, blocks) if adjoint else range(i + 1)
                re, im = one_product(adjoint, x_re, x_im, [(abs(i - j), j) for j in terms])
                product[i, low, lanes] = re
                product[i, high, lanes] = im

    def total(terms):
        terms = list(terms)
        return functools.reduce(lambda one, two: one + two, terms)

    def first_tile(adjoint, x_re, x_im, terms):
        f_re = [filt[d, 0, 0:8, :] for d in range(blocks)]
        first = lax.broadcasted_iota(jnp.int32, (8, LANES), 0) == 0
        imag = [filt[d, 1, 0:8, :] for d in range(blocks)]
        f_im = [jnp.where(first, 0.0, value) for value in imag]
        f_nq = [jnp.where(first, value, f_re[d]) for d, value in enumerate(imag)]
        direct = total(f_re[d] * x_re[j] for d, j in terms)
        crossed = total(f_im[d] * x_im[j] for d, j in terms)
        straight = total(f_nq[d] * x_im[j] for d, j in terms)
        turned = total(f_im[d] * x_re[j] for d, j in terms)
        if adjoint:
            return direct + crossed, straight - turned
        return direct - crossed, straight + turned

    forward_and_adjoint(slice(0, 8), slice(BLOCK, BLOCK + 8), first_tile)

    def products(tile, carry):
        low = pl.ds(pl.multiple_of(tile * 8, 8), 8)
        high = pl.ds(pl.multiple_of(BLOCK + tile * 8, 8), 8)
        f_re = [filt[d, 0, low, :] for d in range(blocks)]
        f_im = [filt[d, 1, low, :] for d in range(blocks)]
        f_less = [f_im[d] - f_re[d] for d in range(blocks)]
        f_more = [f_im[d] + f_re[d] for d in range(blocks)]

        def other_tile(adjoint, x_re, x_im, terms):
            both = total(f_re[d] * (x_re[j] + x_im[j]) for d, j in terms)
            if adjoint:
                return (
                    both + total(f_less[d] * x_im[j] for d, j in terms),
                    both - total(f_more[d] * x_re[j] for d, j in terms),
                )
            return (
                both - total(f_more[d] * x_im[j] for d, j in terms),
                both + total(f_less[d] * x_re[j] for d, j in terms),
            )

        forward_and_adjoint(low, high, other_tile)
        return carry

    lax.fori_loop(1, BLOCK // 8, products, 0)

    table_copies[1].wait()
    for index in range(blocks):
        left = jnp.dot(
            leave[...], product[index].astype(jnp.bfloat16), preferred_element_type=jnp.float32
        )
        ordered[index * BLOCK : (index + 1) * BLOCK, :] = left.astype(jnp.bfloat16)

    sums = [jnp.zeros((8, LANES), jnp.float32)] * 3
    for index in range(stored):
        at = pl.multiple_of(order_ref[index] * rows, rows)
        block = ordered[pl.ds(at, rows), :]
        out_ref[index, :rows, :] = block
        grad_mixed = block[:, LANES:].astype(jnp.float32)
        inv_saved = inv[:, 2 * index + 1 : 2 * index + 2]
        normed = raw_ref[index, rows : 2 * rows, :].astype(jnp.float32) * inv_saved
        once = grad_mixed * normed
        for power, term in enumerate((grad_mixed, once, once * normed)):
            sums[power] = sums[power] + fold(term)

    sums = jnp.concatenate(
        [jnp.sum(total, axis=0, keepdims=True) for total in sums]
        + [jnp.zeros((5, LANES), jnp.float32)],
        axis=0,
    )
    known = known_ref[...].astype(jnp.bfloat16)
    top = sums.astype(jnp.bfloat16)
    rest = (sums - top.astype(jnp.float32)).astype(jnp.bfloat16)
    for index in range(stored):
        out_ref[index, rows : rows + 16, :] = known
        out_ref[index, rows + 16 :, :LANES] = top
        out_ref[index, rows + 16 :, LANES:] = rest
        out_copies[index].start()
    for copy in out_copies:
        copy.wait()


def convolve(where, order, gathered, raw, inv, known, params, spectra, tables):
    stored = raw.shape[0]
    rows = raw.shape[1] // 3
    length = stored * rows
    blocks = length // BLOCK
    return pl.pallas_call(
        conv_kernel,
        out_shape=pltpu.HBM((stored, rows + 24, 2 * LANES), jnp.bfloat16),
        in_specs=[SMEM] * 3 + [VMEM] * 3 + [HBM] * 4,
        out_specs=HBM,
        scratch_shapes=[
            pltpu.VMEM(raw.shape, jnp.bfloat16),
            pltpu.VMEM(spectra.shape, jnp.float32),
            pltpu.VMEM((2 * BLOCK, BLOCK), jnp.bfloat16),
            pltpu.VMEM((BLOCK, 2 * BLOCK), jnp.bfloat16),
            pltpu.VMEM((stored, rows + 24, 2 * LANES), jnp.bfloat16),
            pltpu.VMEM((length, 2 * LANES), jnp.bfloat16),
            pltpu.VMEM((blocks, 2 * BLOCK, 2 * LANES), jnp.float32),
            pltpu.VMEM((blocks, 2 * BLOCK, 2 * LANES), jnp.float32),
            pltpu.VMEM((2 * stored, 128), jnp.float32),
            pltpu.VMEM((128, 128), jnp.float32),
            pltpu.SemaphoreType.DMA((stored,)),
            pltpu.SemaphoreType.DMA((3,)),
            pltpu.SemaphoreType.DMA((stored,)),
        ],
        name="convolve",
        compiler_params=pltpu.CompilerParams(vmem_limit_bytes=28 << 20),
    )(
        where, order, gathered, inv, known, params, in_hbm(spectra), in_hbm(raw),
        *[in_hbm(table) for table in tables],
    )


def forward_terms(at, inputs, conv, params_ref, inv_fwd):
    p = [params_ref[0, row : row + 1, at] for row in range(3)]
    query = inputs * inv_fwd * (p[0] * p[1]) + p[2]
    return inputs + query * conv


def backward_terms(at, saved, sconv, cot, grad_mixed, params_ref, inv_saved):
    p = [params_ref[0, row : row + 1, at] for row in range(7)]
    normed = saved * inv_saved
    mixed_grad = normed * (2.0 * p[0] * p[3] * p[5] * p[0]) + p[0] * (p[6] * p[3] + p[4] * p[5])
    grad_normed = cot * sconv * (p[1] * p[0]) + grad_mixed * mixed_grad
    return cot + inv_saved * grad_normed, grad_normed * normed


def leave_kernel(
    pipe_ref, inv_ref, back_ref, fwd_hbm, saved_ref, sconv_ref, cot_ref, params_ref,
    send_ref, keep_ref, cross_ref, inv, acc, fwd_ref, fwd_sem,
):
    rows, width = fwd_ref.shape[1:]
    fwd_copy = pltpu.make_async_copy(fwd_hbm, fwd_ref, fwd_sem)
    fwd_copy.start()
    inv[...] = rows_to_columns(inv_ref[0:8, :])
    inv_fwd = inv[:, 0:1]
    inv_saved = inv[:, 1:2]

    def both(layer_ref, partial_ref):
        cross = jnp.zeros((rows, LANES), jnp.float32)
        for group in range(width // LANES):
            at = pl.ds(group * LANES, LANES)
            partial, term = backward_terms(
                at,
                saved_ref[0, :, at].astype(jnp.float32),
                sconv_ref[0, :, at].astype(jnp.float32),
                cot_ref[0, :, at].astype(jnp.float32),
                back_ref[group, :rows, LANES:].astype(jnp.float32),
                params_ref,
                inv_saved,
            )
            cross = cross + term
            partial_ref[0, :, at] = partial.astype(jnp.bfloat16)
        acc[...] = cross
        fwd_copy.wait()
        for group in range(width // LANES):
            at = pl.ds(group * LANES, LANES)
            inputs = fwd_ref[0, :, at].astype(jnp.float32)
            conv = back_ref[group, :rows, :LANES].astype(jnp.float32)
            layer = forward_terms(at, inputs, conv, params_ref, inv_fwd)
            layer_ref[0, :, at] = layer.astype(jnp.bfloat16)

    @pl.when(pipe_ref[0] == 0)
    def _():
        both(send_ref, keep_ref)

    @pl.when(pipe_ref[0] != 0)
    def _():
        both(keep_ref, send_ref)

    cross = columns_to_rows([jnp.sum(acc[...], axis=1, keepdims=True)])
    cross_ref[...] = cross * (inv_ref[1:2, :] * inv_ref[1:2, :] / D)


def leave(pipe, inv, back, fwd_in, saved_in, saved_conv, grad_out, mix_params):
    return pl.pallas_call(
        leave_kernel,
        out_shape=(
            pltpu.VMEM(fwd_in.shape, jnp.bfloat16),
            pltpu.VMEM(fwd_in.shape, jnp.bfloat16),
            pltpu.VMEM((8, 128), jnp.float32),
        ),
        in_specs=[SMEM] + [VMEM] * 2 + [HBM] + [VMEM] * 4,
        out_specs=(VMEM, VMEM, VMEM),
        scratch_shapes=[pltpu.VMEM((fwd_in.shape[1], 128), jnp.float32)] * 2
        + [pltpu.VMEM(fwd_in.shape, jnp.bfloat16), pltpu.SemaphoreType.DMA],
        name="leave",
        compiler_params=pltpu.CompilerParams(vmem_limit_bytes=24 << 20),
    )(
        pipe, inv, in_vmem(back), in_hbm(fwd_in),
        *[in_vmem(a) for a in (saved_in, saved_conv, grad_out)], mix_params,
    )


def rows_kernel(
    pipe_ref, back_ref, send_ref, keep_ref, params_ref, layer_hbm, grads_ref, layer_sem
):
    first = pipe_ref[0] == 0
    stored, rows = back_ref.shape[0], send_ref.shape[1]
    sent = pltpu.make_async_copy(send_ref, layer_hbm, layer_sem)
    kept = pltpu.make_async_copy(keep_ref, layer_hbm, layer_sem)

    @pl.when(first)
    def _():
        sent.start()

    @pl.when(jnp.logical_not(first))
    def _():
        kept.start()

    known = back_ref[0, rows : rows + 16, :].astype(jnp.float32)
    for index in range(1, stored):
        known = known + back_ref[index, rows : rows + 16, :].astype(jnp.float32)
    for group in range(stored):
        own = pl.ds(group * LANES, LANES)
        p = [params_ref[0, row : row + 1, own] for row in range(7)]
        extra = back_ref[group, rows + 16 :, :].astype(jnp.float32)
        extra = extra[:, :LANES] + extra[:, LANES:]
        m0, m1, m2 = extra[0:1], extra[1:2], extra[2:3]
        row, side = group // 2, slice(group % 2 * LANES, (group % 2 + 1) * LANES)
        q0, q1 = known[row : row + 1, side], known[row + 8 : row + 9, side]
        key_normed = p[0] * p[5] * m2 + p[6] * m1
        value_normed = p[0] * p[3] * m2 + p[4] * m1
        grads = [
            p[1] * q1 + p[3] * key_normed + p[5] * value_normed,
            p[0] * q1,
            q0,
            p[0] * key_normed,
            p[0] * p[5] * m1 + p[6] * m0,
            p[0] * value_normed,
            p[0] * p[3] * m1 + p[4] * m0,
        ]
        for index, value in enumerate(grads):
            grads_ref[index, :, own] = value

    @pl.when(first)
    def _():
        sent.wait()

    @pl.when(jnp.logical_not(first))
    def _():
        kept.wait()


def finish_rows(pipe, back, send, keep, mix_params):
    return pl.pallas_call(
        rows_kernel,
        out_shape=(
            pltpu.HBM(send.shape, jnp.bfloat16),
            jax.ShapeDtypeStruct((7, 1, send.shape[2]), jnp.float32),
        ),
        in_specs=[SMEM] + [VMEM] * 4,
        out_specs=(HBM, VMEM),
        scratch_shapes=[pltpu.SemaphoreType.DMA],
        name="finish_rows",
        compiler_params=pltpu.CompilerParams(vmem_limit_bytes=8 << 20),
    )(pipe, in_vmem(back), in_vmem(send), in_vmem(keep), mix_params)


def cross_kernel(
    pipe_ref, s0, s1, s2, s3, send_ref, keep_ref, saved_ref, peer_ref, grad_hbm, term_ref,
    grad_ref, scale, grad_sem,
):
    first = pipe_ref[0] == 0
    steps = grad_sem.shape[0]
    wide = grad_ref.shape[1] // steps
    scale[...] = rows_to_columns(s0[...] + s1[...] + s2[...] + s3[...])
    copies = []
    for step in range(steps):
        for group in range(step * wide, (step + 1) * wide, LANES):
            at = pl.ds(group, LANES)
            partial = jnp.where(first, keep_ref[0, :, at], send_ref[0, :, at]).astype(jnp.float32)
            saved = saved_ref[0, :, at].astype(jnp.float32)
            grad_ref[:, at] = (partial - saved * scale[:, 0:1]).astype(jnp.bfloat16)
        chunk = pl.ds(step * wide, wide)
        copy = pltpu.make_async_copy(
            grad_ref.at[:, chunk], grad_hbm.at[0, :, chunk], grad_sem.at[step]
        )
        copy.start()
        copies.append(copy)
    for group in range(0, grad_ref.shape[1], LANES):
        at = pl.ds(group, LANES)
        term_ref[:, at] = peer_ref[0, :, at].astype(jnp.float32) * scale[:, 1:2]
    for copy in copies:
        copy.wait()


def finish_cross(pipe, scales, send, keep, saved_in, peer_saved):
    rows, width = saved_in.shape[1:]
    return pl.pallas_call(
        cross_kernel,
        out_shape=(
            pltpu.HBM(saved_in.shape, jnp.bfloat16),
            pltpu.VMEM((rows, width), jnp.float32),
        ),
        in_specs=[SMEM] + [VMEM] * 8,
        out_specs=(HBM, VMEM),
        scratch_shapes=[
            pltpu.VMEM((rows, width), jnp.bfloat16),
            pltpu.VMEM((rows, 128), jnp.float32),
            pltpu.SemaphoreType.DMA((4,)),
        ],
        name="finish_cross",
        compiler_params=pltpu.CompilerParams(vmem_limit_bytes=8 << 20),
    )(pipe, *scales, in_vmem(send), in_vmem(keep), in_vmem(saved_in), in_vmem(peer_saved))


def received_kernel(value_ref, term_ref, out_hbm, out_ref, out_sem):
    steps = out_sem.shape[0]
    wide = out_ref.shape[1] // steps
    copies = []
    for step in range(steps):
        for at in range(step * wide, (step + 1) * wide, LANES):
            own = pl.ds(at, LANES)
            value = value_ref[0, :, own].astype(jnp.float32)
            out_ref[:, own] = (value - term_ref[:, own]).astype(jnp.bfloat16)
        chunk = pl.ds(step * wide, wide)
        copy = pltpu.make_async_copy(
            out_ref.at[:, chunk], out_hbm.at[0, :, chunk], out_sem.at[step]
        )
        copy.start()
        copies.append(copy)
    for copy in copies:
        copy.wait()


def finish_received(value, term):
    rows, width = term.shape
    return pl.pallas_call(
        received_kernel,
        out_shape=pltpu.HBM(value.shape, jnp.bfloat16),
        in_specs=[VMEM, VMEM],
        out_specs=HBM,
        scratch_shapes=[
            pltpu.VMEM((rows, width), jnp.bfloat16),
            pltpu.SemaphoreType.DMA((8,)),
        ],
        name="received",
        compiler_params=pltpu.CompilerParams(vmem_limit_bytes=8 << 20),
    )(in_vmem(value), in_vmem(term))


def per_device(tables, fwd_in, saved_in, saved_conv, grad_out, filters, mix_params, span_order):
    where = lax.axis_index("seq").astype(jnp.int32).reshape(1)
    pipe = lax.axis_index("pipe").astype(jnp.int32).reshape(1)
    raw, sums = pack(fwd_in, saved_in, grad_out)
    raw = lax.all_to_all(raw, "seq", 0, 0)
    own_sums = sum(over_chan(sums))
    sums = own_sums[:2]
    sums = jnp.concatenate([sums, across(sums, 1)], axis=0)
    sums = jnp.concatenate([sums] + [round_ring(sums, apart) for apart in (1, 2, 3)], axis=0)
    inv = lax.rsqrt(jnp.concatenate([sums, across(sums, 8)], axis=0) / D + EPSILON)
    peer_saved = lax.ppermute(saved_in, "pipe", [(1, 0)])
    spectra = filter_spectra(where, filters, tables)
    known = early(own_sums, saved_in, saved_conv, grad_out)
    back = convolve(where, span_order, gather_order(), raw, inv, known, mix_params, spectra, tables)
    back = lax.all_to_all(back, "seq", 0, 0)
    outgoing, keep, cross = leave(
        pipe, inv, back, fwd_in, saved_in, saved_conv, grad_out, mix_params
    )
    peer_cross = lax.ppermute(cross, "pipe", [(1, 0)])
    incoming = lax.ppermute(outgoing, "pipe", [(0, 1), (1, 0)])
    scales = over_chan(jnp.concatenate([cross[:1], peer_cross[:1], cross[:6]], axis=0))
    layer_out, param_grad = finish_rows(pipe, back, outgoing, keep, mix_params)
    input_grad, term = finish_cross(pipe, scales, outgoing, keep, saved_in, peer_saved)
    received = finish_received(incoming, term)
    return (layer_out, input_grad, param_grad.transpose(1, 0, 2), received)


def solution(mesh):
    tables = transform_tables()
    in_specs = (
        P("pipe", "seq", "chan"),
        P("pipe", "seq", "chan"),
        P("pipe", "seq", "chan"),
        P("pipe", "seq", "chan"),
        P("pipe", None, "chan"),
        P("pipe", None, "chan"),
        P(),
    )
    out_specs = (
        P("pipe", "seq", "chan"),
        P("pipe", "seq", "chan"),
        P("pipe", None, "chan"),
        P("pipe", "seq", "chan"),
    )
    return jax.shard_map(
        functools.partial(per_device, tuple(jnp.asarray(table) for table in tables)),
        mesh=mesh,
        in_specs=in_specs,
        out_specs=out_specs,
        check_vma=False,
    )
```

```python
import functools

import jax
import jax.numpy as jnp
import ml_dtypes
import numpy as np
from jax import lax
from jax.experimental import pallas as pl
from jax.experimental.pallas import tpu as pltpu
from jax.sharding import PartitionSpec as P


D = 8192
EPSILON = 1e-05
BLOCK = 256
LANES = 128


def transform_tables():
    period = 2 * BLOCK
    freq = np.arange(BLOCK)[:, None]
    time = np.arange(BLOCK)[None, :]
    angle = 2.0 * np.pi / period * (freq * time % period)
    real, imag = np.cos(angle), -np.sin(angle)
    imag[0] = np.where(np.arange(BLOCK) % 2 == 0, 1.0, -1.0)
    enter = np.concatenate([real, imag], axis=0)
    angle = 2.0 * np.pi / period * (freq * (time + BLOCK) % period)
    real, imag = 2.0 * np.cos(angle), -2.0 * np.sin(angle)
    real[0] = 1.0
    imag[0] = np.where(np.arange(BLOCK) % 2 == 0, 1.0, -1.0)
    leave = np.concatenate([real, imag], axis=0).T / period
    return tuple(table.astype(np.float32).astype(ml_dtypes.bfloat16) for table in (enter, leave))


def rows_to_columns(rows):
    return jnp.concatenate([rows] * 16, axis=0).T


def columns_to_rows(columns):
    lane = lax.broadcasted_iota(jnp.int32, (128, 128), 1)
    square = jnp.zeros((128, 128), jnp.float32)
    for index, column in enumerate(columns):
        square = jnp.where(lane == index, column, square)
    return square.T[:8]


VMEM = pl.BlockSpec(memory_space=pltpu.VMEM)
SMEM = pl.BlockSpec(memory_space=pltpu.SMEM)


def in_vmem(array):
    return pltpu.with_memory_space_constraint(array, pltpu.VMEM)


HBM = pl.BlockSpec(memory_space=pl.ANY)


def in_hbm(array):
    return pltpu.with_memory_space_constraint(array, pltpu.HBM)


def lane_spec(rows, wide):
    return pl.BlockSpec((1, rows, wide), lambda step, *_: (0, 0, step))


def whole(shape):
    return pl.BlockSpec(shape, lambda step, *_: (0,) * len(shape))


def pack_kernel(fwd_hbm, saved_hbm, cot_hbm, out_hbm, squares_ref, held, in_sem, out_sem):
    rows, width = held.shape[1:]
    steps = in_sem.shape[1]
    wide = width // steps
    sources = (fwd_hbm, saved_hbm, cot_hbm)
    arriving = [
        [
            pltpu.make_async_copy(
                source.at[0, :, pl.ds(step * wide, wide)],
                held.at[index, :, pl.ds(step * wide, wide)],
                in_sem.at[index, step],
            )
            for index, source in enumerate(sources)
        ]
        for step in range(steps)
    ]
    for copies in arriving:
        for copy in copies:
            copy.start()
    leaving = []
    totals = [jnp.zeros((rows, LANES), jnp.float32)] * 2
    for step, copies in enumerate(arriving):
        for index, copy in enumerate(copies):
            copy.wait()
            for group in range(step * wide // LANES, (step + 1) * wide // LANES):
                out = pltpu.make_async_copy(
                    held.at[index, :, pl.ds(group * LANES, LANES)],
                    out_hbm.at[group, pl.ds(index * rows, rows), :],
                    out_sem.at[index, group],
                )
                out.start()
                leaving.append(out)
        for index in range(2):
            for group in range(step * wide // LANES, (step + 1) * wide // LANES):
                value = held[index, :, group * LANES : (group + 1) * LANES].astype(jnp.float32)
                totals[index] = totals[index] + value * value
    squares_ref[...] = columns_to_rows([jnp.sum(total, axis=1, keepdims=True) for total in totals])
    for copy in leaving:
        copy.wait()


def pack(fwd_in, saved_in, grad_out):
    rows, width = fwd_in.shape[1:]
    return pl.pallas_call(
        pack_kernel,
        out_shape=(
            pltpu.HBM((width // LANES, 3 * rows, LANES), jnp.bfloat16),
            jax.ShapeDtypeStruct((8, 128), jnp.float32),
        ),
        in_specs=[HBM] * 3,
        out_specs=(HBM, VMEM),
        scratch_shapes=[
            pltpu.VMEM((3, rows, width), jnp.bfloat16),
            pltpu.SemaphoreType.DMA((3, 4)),
            pltpu.SemaphoreType.DMA((3, width // LANES)),
        ],
        name="pack",
        compiler_params=pltpu.CompilerParams(vmem_limit_bytes=16 << 20),
    )(in_hbm(fwd_in), in_hbm(saved_in), in_hbm(grad_out))


def over_chan(rows):
    count = lax.axis_size("chan")
    got = [rows]
    for apart in range(1, count):
        got.append(
            lax.ppermute(rows, "chan", [(low, (low + apart) % count) for low in range(count)])
        )
    return got


def across(rows, flip):
    count = lax.axis_size("seq")
    return lax.ppermute(rows, "seq", [(low, low ^ flip) for low in range(count)])


def round_ring(rows, apart):
    count = lax.axis_size("seq")
    place = lambda low: low // 8 * 8 + (low + 2 * apart) % 8
    return lax.ppermute(rows, "seq", [(low, place(low)) for low in range(count)])


def gather_order():
    own = lax.axis_index("seq").astype(jnp.int32)
    block = jnp.arange(16, dtype=jnp.int32)
    core = (block ^ own) & 1
    back = (own // 2 - block // 2) % 4
    side = (block // 8) ^ (own // 8)
    return side * 8 + back * 2 + core


def early_kernel(sums_ref, saved_ref, sconv_ref, cot_ref, out_ref, inv):
    step = pl.program_id(0)

    @pl.when(step == 0)
    def _():
        inv[...] = rows_to_columns(lax.rsqrt(sums_ref[...] / D + EPSILON))

    inv_saved = inv[:, 1:2]
    groups = saved_ref.shape[2] // LANES
    half = out_ref.shape[0] // 2
    for group in range(groups):
        at = pl.ds(group * LANES, LANES)
        normed = saved_ref[0, :, at].astype(jnp.float32) * inv_saved
        grad_query = cot_ref[0, :, at].astype(jnp.float32) * sconv_ref[0, :, at].astype(jnp.float32)
        row = step * groups + group
        out_ref[pl.ds(row, 1), :] = jnp.sum(grad_query, axis=0, keepdims=True)
        out_ref[pl.ds(row + half, 1), :] = jnp.sum(grad_query * normed, axis=0, keepdims=True)


def early(sums, saved_in, saved_conv, grad_out):
    rows, width = saved_in.shape[1:]
    wide = 512
    shape = (2 * width // LANES, LANES)
    return pl.pallas_call(
        early_kernel,
        out_shape=jax.ShapeDtypeStruct(shape, jnp.float32),
        grid=(width // wide,),
        in_specs=[VMEM] + [lane_spec(rows, wide)] * 3,
        out_specs=whole(shape),
        scratch_shapes=[pltpu.VMEM((rows, 128), jnp.float32)],
        name="early",
        compiler_params=pltpu.CompilerParams(vmem_limit_bytes=12 << 20),
    )(sums, in_vmem(saved_in), in_vmem(saved_conv), in_vmem(grad_out))


def side_by_side(ref, index):
    at = 2 * index * BLOCK
    return jnp.concatenate([ref[at : at + BLOCK, :], ref[at + BLOCK : at + 2 * BLOCK, :]], axis=1)


def filter_kernel(where_ref, taps_ref, enter, filt):
    del where_ref
    freq = lax.broadcasted_iota(jnp.int32, (2 * BLOCK, LANES), 0)
    parity = jnp.where(freq % 2 == 0, 1.0, -1.0)
    earlier = None
    for pair in range(filt.shape[0] // 2):
        pair_spectra = jnp.dot(
            enter[...], side_by_side(taps_ref.at[0], pair), preferred_element_type=jnp.float32
        )
        for side in range(2):
            current = pair_spectra[:, side * LANES : (side + 1) * LANES]
            both = parity * current
            if earlier is not None:
                both = both + earlier
            earlier = current
            filt[2 * pair + side, 0] = both[:BLOCK]
            filt[2 * pair + side, 1] = both[BLOCK:]


def filter_spectra(where, filters, tables):
    length = filters.shape[1]
    shape = (length // BLOCK, 2, BLOCK, LANES)
    return pl.pallas_call(
        filter_kernel,
        out_shape=pltpu.HBM(shape, jnp.float32),
        grid_spec=pltpu.PrefetchScalarGridSpec(
            num_scalar_prefetch=1,
            grid=(1,),
            in_specs=[pl.BlockSpec((1, length, LANES), lambda step, at: (0, 0, at[0]))]
            + [whole(tables[0].shape)],
            out_specs=whole(shape),
        ),
        name="filter_spectra",
        compiler_params=pltpu.CompilerParams(vmem_limit_bytes=16 << 20),
    )(where, in_hbm(filters), in_hbm(tables[0]))


def fold(block):
    return jnp.sum(block.reshape(block.shape[0] // 8, 8, LANES), axis=0)


def conv_kernel(
    where_ref, order_ref, gathered_ref, inv_ref, params_ref, filt_hbm, raw_hbm, enter_hbm,
    leave_hbm, out_hbm, raw_ref, filt, enter, leave, out_ref, ordered, spectra, product, inv_rows, inv, raw_sem, table_sem, out_sem,
):
    stored = raw_ref.shape[0]
    raw_copies = [
        pltpu.make_async_copy(raw_hbm.at[index], raw_ref.at[index], raw_sem.at[index])
        for index in range(stored)
    ]
    table_copies = [
        pltpu.make_async_copy(source, target, table_sem.at[index])
        for index, (source, target) in enumerate(
            ((enter_hbm, enter), (leave_hbm, leave), (filt_hbm, filt))
        )
    ]
    out_copies = [
        pltpu.make_async_copy(out_ref.at[index], out_hbm.at[index], out_sem.at[index])
        for index in range(stored)
    ]
    for copy in raw_copies + table_copies:
        copy.start()
    rows = raw_ref.shape[1] // 3
    blocks = stored * rows // BLOCK
    lanes = pl.ds(pl.multiple_of(where_ref[0] * LANES, LANES), LANES)
    p = [params_ref[0, row : row + 1, lanes] for row in range(7)]

    gains = [p[0] * p[1], p[0] * p[3], p[0] * p[5]]
    for index in range(stored):
        inv_rows[2 * index : 2 * index + 2, :] = inv_ref[pl.ds(2 * gathered_ref[index], 2), :]
    inv[...] = jnp.concatenate([inv_rows[...]] * (128 // (2 * stored)), axis=0).T
    for index in range(stored):
        if index % 4 == 0:
            for copy in raw_copies[index : index + 4]:
                copy.wait()
        at = pl.multiple_of(order_ref[index] * rows, rows)
        inv_fwd = inv[:, 2 * index : 2 * index + 1]
        inv_saved = inv[:, 2 * index + 1 : 2 * index + 2]
        normed = raw_ref[index, :rows, :].astype(jnp.float32) * inv_fwd
        mixed = (normed * gains[1] + p[4]) * (normed * gains[2] + p[6])
        normed = raw_ref[index, rows : 2 * rows, :].astype(jnp.float32) * inv_saved
        cot = raw_ref[index, 2 * rows :, :].astype(jnp.float32)
        ordered[pl.ds(at, rows), :LANES] = mixed.astype(jnp.bfloat16)
        ordered[pl.ds(at, rows), LANES:] = (cot * (normed * gains[0] + p[2])).astype(jnp.bfloat16)

    table_copies[0].wait()
    for index in range(blocks):
        data = ordered[index * BLOCK : (index + 1) * BLOCK, :]
        spectra[index] = jnp.dot(enter[...], data, preferred_element_type=jnp.float32)

    table_copies[2].wait()

    def forward_and_adjoint(low, high, one_product):
        for adjoint in (False, True):
            lanes = slice(LANES, 2 * LANES) if adjoint else slice(0, LANES)
            x_re = [spectra[j, low, lanes] for j in range(blocks)]
            x_im = [spectra[j, high, lanes] for j in range(blocks)]
            for i in range(blocks):
                terms = range(i, blocks) if adjoint else range(i + 1)
                re, im = one_product(adjoint, x_re, x_im, [(abs(i - j), j) for j in terms])
                product[i, low, lanes] = re
                product[i, high, lanes] = im

    def total(terms):
        terms = list(terms)
        return functools.reduce(lambda one, two: one + two, terms)

    def first_tile(adjoint, x_re, x_im, terms):
        f_re = [filt[d, 0, 0:8, :] for d in range(blocks)]
        first = lax.broadcasted_iota(jnp.int32, (8, LANES), 0) == 0
        imag = [filt[d, 1, 0:8, :] for d in range(blocks)]
        f_im = [jnp.where(first, 0.0, value) for value in imag]
        f_nq = [jnp.where(first, value, f_re[d]) for d, value in enumerate(imag)]
        direct = total(f_re[d] * x_re[j] for d, j in terms)
        crossed = total(f_im[d] * x_im[j] for d, j in terms)
        straight = total(f_nq[d] * x_im[j] for d, j in terms)
        turned = total(f_im[d] * x_re[j] for d, j in terms)
        if adjoint:
            return direct + crossed, straight - turned
        return direct - crossed, straight + turned

    forward_and_adjoint(slice(0, 8), slice(BLOCK, BLOCK + 8), first_tile)

    def products(tile, carry):
        low = pl.ds(pl.multiple_of(tile * 8, 8), 8)
        high = pl.ds(pl.multiple_of(BLOCK + tile * 8, 8), 8)
        f_re = [filt[d, 0, low, :] for d in range(blocks)]
        f_im = [filt[d, 1, low, :] for d in range(blocks)]
        f_less = [f_im[d] - f_re[d] for d in range(blocks)]
        f_more = [f_im[d] + f_re[d] for d in range(blocks)]

        def other_tile(adjoint, x_re, x_im, terms):
            both = total(f_re[d] * (x_re[j] + x_im[j]) for d, j in terms)
            if adjoint:
                return (
                    both + total(f_less[d] * x_im[j] for d, j in terms),
                    both - total(f_more[d] * x_re[j] for d, j in terms),
                )
            return (
                both - total(f_more[d] * x_im[j] for d, j in terms),
                both + total(f_less[d] * x_re[j] for d, j in terms),
            )

        forward_and_adjoint(low, high, other_tile)
        return carry

    lax.fori_loop(1, BLOCK // 8, products, 0)

    table_copies[1].wait()
    for index in range(blocks):
        left = jnp.dot(
            leave[...], product[index].astype(jnp.bfloat16), preferred_element_type=jnp.float32
        )
        ordered[index * BLOCK : (index + 1) * BLOCK, :] = left.astype(jnp.bfloat16)

    sums = [jnp.zeros((8, LANES), jnp.float32)] * 3
    for index in range(stored):
        at = pl.multiple_of(order_ref[index] * rows, rows)
        block = ordered[pl.ds(at, rows), :]
        out_ref[index, :rows, :] = block
        grad_mixed = block[:, LANES:].astype(jnp.float32)
        inv_saved = inv[:, 2 * index + 1 : 2 * index + 2]
        normed = raw_ref[index, rows : 2 * rows, :].astype(jnp.float32) * inv_saved
        once = grad_mixed * normed
        for power, term in enumerate((grad_mixed, once, once * normed)):
            sums[power] = sums[power] + fold(term)

    sums = jnp.concatenate(
        [jnp.sum(total, axis=0, keepdims=True) for total in sums]
        + [jnp.zeros((5, LANES), jnp.float32)],
        axis=0,
    )
    top = sums.astype(jnp.bfloat16)
    rest = (sums - top.astype(jnp.float32)).astype(jnp.bfloat16)
    for index in range(stored):
        out_ref[index, rows:, :LANES] = top
        out_ref[index, rows:, LANES:] = rest
        out_copies[index].start()
    for copy in out_copies:
        copy.wait()


def convolve(where, order, gathered, raw, inv, params, spectra, tables):
    stored = raw.shape[0]
    rows = raw.shape[1] // 3
    length = stored * rows
    blocks = length // BLOCK
    return pl.pallas_call(
        conv_kernel,
        out_shape=pltpu.HBM((stored, rows + 8, 2 * LANES), jnp.bfloat16),
        in_specs=[SMEM] * 3 + [VMEM] * 2 + [HBM] * 4,
        out_specs=HBM,
        scratch_shapes=[
            pltpu.VMEM(raw.shape, jnp.bfloat16),
            pltpu.VMEM(spectra.shape, jnp.float32),
            pltpu.VMEM((2 * BLOCK, BLOCK), jnp.bfloat16),
            pltpu.VMEM((BLOCK, 2 * BLOCK), jnp.bfloat16),
            pltpu.VMEM((stored, rows + 8, 2 * LANES), jnp.bfloat16),
            pltpu.VMEM((length, 2 * LANES), jnp.bfloat16),
            pltpu.VMEM((blocks, 2 * BLOCK, 2 * LANES), jnp.float32),
            pltpu.VMEM((blocks, 2 * BLOCK, 2 * LANES), jnp.float32),
            pltpu.VMEM((2 * stored, 128), jnp.float32),
            pltpu.VMEM((128, 128), jnp.float32),
            pltpu.SemaphoreType.DMA((stored,)),
            pltpu.SemaphoreType.DMA((3,)),
            pltpu.SemaphoreType.DMA((stored,)),
        ],
        name="convolve",
        compiler_params=pltpu.CompilerParams(vmem_limit_bytes=28 << 20),
    )(
        where, order, gathered, inv, params, in_hbm(spectra), in_hbm(raw),
        *[in_hbm(table) for table in tables],
    )


def forward_terms(at, inputs, conv, params_ref, inv_fwd):
    p = [params_ref[0, row : row + 1, at] for row in range(3)]
    query = inputs * inv_fwd * (p[0] * p[1]) + p[2]
    return inputs + query * conv


def backward_terms(at, saved, sconv, cot, grad_mixed, params_ref, inv_saved):
    p = [params_ref[0, row : row + 1, at] for row in range(7)]
    normed = saved * inv_saved
    mixed_grad = normed * (2.0 * p[0] * p[3] * p[5] * p[0]) + p[0] * (p[6] * p[3] + p[4] * p[5])
    grad_normed = cot * sconv * (p[1] * p[0]) + grad_mixed * mixed_grad
    return cot + inv_saved * grad_normed, grad_normed * normed


def leave_kernel(
    pipe_ref, inv_ref, back_ref, fwd_hbm, saved_ref, sconv_ref, cot_ref, params_ref,
    send_ref, keep_ref, cross_ref, inv, acc, fwd_ref, fwd_sem,
):
    rows, width = fwd_ref.shape[1:]
    fwd_copy = pltpu.make_async_copy(fwd_hbm, fwd_ref, fwd_sem)
    fwd_copy.start()
    inv[...] = rows_to_columns(inv_ref[0:8, :])
    inv_fwd = inv[:, 0:1]
    inv_saved = inv[:, 1:2]

    def both(layer_ref, partial_ref):
        cross = jnp.zeros((rows, LANES), jnp.float32)
        for group in range(width // LANES):
            at = pl.ds(group * LANES, LANES)
            partial, term = backward_terms(
                at,
                saved_ref[0, :, at].astype(jnp.float32),
                sconv_ref[0, :, at].astype(jnp.float32),
                cot_ref[0, :, at].astype(jnp.float32),
                back_ref[group, :rows, LANES:].astype(jnp.float32),
                params_ref,
                inv_saved,
            )
            cross = cross + term
            partial_ref[0, :, at] = partial.astype(jnp.bfloat16)
        acc[...] = cross
        fwd_copy.wait()
        for group in range(width // LANES):
            at = pl.ds(group * LANES, LANES)
            inputs = fwd_ref[0, :, at].astype(jnp.float32)
            conv = back_ref[group, :rows, :LANES].astype(jnp.float32)
            layer = forward_terms(at, inputs, conv, params_ref, inv_fwd)
            layer_ref[0, :, at] = layer.astype(jnp.bfloat16)

    @pl.when(pipe_ref[0] == 0)
    def _():
        both(send_ref, keep_ref)

    @pl.when(pipe_ref[0] != 0)
    def _():
        both(keep_ref, send_ref)

    cross = columns_to_rows([jnp.sum(acc[...], axis=1, keepdims=True)])
    cross_ref[...] = cross * (inv_ref[1:2, :] * inv_ref[1:2, :] / D)


def leave(pipe, inv, back, fwd_in, saved_in, saved_conv, grad_out, mix_params):
    return pl.pallas_call(
        leave_kernel,
        out_shape=(
            pltpu.VMEM(fwd_in.shape, jnp.bfloat16),
            pltpu.VMEM(fwd_in.shape, jnp.bfloat16),
            pltpu.VMEM((8, 128), jnp.float32),
        ),
        in_specs=[SMEM] + [VMEM] * 2 + [HBM] + [VMEM] * 4,
        out_specs=(VMEM, VMEM, VMEM),
        scratch_shapes=[pltpu.VMEM((fwd_in.shape[1], 128), jnp.float32)] * 2
        + [pltpu.VMEM(fwd_in.shape, jnp.bfloat16), pltpu.SemaphoreType.DMA],
        name="leave",
        compiler_params=pltpu.CompilerParams(vmem_limit_bytes=24 << 20),
    )(
        pipe, inv, in_vmem(back), in_hbm(fwd_in),
        *[in_vmem(a) for a in (saved_in, saved_conv, grad_out)], mix_params,
    )


def rows_kernel(
    pipe_ref, known_ref, back_ref, send_ref, keep_ref, params_ref, layer_hbm, grads_ref, layer_sem
):
    first = pipe_ref[0] == 0
    stored, rows = back_ref.shape[0], send_ref.shape[1]
    sent = pltpu.make_async_copy(send_ref, layer_hbm, layer_sem)
    kept = pltpu.make_async_copy(keep_ref, layer_hbm, layer_sem)

    @pl.when(first)
    def _():
        sent.start()

    @pl.when(jnp.logical_not(first))
    def _():
        kept.start()

    for group in range(stored):
        own = pl.ds(group * LANES, LANES)
        p = [params_ref[0, row : row + 1, own] for row in range(7)]
        extra = back_ref[group, rows:, :].astype(jnp.float32)
        extra = extra[:, :LANES] + extra[:, LANES:]
        m0, m1, m2 = extra[0:1], extra[1:2], extra[2:3]
        q0 = known_ref[group : group + 1, :]
        q1 = known_ref[stored + group : stored + group + 1, :]
        key_normed = p[0] * p[5] * m2 + p[6] * m1
        value_normed = p[0] * p[3] * m2 + p[4] * m1
        grads = [
            p[1] * q1 + p[3] * key_normed + p[5] * value_normed,
            p[0] * q1,
            q0,
            p[0] * key_normed,
            p[0] * p[5] * m1 + p[6] * m0,
            p[0] * value_normed,
            p[0] * p[3] * m1 + p[4] * m0,
        ]
        for index, value in enumerate(grads):
            grads_ref[index, :, own] = value

    @pl.when(first)
    def _():
        sent.wait()

    @pl.when(jnp.logical_not(first))
    def _():
        kept.wait()


def finish_rows(pipe, known, back, send, keep, mix_params):
    return pl.pallas_call(
        rows_kernel,
        out_shape=(
            pltpu.HBM(send.shape, jnp.bfloat16),
            jax.ShapeDtypeStruct((7, 1, send.shape[2]), jnp.float32),
        ),
        in_specs=[SMEM] + [VMEM] * 5,
        out_specs=(HBM, VMEM),
        scratch_shapes=[pltpu.SemaphoreType.DMA],
        name="finish_rows",
        compiler_params=pltpu.CompilerParams(vmem_limit_bytes=8 << 20),
    )(pipe, known, in_vmem(back), in_vmem(send), in_vmem(keep), mix_params)


def cross_kernel(
    pipe_ref, s0, s1, s2, s3, send_ref, keep_ref, saved_ref, peer_ref, grad_hbm, term_ref,
    grad_ref, scale, grad_sem,
):
    first = pipe_ref[0] == 0
    steps = grad_sem.shape[0]
    wide = grad_ref.shape[1] // steps
    scale[...] = rows_to_columns(s0[...] + s1[...] + s2[...] + s3[...])
    copies = []
    for step in range(steps):
        for group in range(step * wide, (step + 1) * wide, LANES):
            at = pl.ds(group, LANES)
            partial = jnp.where(first, keep_ref[0, :, at], send_ref[0, :, at]).astype(jnp.float32)
            saved = saved_ref[0, :, at].astype(jnp.float32)
            grad_ref[:, at] = (partial - saved * scale[:, 0:1]).astype(jnp.bfloat16)
        chunk = pl.ds(step * wide, wide)
        copy = pltpu.make_async_copy(
            grad_ref.at[:, chunk], grad_hbm.at[0, :, chunk], grad_sem.at[step]
        )
        copy.start()
        copies.append(copy)
    for group in range(0, grad_ref.shape[1], LANES):
        at = pl.ds(group, LANES)
        term_ref[:, at] = peer_ref[0, :, at].astype(jnp.float32) * scale[:, 1:2]
    for copy in copies:
        copy.wait()


def finish_cross(pipe, scales, send, keep, saved_in, peer_saved):
    rows, width = saved_in.shape[1:]
    return pl.pallas_call(
        cross_kernel,
        out_shape=(
            pltpu.HBM(saved_in.shape, jnp.bfloat16),
            pltpu.VMEM((rows, width), jnp.float32),
        ),
        in_specs=[SMEM] + [VMEM] * 8,
        out_specs=(HBM, VMEM),
        scratch_shapes=[
            pltpu.VMEM((rows, width), jnp.bfloat16),
            pltpu.VMEM((rows, 128), jnp.float32),
            pltpu.SemaphoreType.DMA((4,)),
        ],
        name="finish_cross",
        compiler_params=pltpu.CompilerParams(vmem_limit_bytes=8 << 20),
    )(pipe, *scales, in_vmem(send), in_vmem(keep), in_vmem(saved_in), in_vmem(peer_saved))


def received_kernel(value_ref, term_ref, out_hbm, out_ref, out_sem):
    steps = out_sem.shape[0]
    wide = out_ref.shape[1] // steps
    copies = []
    for step in range(steps):
        for at in range(step * wide, (step + 1) * wide, LANES):
            own = pl.ds(at, LANES)
            value = value_ref[0, :, own].astype(jnp.float32)
            out_ref[:, own] = (value - term_ref[:, own]).astype(jnp.bfloat16)
        chunk = pl.ds(step * wide, wide)
        copy = pltpu.make_async_copy(
            out_ref.at[:, chunk], out_hbm.at[0, :, chunk], out_sem.at[step]
        )
        copy.start()
        copies.append(copy)
    for copy in copies:
        copy.wait()


def finish_received(value, term):
    rows, width = term.shape
    return pl.pallas_call(
        received_kernel,
        out_shape=pltpu.HBM(value.shape, jnp.bfloat16),
        in_specs=[VMEM, VMEM],
        out_specs=HBM,
        scratch_shapes=[
            pltpu.VMEM((rows, width), jnp.bfloat16),
            pltpu.SemaphoreType.DMA((8,)),
        ],
        name="received",
        compiler_params=pltpu.CompilerParams(vmem_limit_bytes=8 << 20),
    )(in_vmem(value), in_vmem(term))


def per_device(tables, fwd_in, saved_in, saved_conv, grad_out, filters, mix_params, span_order):
    where = lax.axis_index("seq").astype(jnp.int32).reshape(1)
    pipe = lax.axis_index("pipe").astype(jnp.int32).reshape(1)
    raw, sums = pack(fwd_in, saved_in, grad_out)
    raw = lax.all_to_all(raw, "seq", 0, 0)
    own_sums = sum(over_chan(sums))
    sums = own_sums[:2]
    known = early(own_sums, saved_in, saved_conv, grad_out)
    got = across(jnp.concatenate([sums, known], axis=0), 1)
    sums = jnp.concatenate([sums, got[:2]], axis=0)
    known = known + got[2:]
    message = jnp.concatenate([sums, known], axis=0)
    got = [message] + [round_ring(message, apart) for apart in (1, 2, 3)]
    sums = jnp.concatenate([rows[:4] for rows in got], axis=0)
    got = [rows[4:] for rows in got]
    known = (got[0] + got[2]) + (got[1] + got[3])
    got = across(jnp.concatenate([sums, known], axis=0), 8)
    inv = lax.rsqrt(jnp.concatenate([sums, got[:16]], axis=0) / D + EPSILON)
    known = known + got[16:]
    peer_saved = lax.ppermute(saved_in, "pipe", [(1, 0)])
    spectra = filter_spectra(where, filters, tables)
    back = convolve(where, span_order, gather_order(), raw, inv, mix_params, spectra, tables)
    back = lax.all_to_all(back, "seq", 0, 0)
    outgoing, keep, cross = leave(
        pipe, inv, back, fwd_in, saved_in, saved_conv, grad_out, mix_params
    )
    peer_cross = lax.ppermute(cross, "pipe", [(1, 0)])
    incoming = lax.ppermute(outgoing, "pipe", [(0, 1), (1, 0)])
    scales = over_chan(jnp.concatenate([cross[:1], peer_cross[:1], cross[:6]], axis=0))
    layer_out, param_grad = finish_rows(pipe, known, back, outgoing, keep, mix_params)
    input_grad, term = finish_cross(pipe, scales, outgoing, keep, saved_in, peer_saved)
    received = finish_received(incoming, term)
    return (layer_out, input_grad, param_grad.transpose(1, 0, 2), received)


def solution(mesh):
    tables = transform_tables()
    in_specs = (
        P("pipe", "seq", "chan"),
        P("pipe", "seq", "chan"),
        P("pipe", "seq", "chan"),
        P("pipe", "seq", "chan"),
        P("pipe", None, "chan"),
        P("pipe", None, "chan"),
        P(),
    )
    out_specs = (
        P("pipe", "seq", "chan"),
        P("pipe", "seq", "chan"),
        P("pipe", None, "chan"),
        P("pipe", "seq", "chan"),
    )
    return jax.shard_map(
        functools.partial(per_device, tuple(jnp.asarray(table) for table in tables)),
        mesh=mesh,
        in_specs=in_specs,
        out_specs=out_specs,
        check_vma=False,
    )
```
